32 devices in a mesh: seq: 8 (over y, x, core), head: 4 (over z).
Axes of the slice: x: 2, y: 2, z: 4, core: 2. Of those that a mesh axis runs over, the one named last changes fastest.
Arguments:
- tokens: bfloat16 [8192, 2048], P('seq'), may hold values from -6 to 6
- seq_ids: int32 [64], P('seq'), may hold values from 0 to 7, never falling along the last dimension, each value on 1 to 16 neighbouring positions
- gain_attn: bfloat16 [2048], P('seq'), may hold values from 0.5 to 1.5
- w_qk: bfloat16 [2048, 512], P('seq', 'head'), may hold values from -0.125 to 0.125
- w_v: bfloat16 [2048, 2048], P('seq', 'head'), may hold values from -0.125 to 0.125
- w_out: bfloat16 [2048, 2048], P('seq', 'head'), may hold values from -1.5 to 1.5
- gain_mlp: bfloat16 [2048], P('seq'), may hold values from 0.5 to 1.5
- w_gate: bfloat16 [2048, 5632], P('seq', 'head'), may hold values from -0.125 to 0.125
- w_up: bfloat16 [2048, 5632], P('seq', 'head'), may hold values from -0.125 to 0.125
- w_down: bfloat16 [2048, 5632], P('seq', 'head'), may hold values from -0.078125 to 0.078125
- cotangent: bfloat16 [8192, 2048], P('seq'), may hold values from -6 to 6
Outputs:
- layer_out: bfloat16 [8192, 2048], P('seq')
- grad_tokens: float32 [8192, 2048], P('seq')
- grad_w_qk: float32 [2048, 512], P('seq', 'head')
- grad_w_v: float32 [2048, 2048], P('seq', 'head')
- grad_w_out: float32 [2048, 2048], P('seq', 'head')
- grad_w_gate: float32 [2048, 5632], P('seq', 'head')
- grad_w_up: float32 [2048, 5632], P('seq', 'head')
- grad_w_down: float32 [2048, 5632], P('seq', 'head')
- grad_gain_attn: float32 [2048], P('seq')
- grad_gain_mlp: float32 [2048], P('seq')
The draws below stay inside these ranges and needn't reach their ends.
Inputs may be any that keep to these rules, and one draw needn't show every extreme that they name: `seq_ids`: ids never fall along the array; every sequence holds 1 to 16 blocks, and one holds exactly 16.
All inputs are finite; a program needn't handle non-finite values.
Results may differ from the reference program's by a relative error of at most 0.015.
Values may be sent and summed in bfloat16 or wider, within the bound.
No kernel may reach another device: no remote copies, remote signals or barrier semaphores. Data moves between devices by JAX's collectives and lax.ppermute only.
A program may use at most 256 MiB of HBM per device.

```python
import math
import jax
import jax.numpy as jnp
import numpy as np
from jax import lax

D = 2048
HEADS = 16
FEAT = 16
HV = 128
FF = 5632
FM = 273
GROUP = 128
SEQ_GROUPS = 16
NCHUNKS = 64
TOKENS = 8192
SEQS = 8


def strengthened(drawn, rng, source, target, shards_of, factor):
    def block_of(position):
        return (jnp.arange(drawn.shape[position]) // (drawn.shape[position] // shards_of)).reshape((-1,) + (1,) * (drawn.ndim - 1 - position))

    one_side = jax.random.permutation(rng, shards_of)[block_of(target)]
    other_side = (block_of(target) + shards_of // 2) % shards_of
    return jnp.where((block_of(source) == one_side) | (block_of(source) == other_side), factor * drawn, drawn)


def level_of(own_key, extent, cuts, low, largest):
    level, own = 1.0, jax.random.fold_in(own_key, 6)
    for axis_at, blocks in cuts:
        steps = jnp.exp(jax.random.uniform(jax.random.fold_in(own, axis_at), (blocks,), jnp.float32, low / len(cuts), largest / len(cuts)))
        level = level * jnp.repeat(steps, extent[axis_at] // blocks).reshape([-1 if axis == axis_at else 1 for axis in range(len(extent))])
    return level


def split_up(number_of, total, limit, lean):
    portions = [(1 << 20) // math.isqrt(grade ** lean) + 1 for grade in range(2, number_of + 1)]
    rest, holding = total - limit - (number_of - 1), [1] * (number_of - 1)
    while rest > 0:
        candidates = [i for i in range(number_of - 1) if holding[i] < limit]
        mass, budget = sum([portions[i] for i in candidates]), rest
        for i in candidates:
            addition = min(limit - holding[i], max(1, budget * portions[i] // mass), rest)
            holding[i] = holding[i] + addition
            rest = rest - addition
    return np.array([limit] + holding)


def ragged(key, number_of, total, limit, lean):
    if number_of == 2:
        one = jax.random.randint(key, (), max(1, total - limit), min(limit, total - 1) + 1)
        return jnp.stack([one, total - one])
    lengths = jnp.asarray(split_up(number_of, total, limit, lean), jnp.int32)
    couples = (number_of - 1) // 2
    giver, taker = lengths[1:1 + 2 * couples:2], lengths[2:2 + 2 * couples:2]
    slack = jnp.minimum(giver - 1, limit - taker)
    passed = jax.random.randint(jax.random.fold_in(key, 1), (couples,), 0, 1 << 20) % (slack + 1)
    lengths = lengths.at[1:1 + 2 * couples:2].set(giver - passed).at[2:2 + 2 * couples:2].set(taker + passed)
    return lengths[jax.random.permutation(jax.random.fold_in(key, 2), number_of)]


def normal_values(key, shape, deviation, reach, cuts=(), held_as=jnp.bfloat16):
    gain = level_of(key, shape, cuts, -0.22, 0.18) if cuts else 1.0
    drawn = jax.random.normal(key, shape, jnp.float32) * deviation * gain
    return jnp.minimum(jnp.maximum(drawn, -reach), reach).astype(held_as)


def gaussian_with(stream_key, extent, deviation, bound, shards, heavy, dtype=jnp.bfloat16):
    entries = deviation * jax.random.normal(stream_key, extent, jnp.float32)
    if shards:
        entries = entries * level_of(stream_key, extent, shards, -0.22, 0.18)
    return jnp.clip(strengthened(entries, jax.random.fold_in(stream_key, 3), *heavy), -bound, bound).astype(dtype)


def setup_inputs(seed: int = 0) -> dict:
    seeds = jax.random.split(jax.random.key(seed), 12)
    return {
        "tokens": gaussian_with(seeds[0], (TOKENS, D), 1.0, 6.0, ((0, 8),), (0, 1, 8, 2.0)),
        "seq_ids": jnp.searchsorted(jnp.cumsum(ragged(seeds[1], SEQS, NCHUNKS, SEQ_GROUPS, 0)), jnp.arange(NCHUNKS), side="right").astype(jnp.int32),
        "gain_attn": jnp.clip(1.0 + 0.1 * jax.random.normal(seeds[2], (D,), jnp.float32), 0.5, 1.5).astype(jnp.bfloat16),
        "w_qk": normal_values(seeds[3], (D, 2 * HEADS * FEAT), D ** -0.5, 0.125, ((0, 8), (1, 4))),
        "w_v": normal_values(seeds[4], (D, HEADS * HV), D ** -0.5, 0.125, ((0, 8), (1, 4))),
        "w_out": normal_values(seeds[5], (D, D), (max(D // 128, 1)) ** -0.5, 1.5, ((0, 8), (1, 4))),
        "gain_mlp": jnp.clip(1.0 + 0.1 * jax.random.normal(seeds[6], (D,), jnp.float32), 0.5, 1.5).astype(jnp.bfloat16),
        "w_gate": normal_values(seeds[7], (D, FF), D ** -0.5, 0.125, ((0, 8), (1, 4))),
        "w_up": normal_values(seeds[8], (D, FF), D ** -0.5, 0.125, ((0, 8), (1, 4))),
        "w_down": normal_values(seeds[9], (D, FF), FF ** -0.5, 0.078125, ((0, 8), (1, 4))),
        "cotangent": gaussian_with(seeds[10], (TOKENS, D), 1.0, 6.0, ((0, 8),), (0, 1, 8, 2.0)),
    }


@jax.custom_vjp
def low(v):
    return lax.optimization_barrier(v.astype(jnp.bfloat16)).astype(jnp.float32)

@jax.custom_vjp
def low_back(v):
    return v

def low_keep(v):
    return (low(v), None)

def low_pass(kept, grad):
    return (grad,)

def back_keep(v):
    return (v, None)

def back_low(kept, grad):
    return (low(grad),)
low.defvjp(low_keep, low_pass)
low_back.defvjp(back_keep, back_low)
epsilon = 1e-06
highest = lax.Precision.HIGHEST

def feature_map(values):
    feat_width = values.shape[-1]
    fourth_root = feat_width ** 0.25
    outer_terms = (values[..., :, None] * values[..., None, :]).reshape(values.shape[:-1] + (feat_width * feat_width,))
    constant = jnp.ones(values.shape[:-1] + (1,), jnp.float32)
    return jnp.concatenate([constant, values / fourth_root, outer_terms / (math.sqrt(2.0) * fourth_root * fourth_root)], axis=-1)

def attention(queries, keys_all, values, seq_ids):
    score_scale = FEAT ** (-0.5)
    positions = jnp.arange(GROUP)
    causal = (positions[:, None] >= positions[None, :]).astype(jnp.float32)

    def advance(carried, inputs):
        states, norms, previous = carried
        query_block, key_block, value_block, block_id = inputs
        same_seq = (block_id == previous).astype(jnp.float32)
        states = states * same_seq
        norms = norms * same_seq
        feat_q = low(feature_map(query_block))
        feat_k = low(feature_map(key_block))
        raw_scores = low_back(jnp.einsum('thf,ihf->hti', query_block, key_block, precision=highest))
        shifted = raw_scores * score_scale
        weights = causal * (1.0 + shifted + 0.5 * shifted * shifted)
        numerator = low_back(jnp.einsum('hti,ihv->thv', low(weights), value_block, precision=highest) + jnp.einsum('thm,hmv->thv', feat_q, low(states), precision=highest))
        denominator = lax.optimization_barrier(jnp.sum(weights, axis=-1)).T + jnp.einsum('thm,hm->th', feat_q, norms, precision=highest)
        head_rows = low(low_back(numerator / denominator[..., None]))
        states = states + low_back(jnp.einsum('ihm,ihv->hmv', feat_k, value_block, precision=highest))
        norms = norms + lax.optimization_barrier(jnp.sum(feat_k, axis=0))
        return ((states, norms, block_id), head_rows)
    start = (jnp.zeros((HEADS, FM, HV), jnp.float32), jnp.zeros((HEADS, FM), jnp.float32), jnp.array(-1, jnp.int32))
    _, outputs = lax.scan(jax.checkpoint(advance), start, (queries, keys_all, values, seq_ids))
    return outputs

def forward(inputs, gain_one, w_qk, w_v, w_out, gain_two, w_gate, w_up, w_down, seq_ids):
    scale_one = lax.rsqrt(lax.optimization_barrier(jnp.mean(inputs * inputs, axis=-1, keepdims=True)) + epsilon)
    normed = low(inputs * scale_one * gain_one)
    proj_qk = low(low_back(jnp.dot(normed, w_qk, precision=highest)))
    proj_v = low(low_back(jnp.dot(normed, w_v, precision=highest)))
    paired = proj_qk.reshape(NCHUNKS, GROUP, HEADS, 2, FEAT)
    values = proj_v.reshape(NCHUNKS, GROUP, HEADS, HV)
    heads = attention(paired[:, :, :, 0], paired[:, :, :, 1], values, seq_ids).reshape(TOKENS, D)
    branch = low_back(jnp.dot(heads, w_out, precision=highest))
    residual = inputs + branch
    scale_two = lax.rsqrt(lax.optimization_barrier(jnp.mean(residual * residual, axis=-1, keepdims=True)) + epsilon)
    normed_two = low(residual * scale_two * gain_two)
    gate_pre = low_back(jnp.dot(normed_two, w_gate, precision=highest))
    up_pre = low_back(jnp.dot(normed_two, w_up, precision=highest))
    active = low(jax.nn.silu(gate_pre) * up_pre)
    return residual + jnp.dot(active, w_down.T, precision=highest)

def reference(tokens, seq_ids, gain_attn, w_qk, w_v, w_out, gain_mlp, w_gate, w_up, w_down, cotangent):
    primals = (tokens.astype(jnp.float32), gain_attn.astype(jnp.float32), w_qk.astype(jnp.float32), w_v.astype(jnp.float32), w_out.astype(jnp.float32), gain_mlp.astype(jnp.float32), w_gate.astype(jnp.float32), w_up.astype(jnp.float32), w_down.astype(jnp.float32))

    def layer(inputs, gain_one, qk_weight, v_weight, out_weight, gain_two, gate_weight, up_weight, down_weight):
        return forward(inputs, gain_one, qk_weight, v_weight, out_weight, gain_two, gate_weight, up_weight, down_weight, seq_ids)
    result, pullback = jax.vjp(layer, *primals)
    grads = pullback(cotangent.astype(jnp.float32))
    return (result.astype(jnp.bfloat16), grads[0], grads[2], grads[3], grads[4], grads[6], grads[7], grads[8], grads[1], grads[5])
```

```python
import math

import jax
import jax.numpy as jnp
from jax import lax
from jax.sharding import PartitionSpec as P

FEAT = 16
HV = 128
MAX_BLOCKS = 16


epsilon = 1e-06
highest = lax.Precision.HIGHEST
bf16 = jnp.bfloat16
f32 = jnp.float32


def feature_map(values):
    feat_width = values.shape[-1]
    fourth_root = feat_width**0.25
    outer_terms = (values[..., :, None] * values[..., None, :]).reshape(
        values.shape[:-1] + (feat_width * feat_width,)
    )
    constant = jnp.ones(values.shape[:-1] + (1,), f32)
    return jnp.concatenate(
        [
            constant,
            values / fourth_root,
            outer_terms / (math.sqrt(2.0) * fourth_root * fourth_root),
        ],
        axis=-1,
    )


def feature_grad(values, grad_feat):
    feat_width = values.shape[-1]
    fourth_root = feat_width**0.25
    linear = grad_feat[..., 1 : 1 + feat_width] / fourth_root
    square = grad_feat[..., 1 + feat_width :].reshape(values.shape + (feat_width,))
    square = square + jnp.swapaxes(square, -1, -2)
    quadratic = jnp.einsum("...ab,...b->...a", square, values, precision=highest)
    return linear + quadratic / (math.sqrt(2.0) * fourth_root * fourth_root)


def rows_dot(left, right):
    return lax.dot_general(left, right, (((0,), (0,)), ((), ())), preferred_element_type=f32)


def cols_dot(left, right):
    return lax.dot_general(left, right, (((1,), (1,)), ((), ())), preferred_element_type=f32)


def dot(left, right):
    return jnp.dot(left, right, preferred_element_type=f32)


def turn(value, axis, step):
    count = lax.axis_size(axis)
    return lax.ppermute(value, axis, [(i, (i + step) % count) for i in range(count)])


def gather_blocks(block, axis, dim):
    count, mine = lax.axis_size(axis), lax.axis_index(axis)
    width = block.shape[dim]
    shape = list(block.shape)
    shape[dim] = width * count
    whole = jnp.zeros(shape, block.dtype)
    whole = lax.dynamic_update_slice_in_dim(whole, block, mine * width, dim)
    for step in range(1, count):
        got = turn(block, axis, step)
        whole = lax.dynamic_update_slice_in_dim(whole, got, ((mine - step) % count) * width, dim)
    return whole


def neighbour_sums(tail, first_id, last_id, step, reach):
    count, mine = lax.axis_size("seq"), lax.axis_index("seq")
    total = None
    for k in range(1, reach + 1):
        if k >= count:
            break
        got, tag = [
            lax.ppermute(
                part,
                "seq",
                [(i, i + k * step) for i in range(count) if 0 <= i + k * step < count],
            )
            for part in (tail, last_id)
        ]
        there = (mine - k >= 0) if step > 0 else (mine + k < count)
        use = (there & (tag == first_id)).astype(f32)
        part = use * got
        total = part if total is None else total + part
    return jnp.zeros_like(tail) if total is None else total


def body(tokens, seq_ids, gain_attn, w_qk, w_v, w_out, gain_mlp, w_gate, w_up, w_down, cotangent):
    zc, z = lax.axis_size("head"), lax.axis_index("head")
    token_count, width = tokens.shape
    blocks = seq_ids.shape[0]
    block_len = token_count // blocks
    heads_here = w_v.shape[1] // HV
    qk_cols = w_qk.shape[1]
    share = token_count // zc
    reach = -(-(MAX_BLOCKS - 1) // blocks)

    gains = lax.all_gather(jnp.stack([gain_attn, gain_mlp]), "seq", axis=1, tiled=True).astype(f32)
    gain_one, gain_two = gains[0], gains[1]
    qkv_part = jnp.concatenate([w_qk, w_v], axis=1)
    full_qkv = lax.all_gather(qkv_part, "seq", axis=0, tiled=True)
    out_rows = gather_blocks(w_out, "head", 1)
    full_out = lax.all_gather(out_rows, "seq", axis=0, tiled=True)
    full_gate = lax.all_gather(w_gate, "seq", axis=0, tiled=True)
    full_up = lax.all_gather(w_up, "seq", axis=0, tiled=True)
    full_down = lax.all_gather(w_down, "seq", axis=0, tiled=True)
    qkv_rows = gather_blocks(qkv_part, "head", 1)
    all_qkv = lax.all_gather(qkv_rows, "seq", axis=0, tiled=True)

    inputs = tokens.astype(f32)
    scale_one = lax.rsqrt(jnp.mean(inputs * inputs, axis=-1, keepdims=True) + epsilon)
    normed = (inputs * scale_one * gain_one).astype(bf16)
    proj = dot(normed, full_qkv).astype(bf16)
    proj_qk, proj_v = proj[:, :qk_cols], proj[:, qk_cols:]
    paired = proj_qk.reshape(blocks, block_len, heads_here, 2, FEAT)
    queries = paired[:, :, :, 0]
    keys_all = paired[:, :, :, 1]
    values = proj_v.reshape(blocks, block_len, heads_here, HV)
    score_scale = FEAT ** (-0.5)
    positions = jnp.arange(block_len)
    causal = (positions[:, None] >= positions[None, :]).astype(f32)
    feat_q = feature_map(queries.astype(f32)).astype(bf16)
    feat_k = feature_map(keys_all.astype(f32)).astype(bf16)
    raw_scores = jnp.einsum("cthf,cihf->chti", queries, keys_all, preferred_element_type=f32)
    shifted = raw_scores * score_scale
    weights_full = causal * (1.0 + shifted + 0.5 * shifted * shifted)
    weights_low = weights_full.astype(bf16)
    block_states = jnp.einsum("cihm,cihv->chmv", feat_k, values, preferred_element_type=f32)
    block_norms = jnp.sum(feat_k.astype(f32), axis=1)
    block_order = jnp.arange(blocks)
    same_seq = seq_ids[:, None] == seq_ids[None, :]
    earlier_mask = (same_seq & (block_order[None, :] < block_order[:, None])).astype(f32)
    first_id, last_id = seq_ids[:1], seq_ids[-1:]
    last_mask = (seq_ids == last_id).astype(f32)
    first_mask = (seq_ids == first_id).astype(f32)
    states_ext = jnp.concatenate([block_states, block_norms[..., None]], axis=-1)
    local_prefix = jnp.einsum("jc,chmv->jhmv", earlier_mask, states_ext, precision=highest)
    tail = jnp.einsum("c,chmv->hmv", last_mask, states_ext, precision=highest)
    incoming = neighbour_sums(tail, first_id, last_id, 1, reach)
    prefix_ext = local_prefix + first_mask[:, None, None, None] * incoming
    prefix_norms = prefix_ext[..., HV]
    prefix_low = prefix_ext[..., :HV].astype(bf16)
    numerator = jnp.einsum(
        "chti,cihv->cthv", weights_low, values, preferred_element_type=f32
    ) + jnp.einsum("cthm,chmv->cthv", feat_q, prefix_low, preferred_element_type=f32)
    denominator = jnp.einsum("chti->cth", weights_full) + jnp.einsum(
        "cthm,chm->cth", feat_q.astype(f32), prefix_norms, precision=highest
    )
    head_rows = (
        (numerator / denominator[..., None]).astype(bf16).reshape(token_count, heads_here * HV)
    )

    heads_own = lax.all_to_all(head_rows, "head", 0, 1, tiled=True)
    own_in = lax.dynamic_slice_in_dim(tokens, z * share, share, 0).astype(f32)
    residual = own_in + dot(heads_own, full_out)
    scale_two = lax.rsqrt(jnp.mean(residual * residual, axis=-1, keepdims=True) + epsilon)
    normed_own = (residual * scale_two * gain_two).astype(bf16)

    order = [0] + sorted(range(1, zc), key=lambda k: min(k, zc - k))
    normed_parts, cot_parts, act_parts, dgate_parts, dup_parts = [], [], [], [], []
    feed, grad_normed = None, None
    for k in order:
        normed_two = normed_own if k == 0 else turn(normed_own, "head", k)
        owner = (z - k) % zc
        cot = lax.dynamic_slice_in_dim(cotangent, owner * share, share, 0)
        gate_pre = dot(normed_two, full_gate)
        up_pre = dot(normed_two, full_up)
        gate_sigmoid = jax.nn.sigmoid(gate_pre)
        active = (gate_pre * gate_sigmoid * up_pre).astype(bf16)
        grad_active = dot(cot, full_down)
        grad_gate = (
            grad_active * up_pre * gate_sigmoid * (1.0 + gate_pre * (1.0 - gate_sigmoid))
        ).astype(bf16)
        grad_upper = (grad_active * gate_pre * gate_sigmoid).astype(bf16)
        back = cols_dot(grad_gate, full_gate) + cols_dot(grad_upper, full_up)
        out = cols_dot(active, full_down)
        if k:
            back = turn(back.astype(bf16), "head", -k).astype(f32)
            out = turn(out.astype(bf16), "head", -k).astype(f32)
        feed = out if feed is None else feed + out
        grad_normed = back if grad_normed is None else grad_normed + back
        normed_parts.append(normed_two)
        cot_parts.append(cot)
        act_parts.append(active)
        dgate_parts.append(grad_gate)
        dup_parts.append(grad_upper)
    result_own = (residual + feed).astype(bf16)

    normed_all = jnp.concatenate(normed_parts)
    down_grad = rows_dot(jnp.concatenate(cot_parts), jnp.concatenate(act_parts)).astype(bf16)
    gate_grad = rows_dot(normed_all, jnp.concatenate(dgate_parts)).astype(bf16)
    up_grad = rows_dot(normed_all, jnp.concatenate(dup_parts)).astype(bf16)

    cot_own = lax.dynamic_slice_in_dim(cotangent, z * share, share, 0).astype(f32)
    weighted = grad_normed * gain_two
    grad_mid = (
        cot_own
        + scale_two * weighted
        - residual * scale_two**3 * jnp.mean(weighted * residual, axis=-1, keepdims=True)
    )
    gain_two_term = jnp.sum(grad_normed * residual * scale_two, axis=0)
    grad_branch = grad_mid.astype(bf16)
    out_grad = rows_dot(heads_own, grad_branch).astype(bf16)
    grad_heads = lax.all_to_all(
        cols_dot(grad_branch, full_out).astype(bf16), "head", 1, 0, tiled=True
    )
    grad_rows = grad_heads.reshape(blocks, block_len, heads_here, HV).astype(f32)
    grad_numer = (grad_rows / denominator[..., None]).astype(bf16)
    grad_denom = -jnp.sum(grad_rows * numerator, axis=-1) / (denominator * denominator)
    grad_weights = jnp.einsum("cthv,cihv->chti", grad_numer, values, preferred_element_type=f32)
    grad_full = causal * (grad_weights + jnp.transpose(grad_denom, (0, 2, 1))[..., None])
    grad_raw = (grad_full * (1.0 + shifted) * score_scale).astype(bf16)
    grad_q_inner = jnp.einsum("chti,cihf->cthf", grad_raw, keys_all, preferred_element_type=f32)
    grad_k_inner = jnp.einsum("chti,cthf->cihf", grad_raw, queries, preferred_element_type=f32)
    grad_v_inner = jnp.einsum("chti,cthv->cihv", weights_low, grad_numer, preferred_element_type=f32)
    grad_prefix = jnp.einsum("cthm,cthv->chmv", feat_q, grad_numer, preferred_element_type=f32)
    grad_pnorm = jnp.einsum("cthm,cth->chm", feat_q.astype(f32), grad_denom, precision=highest)
    grad_fq = (
        jnp.einsum("cthv,chmv->cthm", grad_numer, prefix_low, preferred_element_type=f32)
        + grad_denom[..., None] * prefix_norms[:, None]
    )
    grad_ext = jnp.concatenate([grad_prefix, grad_pnorm[..., None]], axis=-1)
    local_after = jnp.einsum("jc,jhmv->chmv", earlier_mask, grad_ext, precision=highest)
    head_part = jnp.einsum("c,chmv->hmv", first_mask, grad_ext, precision=highest)
    outgoing = neighbour_sums(head_part, last_id, first_id, -1, reach)
    after = local_after + last_mask[:, None, None, None] * outgoing
    grad_states = after[..., :HV].astype(bf16)
    grad_norms = after[..., HV]
    grad_fk = (
        jnp.einsum("cihv,chmv->cihm", values, grad_states, preferred_element_type=f32)
        + grad_norms[:, None]
    )
    grad_v_state = jnp.einsum("cihm,chmv->cihv", feat_k, grad_states, preferred_element_type=f32)
    grad_q = (grad_q_inner + feature_grad(queries.astype(f32), grad_fq)).astype(bf16)
    grad_k = (grad_k_inner + feature_grad(keys_all.astype(f32), grad_fk)).astype(bf16)
    grad_qk = jnp.stack([grad_q, grad_k], axis=3).reshape(token_count, qk_cols)
    grad_v = (grad_v_inner + grad_v_state).astype(bf16).reshape(token_count, heads_here * HV)
    grad_qkv = jnp.concatenate([grad_qk, grad_v], axis=1)
    qkv_grad = rows_dot(normed, grad_qkv)

    own_qkv = lax.all_to_all(grad_qkv, "head", 0, 1, tiled=True)
    grad_norm_one = cols_dot(own_qkv, all_qkv)
    own_scale = lax.dynamic_slice_in_dim(scale_one, z * share, share, 0)
    weighted_one = grad_norm_one * gain_one
    grad_own = (
        grad_mid
        + own_scale * weighted_one
        - own_in * own_scale**3 * jnp.mean(weighted_one * own_in, axis=-1, keepdims=True)
    )
    gain_one_term = jnp.sum(grad_norm_one * own_in * own_scale, axis=0)
    grad_tokens = gather_blocks(grad_own.astype(bf16), "head", 0).astype(f32)
    result = gather_blocks(result_own, "head", 0)

    def scatter(grad):
        return lax.psum_scatter(grad, "seq", scatter_dimension=0, tiled=True)

    down_shard = scatter(down_grad).astype(f32)
    gate_shard = scatter(gate_grad).astype(f32)
    up_shard = scatter(up_grad).astype(f32)
    out_part = scatter(out_grad)
    out_pieces = lax.all_to_all(out_part, "head", 1, 0, tiled=True)
    out_shard = jnp.sum(
        out_pieces.reshape(zc, w_out.shape[0], w_out.shape[1]).astype(f32), axis=0
    )
    gain_terms = jnp.pad(jnp.stack([gain_one_term, gain_two_term], axis=1), ((0, 0), (0, 126)))
    last = scatter(jnp.concatenate([qkv_grad, gain_terms], axis=1).astype(bf16)).astype(f32)
    gain_sums = lax.psum(last[:, -128:-126].T, "head")
    return (
        result,
        grad_tokens,
        last[:, :qk_cols],
        last[:, qk_cols:-128],
        out_shard,
        gate_shard,
        up_shard,
        down_shard,
        gain_sums[0],
        gain_sums[1],
    )


def solution(mesh):
    return jax.shard_map(
        body,
        mesh=mesh,
        in_specs=(
            P("seq", None),
            P("seq"),
            P("seq"),
            P("seq", "head"),
            P("seq", "head"),
            P("seq", "head"),
            P("seq"),
            P("seq", "head"),
            P("seq", "head"),
            P("seq", "head"),
            P("seq", None),
        ),
        out_specs=(
            P("seq", None),
            P("seq", None),
            P("seq", "head"),
            P("seq", "head"),
            P("seq", "head"),
            P("seq", "head"),
            P("seq", "head"),
            P("seq", "head"),
            P("seq"),
            P("seq"),
        ),
        check_vma=False,
    )
```

```python
import math

import jax
import jax.numpy as jnp
import numpy as np
from jax import lax
from jax.experimental import pallas as pl
from jax.experimental.pallas import tpu as pltpu
from jax.sharding import PartitionSpec as P

FEAT = 16
HV = 128
MAX_BLOCKS = 16


epsilon = 1e-06
bf16 = jnp.bfloat16
f32 = jnp.float32


FS = 160
FL = 256


def selection_tables(heads):
    pairs = [(a, b) for a in range(FEAT) for b in range(a, FEAT)]
    first = np.zeros((FEAT, FL), np.float32)
    second = np.zeros((FEAT, FL), np.float32)
    one_a, one_b = np.zeros(FL, np.float32), np.zeros(FL, np.float32)
    scale, twice = np.zeros(FL, np.float32), np.ones(FL, np.float32)
    one_a[0] = one_b[0] = scale[0] = 1.0
    for a in range(FEAT):
        first[a, 1 + a] = 1.0
        one_b[1 + a] = 1.0
        scale[1 + a] = 1.0 / FEAT**0.25
    for at, (a, b) in enumerate(pairs):
        at += 1 + FEAT
        first[a, at] = second[b, at] = 1.0
        scale[at] = 1.0 / (math.sqrt(2.0) * FEAT**0.5)
        twice[at] = 1.0 if a == b else 2.0
    cols = heads * 2 * FEAT
    wide = np.zeros((4, heads, cols, FL), np.float32)
    moves = np.zeros((2, heads, cols, cols), np.float32)
    for h in range(heads):
        q0, k0 = h * 2 * FEAT, h * 2 * FEAT + FEAT
        wide[0, h, q0:k0], wide[1, h, q0:k0] = first, second
        wide[2, h, k0 : k0 + FEAT], wide[3, h, k0 : k0 + FEAT] = first, second
        for a in range(FEAT):
            moves[0, h, k0 + a, q0 + a] = 1.0
            moves[1, h, q0 + a, k0 + a] = 1.0
    tall = np.swapaxes(wide, 2, 3)[:, :, :FS]
    rows = np.zeros((8, FL), np.float32)
    rows[0], rows[1], rows[2], rows[3] = one_a, one_b, scale, twice
    columns = np.repeat(rows[:3, :FS, None], cols, axis=2)
    return (
        jnp.asarray(wide, bf16),
        jnp.asarray(np.ascontiguousarray(tall), bf16),
        jnp.asarray(moves, bf16),
        jnp.asarray(rows, f32),
        jnp.asarray(columns, f32),
    )


def mm(left, right):
    return lax.dot_general(left, right, (((1,), (0,)), ((), ())), preferred_element_type=f32)


def mm_nt(left, right):
    return lax.dot_general(left, right, (((1,), (1,)), ((), ())), preferred_element_type=f32)


def lane_marks(rows, lanes):
    lane = lax.broadcasted_iota(jnp.int32, (rows, HV), 1)
    return (lane < lanes).astype(bf16)


def features_wide(x, first, second, rows):
    one = mm(x, first) + rows[0:1]
    two = mm(x, second) + rows[1:2]
    return one, two, (one * two) * rows[2:3]


def features_tall(x, first, second, columns):
    one = mm_nt(first, x) + columns[0]
    two = mm_nt(second, x) + columns[1]
    return ((one * two) * columns[2]).astype(bf16)


def split_state(state):
    left, right = state[:, :HV], state[:, HV:]
    lane = lax.broadcasted_iota(jnp.int32, right.shape, 1)
    high = right.astype(bf16)
    low = (right - high.astype(f32)).astype(bf16)
    return left.astype(bf16), jnp.where(lane == 2, low, high)


def join_state(state, both):
    right = state[:, HV:]
    lane = lax.broadcasted_iota(jnp.int32, right.shape, 1)
    whole = right[:, 0:1] + right[:, 2:3]
    if both:
        new = jnp.where(lane < 3, whole, 0.0)
    else:
        new = jnp.where(lane == 1, right, jnp.where(lane < 3, whole, 0.0))
    return jnp.concatenate([state[:, :HV], new], axis=1)


def tail_kernel(ids, proj, tall, columns, out, acc):
    at, last = pl.program_id(0), pl.num_programs(0) - 1
    heads = out.shape[0]
    qk = heads * 2 * FEAT

    @pl.when(at == 0)
    def _():
        acc[...] = jnp.zeros_like(acc)

    @pl.when(ids[at] == ids[last])
    def _():
        x = proj[:, :qk]
        marks = lane_marks(x.shape[0], 3)
        for h in range(heads):
            tall_k = features_tall(x, tall[2, h], tall[3, h], columns)
            v = proj[:, qk + h * HV : qk + (h + 1) * HV]
            acc[h] += mm(tall_k, jnp.concatenate([v, marks], axis=1))

    @pl.when(at == last)
    def _():
        for h in range(heads):
            left, right = split_state(acc[h])
            out[h, :, :HV] = left
            out[h, :, HV:] = right


def forward_kernel(
    ids, proj, incoming, wide, tall, moves, rows, columns, heads_out, num_out, den_out, state_out, acc
):
    at = pl.program_id(0)
    heads = acc.shape[0]
    qk = heads * 2 * FEAT

    @pl.when(at == 0)
    def _():
        for h in range(heads):
            acc[h] = join_state(incoming[h], True)

    @pl.when((at > 0) & (ids[at] != ids[jnp.maximum(at - 1, 0)]))
    def _():
        acc[...] = jnp.zeros_like(acc)

    x = proj[:, :qk]
    size = x.shape[0]
    marks = lane_marks(size, 3)
    row = lax.broadcasted_iota(jnp.int32, (size, size), 0)
    col = lax.broadcasted_iota(jnp.int32, (size, size), 1)
    dens = jnp.zeros((size, HV), f32)
    for h in range(heads):
        v = proj[:, qk + h * HV : qk + (h + 1) * HV]
        left, right = split_state(acc[h])
        state = jnp.concatenate(
            [jnp.concatenate([left, right], axis=1), jnp.zeros((FL - FS, 2 * HV), bf16)], axis=0
        )
        state_out[0, h] = state
        _, _, fq = features_wide(x, wide[0, h], wide[1, h], rows)
        fq = fq.astype(bf16) * rows[3:4].astype(bf16)
        moved = mm(x, moves[0, h]).astype(bf16)
        s = mm_nt(x, moved) * FEAT**-0.5
        a = jnp.where(row >= col, 1.0 + s + 0.5 * s * s, 0.0)
        ext = mm(fq, state)
        num = mm(a.astype(bf16), v) + ext[:, :HV]
        den = (
            jnp.sum(a, axis=1, keepdims=True)
            + ext[:, HV : HV + 1]
            + ext[:, HV + 2 : HV + 3]
        )
        heads_out[:, h * HV : (h + 1) * HV] = (num / den).astype(bf16)
        num_out[:, h * HV : (h + 1) * HV] = num
        dens = jnp.where(col[:, :HV] == h, den, dens)
        tall_k = features_tall(x, tall[2, h], tall[3, h], columns)
        acc[h] += mm(tall_k, jnp.concatenate([v, marks], axis=1))
    den_out[...] = dens


def grad_tail_kernel(ids, proj, dheads, num, den, tall, columns, dnum_out, out, acc):
    at, last = pl.program_id(0), pl.num_programs(0) - 1
    heads = out.shape[0]
    qk = heads * 2 * FEAT

    @pl.when(at == 0)
    def _():
        acc[...] = jnp.zeros_like(acc)

    x = proj[:, :qk]
    size = x.shape[0]
    lane = lax.broadcasted_iota(jnp.int32, (size, HV), 1)
    for h in range(heads):
        d = den[:, h : h + 1]
        g = dheads[:, h * HV : (h + 1) * HV].astype(f32)
        dnum = (g / d).astype(bf16)
        dden = -jnp.sum(g * num[:, h * HV : (h + 1) * HV], axis=1, keepdims=True) / (d * d)
        high = dden.astype(bf16)
        low = (dden - high.astype(f32)).astype(bf16)
        side = jnp.where(
            (lane == 0) | (lane == 2), high.astype(f32), jnp.where(lane == 1, low.astype(f32), 0.0)
        ).astype(bf16)
        dnum_out[:, h * 2 * HV : h * 2 * HV + HV] = dnum
        dnum_out[:, h * 2 * HV + HV : (h + 1) * 2 * HV] = side

    @pl.when(ids[at] == ids[0])
    def _():
        for h in range(heads):
            tall_q = features_tall(x, tall[0, h], tall[1, h], columns)
            acc[h] += mm(tall_q, dnum_out[:, h * 2 * HV : (h + 1) * 2 * HV])

    @pl.when(at == last)
    def _():
        for h in range(heads):
            left, right = split_state(acc[h])
            out[h, :, :HV] = left
            out[h, :, HV:] = right


def backward_kernel(
    ids, proj, dnum_in, state_in, incoming, wide, tall, moves, rows, columns, out, acc
):
    step, last = pl.program_id(0), pl.num_programs(0) - 1
    at = last - step
    heads = acc.shape[0]
    qk = heads * 2 * FEAT

    @pl.when(step == 0)
    def _():
        for h in range(heads):
            acc[h] = join_state(incoming[h], False)

    @pl.when((step > 0) & (ids[at] != ids[jnp.minimum(at + 1, last)]))
    def _():
        acc[...] = jnp.zeros_like(acc)

    x = proj[:, :qk]
    size = x.shape[0]
    row = lax.broadcasted_iota(jnp.int32, (size, size), 0)
    col = lax.broadcasted_iota(jnp.int32, (size, size), 1)
    marks2, marks3 = lane_marks(size, 2), lane_marks(size, 3)
    weight = rows[2:3] * rows[3:4]
    twice = rows[3:4].astype(bf16)
    total = jnp.zeros((size, qk), f32)
    for h in range(heads):
        v = proj[:, qk + h * HV : qk + (h + 1) * HV]
        dn = dnum_in[:, h * 2 * HV : (h + 1) * 2 * HV]
        dnum = dn[:, :HV]
        left, right = split_state(acc[h])
        dstate = jnp.concatenate(
            [jnp.concatenate([left, right], axis=1), jnp.zeros((FL - FS, 2 * HV), bf16)], axis=0
        )
        q1, q2, _ = features_wide(x, wide[0, h], wide[1, h], rows)
        k1, k2, fk = features_wide(x, wide[2, h], wide[3, h], rows)
        fk = fk.astype(bf16) * twice
        kq = mm(x, moves[0, h]).astype(bf16)
        qk_moved = mm(x, moves[1, h]).astype(bf16)
        s = mm_nt(x, kq) * FEAT**-0.5
        st = mm_nt(kq, x) * FEAT**-0.5
        at_low = jnp.where(row <= col, 1.0 + st + 0.5 * st * st, 0.0).astype(bf16)
        v2 = jnp.concatenate([v, marks2], axis=1)
        da = mm_nt(dn, v2)
        dat = mm_nt(v2, dn)
        draw = jnp.where(row >= col, da * (1.0 + s) * FEAT**-0.5, 0.0).astype(bf16)
        drawt = jnp.where(row <= col, dat * (1.0 + st) * FEAT**-0.5, 0.0).astype(bf16)
        wq = mm_nt(dn, state_in[0, h]) * weight
        wk = mm_nt(jnp.concatenate([v, marks3], axis=1), dstate) * weight
        total += (
            mm(draw, kq)
            + mm(drawt, qk_moved)
            + mm_nt((wq * q2).astype(bf16), wide[0, h])
            + mm_nt((wq * q1).astype(bf16), wide[1, h])
            + mm_nt((wk * k2).astype(bf16), wide[2, h])
            + mm_nt((wk * k1).astype(bf16), wide[3, h])
        )
        dv = mm(at_low, dnum) + mm(fk, dstate)[:, :HV]
        out[:, qk + h * HV : qk + (h + 1) * HV] = dv.astype(bf16)
        tall_q = features_tall(x, tall[0, h], tall[1, h], columns)
        acc[h] += mm(tall_q, dn)
    out[:, :qk] = total.astype(bf16)


def whole_spec(array):
    zeros = (0,) * array.ndim
    return pl.BlockSpec(array.shape, lambda i, ids: zeros)


def attention_calls(blocks, block_len, heads, tables):
    wide, tall, moves, rows, columns = tables
    qk = heads * 2 * FEAT
    tokens = blocks * block_len
    state = (heads, FS, 2 * HV)

    def at_block(cols, reverse=False):
        if reverse:
            return pl.BlockSpec((block_len, cols), lambda i, ids: (blocks - 1 - i, 0))
        return pl.BlockSpec((block_len, cols), lambda i, ids: (i, 0))

    def states_spec(reverse=False):
        if reverse:
            return pl.BlockSpec((1, heads, FL, 2 * HV), lambda i, ids: (blocks - 1 - i, 0, 0, 0))
        return pl.BlockSpec((1, heads, FL, 2 * HV), lambda i, ids: (i, 0, 0, 0))

    def call(kernel, name, in_specs, out_specs, out_shape, flops, moved):
        return pl.pallas_call(
            kernel,
            out_shape=out_shape,
            grid_spec=pltpu.PrefetchScalarGridSpec(
                num_scalar_prefetch=1,
                grid=(blocks,),
                in_specs=in_specs,
                out_specs=out_specs,
                scratch_shapes=[pltpu.VMEM(state, f32)],
            ),
            compiler_params=pltpu.CompilerParams(dimension_semantics=("arbitrary",)),
            cost_estimate=pl.CostEstimate(flops=flops, transcendentals=0, bytes_accessed=moved),
            name=name,
        )

    full_state = pl.BlockSpec(state, lambda i, ids: (0, 0, 0))
    proj_cols = qk + heads * HV

    def tail(ids, proj):
        return call(
            tail_kernel,
            "state_tail",
            [at_block(proj_cols), whole_spec(tall), whole_spec(columns)],
            full_state,
            jax.ShapeDtypeStruct(state, bf16),
            int(4e9),
            int(4e6),
        )(ids, proj, tall, columns)

    def forward(ids, proj, incoming):
        return call(
            forward_kernel,
            "attention_forward",
            [at_block(proj_cols), full_state]
            + [whole_spec(t) for t in (wide, tall, moves, rows, columns)],
            [at_block(heads * HV), at_block(heads * HV), at_block(HV), states_spec()],
            [
                jax.ShapeDtypeStruct((tokens, heads * HV), bf16),
                jax.ShapeDtypeStruct((tokens, heads * HV), f32),
                jax.ShapeDtypeStruct((tokens, HV), f32),
                jax.ShapeDtypeStruct((blocks, heads, FL, 2 * HV), bf16),
            ],
            int(9e9),
            int(2e7),
        )(ids, proj, incoming, wide, tall, moves, rows, columns)

    def grad_tail(ids, proj, dheads, num, den):
        return call(
            grad_tail_kernel,
            "state_grad_tail",
            [at_block(proj_cols), at_block(heads * HV), at_block(heads * HV), at_block(HV)]
            + [whole_spec(tall), whole_spec(columns)],
            [at_block(heads * 2 * HV), full_state],
            [
                jax.ShapeDtypeStruct((tokens, heads * 2 * HV), bf16),
                jax.ShapeDtypeStruct(state, bf16),
            ],
            int(4e9),
            int(1e7),
        )(ids, proj, dheads, num, den, tall, columns)

    def backward(ids, proj, dnum, states, incoming):
        return call(
            backward_kernel,
            "attention_backward",
            [at_block(proj_cols, True), at_block(heads * 2 * HV, True), states_spec(True), full_state]
            + [whole_spec(t) for t in (wide, tall, moves, rows, columns)],
            at_block(proj_cols, True),
            jax.ShapeDtypeStruct((tokens, proj_cols), bf16),
            int(2e10),
            int(2e7),
        )(ids, proj, dnum, states, incoming, wide, tall, moves, rows, columns)

    return tail, forward, grad_tail, backward


def rows_dot(left, right):
    return lax.dot_general(left, right, (((0,), (0,)), ((), ())), preferred_element_type=f32)


def cols_dot(left, right):
    return lax.dot_general(left, right, (((1,), (1,)), ((), ())), preferred_element_type=f32)


def dot(left, right):
    return jnp.dot(left, right, preferred_element_type=f32)


def turn(value, axis, step):
    count = lax.axis_size(axis)
    return lax.ppermute(value, axis, [(i, (i + step) % count) for i in range(count)])


def tie(*values):
    return lax.optimization_barrier(values)


def place(pieces, offsets, shape, along_columns=False, dtype=None):
    count = len(pieces)
    kept = pieces[0].dtype
    dtype = dtype or kept
    wider = dtype != kept

    def kernel(offs, *refs):
        out = refs[count]
        held = refs[count + 1 : 2 * count + 1]
        sent = refs[2 * count + 1 : 3 * count + 1] if wider else held
        sems = refs[-1]

        def bring(j):
            return pltpu.make_async_copy(refs[j], held[j], sems.at[0, j])

        def send(j):
            at = pl.multiple_of(jnp.maximum(offs[j], 0), 128)
            if along_columns:
                target = out.at[:, pl.ds(at, pieces[j].shape[1])]
            else:
                target = out.at[pl.ds(at, pieces[j].shape[0])]
            return pltpu.make_async_copy(sent[j], target, sems.at[1, j])

        def each(action):
            for j in range(count):

                @pl.when(offs[j] >= 0)
                def _(j=j):
                    action(j)

        def forward(j):
            bring(j).wait()
            if wider:
                sent[j][...] = held[j][...].astype(dtype)
            send(j).start()

        each(lambda j: bring(j).start())
        each(forward)
        each(lambda j: send(j).wait())

    anywhere = pl.BlockSpec(memory_space=pl.ANY)
    size = int(np.prod(shape))
    buffers = [pltpu.VMEM(piece.shape, kept) for piece in pieces]
    if wider:
        buffers += [pltpu.VMEM(piece.shape, dtype) for piece in pieces]
    return pl.pallas_call(
        kernel,
        out_shape=jax.ShapeDtypeStruct(shape, dtype),
        grid_spec=pltpu.PrefetchScalarGridSpec(
            num_scalar_prefetch=1,
            grid=(1,),
            in_specs=[anywhere] * count,
            out_specs=anywhere,
            scratch_shapes=buffers + [pltpu.SemaphoreType.DMA((2, count))],
        ),
        cost_estimate=pl.CostEstimate(flops=0, transcendentals=0, bytes_accessed=4 * size),
        name="place",
    )(jnp.stack([jnp.asarray(o, jnp.int32) for o in offsets]), *pieces)


def gather_columns(block, axis):
    count, mine = lax.axis_size(axis), lax.axis_index(axis)
    width = block.shape[1]
    pieces = [block] + [turn(block, axis, step) for step in range(1, count)]
    offsets = [((mine - step) % count) * width for step in range(count)]
    return place(pieces, offsets, (block.shape[0], width * count), along_columns=True)


def along(value, step):
    count = lax.axis_size("head")
    pairs = [(i, i + step) for i in range(count) if 0 <= i + step < count]
    return lax.ppermute(value, "head", pairs)


def sum_parts(parts, far, low=None, high=None):
    count = lax.axis_size("head")
    up, down = parts[-far % count], parts[far]
    if low is not None:
        up = (up.astype(f32) + low.astype(f32)).astype(bf16)
        down = (down.astype(f32) + high.astype(f32)).astype(bf16)
    return up, down


def sum_send(up, down, far):
    count = lax.axis_size("head")
    return (
        lax.ppermute(up, "head", [(i, i + 1) for i in range(count - far)]),
        lax.ppermute(down, "head", [(i, i - 1) for i in range(far, count)]),
    )


def sum_step(parts, far, low=None, high=None):
    return sum_send(*sum_parts(parts, far, low, high), far)


def join_line(own, from_low, from_high, dtype=None):
    count, mine = lax.axis_size("head"), lax.axis_index("head")
    rows = own.shape[0]
    pieces, offsets = [own], [mine * rows]
    for far, (low, high) in enumerate(zip(from_low, from_high), 1):
        pieces += [low, high]
        offsets.append((mine - far) * rows)
        offsets.append(jnp.where(mine + far < count, (mine + far) * rows, -1))
    return place(pieces, offsets, (rows * count, own.shape[1]), dtype=dtype)


def neighbour_sums(tail, first_id, last_id, step, reach):
    count, mine = lax.axis_size("seq"), lax.axis_index("seq")
    total = None
    for k in range(1, reach + 1):
        if k >= count:
            break
        got, tag = [
            lax.ppermute(
                part,
                "seq",
                [(i, i + k * step) for i in range(count) if 0 <= i + k * step < count],
            )
            for part in (tail, last_id)
        ]
        there = (mine - k >= 0) if step > 0 else (mine + k < count)
        use = (there & (tag == first_id)).astype(f32)
        part = use * got.astype(f32)
        total = part if total is None else total + part
    return jnp.zeros(tail.shape, f32) if total is None else total


def body(tokens, seq_ids, gain_attn, w_qk, w_v, w_out, gain_mlp, w_gate, w_up, w_down, cotangent):
    zc, z = lax.axis_size("head"), lax.axis_index("head")
    token_count, width = tokens.shape
    blocks = seq_ids.shape[0]
    block_len = token_count // blocks
    heads_here = w_v.shape[1] // HV
    qk_cols = w_qk.shape[1]
    share = token_count // zc
    reach = -(-(MAX_BLOCKS - 1) // blocks)

    gains = lax.all_gather(jnp.stack([gain_attn, gain_mlp]), "seq", axis=1, tiled=True).astype(f32)
    gain_one, gain_two = gains[0], gains[1]
    qkv_part = jnp.concatenate([w_qk, w_v], axis=1)
    full_qkv = lax.all_gather(qkv_part, "seq", axis=0, tiled=True)
    full_both = lax.all_gather(
        jnp.concatenate([w_gate, w_up], axis=1), "seq", axis=0, tiled=True
    )
    full_down = lax.all_gather(w_down, "seq", axis=0, tiled=True)
    out_rows = gather_columns(w_out, "head")
    full_qkv, out_rows = tie(full_qkv, out_rows)
    full_out = lax.all_gather(out_rows, "seq", axis=0, tiled=True)
    qkv_rows = gather_columns(tie(qkv_part, full_qkv)[0], "head")

    inputs = tokens.astype(f32)
    scale_one = lax.rsqrt(jnp.mean(inputs * inputs, axis=-1, keepdims=True) + epsilon)
    normed = (inputs * scale_one * gain_one).astype(bf16)
    proj = dot(normed, full_qkv).astype(bf16)
    tables = selection_tables(heads_here)
    tail_call, forward_call, grad_tail_call, backward_call = attention_calls(
        blocks, block_len, heads_here, tables
    )
    first_id, last_id = seq_ids[:1], seq_ids[-1:]
    incoming = neighbour_sums(tail_call(seq_ids, proj), first_id, last_id, 1, reach)
    head_rows, numerator, denominator, states = forward_call(seq_ids, proj, incoming)
    head_rows, qkv_rows = tie(head_rows, qkv_rows)
    all_qkv = lax.all_gather(qkv_rows, "seq", axis=0, tiled=True)

    heads_own = lax.all_to_all(head_rows, "head", 0, 1, tiled=True)
    own_in = lax.dynamic_slice_in_dim(tokens, z * share, share, 0).astype(f32)
    residual = own_in + dot(heads_own, full_out)
    scale_two = lax.rsqrt(jnp.mean(residual * residual, axis=-1, keepdims=True) + epsilon)
    normed_own = (residual * scale_two * gain_two).astype(bf16)

    order = [0] + sorted(range(1, zc), key=lambda k: min(k, zc - k))
    hidden = w_gate.shape[1]
    normed_parts, cot_parts, act_parts, both_parts = [], [], [], []
    outs, backs = {}, {}
    for k in order:
        normed_two = normed_own if k == 0 else turn(normed_own, "head", k)
        owner = (z - k) % zc
        cot = lax.dynamic_slice_in_dim(cotangent, owner * share, share, 0)
        pre = dot(normed_two, full_both)
        gate_pre, up_pre = pre[:, :hidden], pre[:, hidden:]
        gate_sigmoid = jax.nn.sigmoid(gate_pre)
        active = (gate_pre * gate_sigmoid * up_pre).astype(bf16)
        grad_active = dot(cot, full_down)
        grad_gate = grad_active * up_pre * gate_sigmoid * (1.0 + gate_pre * (1.0 - gate_sigmoid))
        grad_upper = grad_active * gate_pre * gate_sigmoid
        grad_both = jnp.concatenate([grad_gate.astype(bf16), grad_upper.astype(bf16)], axis=1)
        backs[k] = cols_dot(grad_both, full_both)
        outs[k] = cols_dot(active, full_down)
        if k:
            backs[k], outs[k] = backs[k].astype(bf16), outs[k].astype(bf16)
        normed_parts.append(normed_two)
        cot_parts.append(cot)
        act_parts.append(active)
        both_parts.append(grad_both)
    low = high = None
    for far in range(zc - 1, 2, -1):
        low, high = sum_step(backs, far, low, high)
    up, down = sum_parts(backs, 2, low, high)
    up, down, normed_parts[0], both_parts[0] = tie(up, down, normed_parts[0], both_parts[0])
    low, high = sum_send(up, down, 2)
    both_grad = rows_dot(jnp.concatenate(normed_parts), jnp.concatenate(both_parts)).astype(bf16)
    low, high, both_grad, *first = tie(low, high, both_grad, *sum_step(outs, zc - 1))
    up, down = sum_parts(backs, 1, low, high)
    up, down, act_parts[0], cot_parts[0] = tie(up, down, act_parts[0], cot_parts[0])
    low, high = sum_send(up, down, 1)
    down_grad = rows_dot(jnp.concatenate(cot_parts), jnp.concatenate(act_parts)).astype(bf16)
    tied = tie(backs[0], low, high, down_grad, both_grad, *[outs[k] for k in order], all_qkv)
    grad_normed = tied[0] + tied[1].astype(f32) + tied[2].astype(f32)
    down_grad, both_grad = tied[3:5]
    outs = dict(zip(order, tied[5:]))
    all_qkv = tied[-1]

    cot_own = lax.dynamic_slice_in_dim(cotangent, z * share, share, 0).astype(f32)
    weighted = grad_normed * gain_two
    grad_mid = (
        cot_own
        + scale_two * weighted
        - residual * scale_two**3 * jnp.mean(weighted * residual, axis=-1, keepdims=True)
    )
    gain_two_term = jnp.sum(grad_normed * residual * scale_two, axis=0)
    grad_branch = grad_mid.astype(bf16)
    grad_heads = cols_dot(grad_branch, full_out).astype(bf16)
    low, high = sum_step(outs, 2, *first)
    grad_heads, low, high = tie(grad_heads, low, high)
    grad_heads = lax.all_to_all(grad_heads, "head", 1, 0, tiled=True)
    dnum, head_part = grad_tail_call(seq_ids, proj, grad_heads, numerator, denominator)
    outgoing = neighbour_sums(head_part, last_id, first_id, -1, reach)
    low, high = sum_step(outs, 1, low, high)
    dnum, low, high = tie(dnum, low, high)
    result_own = (residual + outs[0] + low.astype(f32) + high.astype(f32)).astype(bf16)
    res_low, res_high = [along(result_own, 1)], [along(result_own, -1)]
    grad_qkv = backward_call(seq_ids, proj, dnum, states, outgoing)
    grad_qkv, res_low[0], res_high[0], heads_own = tie(
        grad_qkv, res_low[0], res_high[0], heads_own
    )
    out_grad = rows_dot(heads_own, grad_branch).astype(bf16)
    down_shard = lax.psum_scatter(down_grad, "seq", scatter_dimension=0, tiled=True)
    both_shard = lax.psum_scatter(both_grad, "seq", scatter_dimension=0, tiled=True)
    out_part = lax.psum_scatter(out_grad, "seq", scatter_dimension=0, tiled=True)
    qkv_grad = rows_dot(normed, grad_qkv)

    own_qkv = lax.all_to_all(grad_qkv, "head", 0, 1, tiled=True)
    own_qkv, down_shard, both_shard = tie(own_qkv, down_shard, both_shard)
    grad_norm_one = cols_dot(own_qkv, all_qkv)
    res_low.append(along(res_low[-1], 1))
    res_high.append(along(res_high[-1], -1))
    grad_norm_one, res_low[1], res_high[1] = tie(grad_norm_one, res_low[1], res_high[1])
    own_scale = lax.dynamic_slice_in_dim(scale_one, z * share, share, 0)
    weighted_one = grad_norm_one * gain_one
    grad_own = (
        grad_mid
        + own_scale * weighted_one
        - own_in * own_scale**3 * jnp.mean(weighted_one * own_in, axis=-1, keepdims=True)
    )
    gain_one_term = jnp.sum(grad_norm_one * own_in * own_scale, axis=0)
    tok_own = grad_own.astype(bf16)
    tok_low, tok_high = [tok_own], [tok_own]
    for far in range(1, zc):
        if far > 2:
            res_low.append(along(res_low[-1], 1))
            res_high.append(along(res_high[-1], -1))
        tok_low.append(along(tok_low[-1], 1))
        tok_high.append(along(tok_high[-1], -1))
        if far == 2:
            tok_low[-1], out_part = tie(tok_low[-1], out_part)
    grad_tokens = join_line(tok_own, tok_low[1:], tok_high[1:], f32)
    result = join_line(result_own, res_low, res_high)

    def scatter(grad):
        return lax.psum_scatter(grad, "seq", scatter_dimension=0, tiled=True)

    down_shard = down_shard.astype(f32)
    both_shard = both_shard.astype(f32)
    out_pieces = lax.all_to_all(out_part, "head", 1, 0, tiled=True)
    out_shard = jnp.sum(
        out_pieces.reshape(zc, w_out.shape[0], w_out.shape[1]).astype(f32), axis=0
    )
    gain_terms = jnp.pad(jnp.stack([gain_one_term, gain_two_term], axis=1), ((0, 0), (0, 126)))
    last = scatter(jnp.concatenate([qkv_grad, gain_terms], axis=1).astype(bf16)).astype(f32)
    gain_sums = lax.psum(last[:, -128:-126].T, "head")
    return (
        result,
        grad_tokens,
        last[:, :qk_cols],
        last[:, qk_cols:-128],
        out_shard,
        both_shard[:, :hidden],
        both_shard[:, hidden:],
        down_shard,
        gain_sums[0],
        gain_sums[1],
    )


def solution(mesh):
    return jax.shard_map(
        body,
        mesh=mesh,
        in_specs=(
            P("seq", None),
            P("seq"),
            P("seq"),
            P("seq", "head"),
            P("seq", "head"),
            P("seq", "head"),
            P("seq"),
            P("seq", "head"),
            P("seq", "head"),
            P("seq", "head"),
            P("seq", None),
        ),
        out_specs=(
            P("seq", None),
            P("seq", None),
            P("seq", "head"),
            P("seq", "head"),
            P("seq", "head"),
            P("seq", "head"),
            P("seq", "head"),
            P("seq", "head"),
            P("seq"),
            P("seq"),
        ),
        check_vma=False,
    )
```

```python
import math

import jax
import jax.numpy as jnp
import numpy as np
from jax import lax
from jax.experimental import pallas as pl
from jax.experimental.pallas import tpu as pltpu
from jax.sharding import PartitionSpec as P

FEAT = 16
HV = 128
MAX_BLOCKS = 16


epsilon = 1e-06
bf16 = jnp.bfloat16
f32 = jnp.float32


FS = 160
FL = 256


def selection_tables(heads):
    pairs = [(a, b) for a in range(FEAT) for b in range(a, FEAT)]
    first = np.zeros((FEAT, FL), np.float32)
    second = np.zeros((FEAT, FL), np.float32)
    one_a, one_b = np.zeros(FL, np.float32), np.zeros(FL, np.float32)
    scale, twice = np.zeros(FL, np.float32), np.ones(FL, np.float32)
    one_a[0] = one_b[0] = scale[0] = 1.0
    for a in range(FEAT):
        first[a, 1 + a] = 1.0
        one_b[1 + a] = 1.0
        scale[1 + a] = 1.0 / FEAT**0.25
    for at, (a, b) in enumerate(pairs):
        at += 1 + FEAT
        first[a, at] = second[b, at] = 1.0
        scale[at] = 1.0 / (math.sqrt(2.0) * FEAT**0.5)
        twice[at] = 1.0 if a == b else 2.0
    cols = heads * 2 * FEAT
    wide = np.zeros((4, heads, cols, FL), np.float32)
    moves = np.zeros((2, heads, cols, cols), np.float32)
    for h in range(heads):
        q0, k0 = h * 2 * FEAT, h * 2 * FEAT + FEAT
        wide[0, h, q0:k0], wide[1, h, q0:k0] = first, second
        wide[2, h, k0 : k0 + FEAT], wide[3, h, k0 : k0 + FEAT] = first, second
        for a in range(FEAT):
            moves[0, h, k0 + a, q0 + a] = 1.0
            moves[1, h, q0 + a, k0 + a] = 1.0
    tall = np.swapaxes(wide, 2, 3)[:, :, :FS]
    rows = np.zeros((8, FL), np.float32)
    rows[0], rows[1], rows[2], rows[3] = one_a, one_b, scale, twice
    columns = np.repeat(rows[:3, :FS, None], cols, axis=2)
    return (
        jnp.asarray(wide, bf16),
        jnp.asarray(np.ascontiguousarray(tall), bf16),
        jnp.asarray(moves, bf16),
        jnp.asarray(rows, f32),
        jnp.asarray(columns, f32),
    )


def mm(left, right):
    return lax.dot_general(left, right, (((1,), (0,)), ((), ())), preferred_element_type=f32)


def mm_nt(left, right):
    return lax.dot_general(left, right, (((1,), (1,)), ((), ())), preferred_element_type=f32)


def lane_marks(rows, lanes):
    lane = lax.broadcasted_iota(jnp.int32, (rows, HV), 1)
    return (lane < lanes).astype(bf16)


def features_wide(x, first, second, rows):
    one = mm(x, first) + rows[0:1]
    two = mm(x, second) + rows[1:2]
    return one, two, (one * two) * rows[2:3]


def features_tall(x, first, second, columns):
    one = mm_nt(first, x) + columns[0]
    two = mm_nt(second, x) + columns[1]
    return ((one * two) * columns[2]).astype(bf16)


def split_state(state):
    left, right = state[:, :HV], state[:, HV:]
    lane = lax.broadcasted_iota(jnp.int32, right.shape, 1)
    high = right.astype(bf16)
    low = (right - high.astype(f32)).astype(bf16)
    return left.astype(bf16), jnp.where(lane == 2, low, high)


def join_state(state, both):
    right = state[:, HV:]
    lane = lax.broadcasted_iota(jnp.int32, right.shape, 1)
    whole = right[:, 0:1] + right[:, 2:3]
    if both:
        new = jnp.where(lane < 3, whole, 0.0)
    else:
        new = jnp.where(lane == 1, right, jnp.where(lane < 3, whole, 0.0))
    return jnp.concatenate([state[:, :HV], new], axis=1)


def tail_kernel(ids, proj, tall, columns, out, acc):
    at, last = pl.program_id(0), pl.num_programs(0) - 1
    heads = out.shape[0]
    qk = heads * 2 * FEAT

    @pl.when(at == 0)
    def _():
        acc[...] = jnp.zeros_like(acc)

    @pl.when(ids[at] == ids[last])
    def _():
        x = proj[:, :qk]
        marks = lane_marks(x.shape[0], 3)
        for h in range(heads):
            tall_k = features_tall(x, tall[2, h], tall[3, h], columns)
            v = proj[:, qk + h * HV : qk + (h + 1) * HV]
            acc[h] += mm(tall_k, jnp.concatenate([v, marks], axis=1))

    @pl.when(at == last)
    def _():
        for h in range(heads):
            left, right = split_state(acc[h])
            out[h, :, :HV] = left
            out[h, :, HV:] = right


def inner_kernel(ids, proj, moves, num_out, den_out):
    heads = moves.shape[1]
    qk = heads * 2 * FEAT
    x = proj[:, :qk]
    size = x.shape[0]
    row = lax.broadcasted_iota(jnp.int32, (size, size), 0)
    col = lax.broadcasted_iota(jnp.int32, (size, size), 1)
    lane = lax.broadcasted_iota(jnp.int32, (size, HV), 1)
    dens = jnp.zeros((size, HV), f32)
    for h in range(heads):
        v = proj[:, qk + h * HV : qk + (h + 1) * HV]
        moved = mm(x, moves[0, h]).astype(bf16)
        s = mm_nt(x, moved) * FEAT**-0.5
        a = jnp.where(row >= col, 1.0 + s + 0.5 * s * s, 0.0)
        num_out[:, h * HV : (h + 1) * HV] = mm(a.astype(bf16), v)
        dens = jnp.where(lane == h, jnp.sum(a, axis=1, keepdims=True), dens)
    den_out[...] = dens


def forward_kernel(
    ids, proj, num_in, den_in, incoming, wide, tall, rows, columns, heads_out, num_out, den_out, state_out, acc
):
    at = pl.program_id(0)
    heads = acc.shape[0]
    qk = heads * 2 * FEAT

    @pl.when(at == 0)
    def _():
        for h in range(heads):
            acc[h] = join_state(incoming[h], True)

    @pl.when((at > 0) & (ids[at] != ids[jnp.maximum(at - 1, 0)]))
    def _():
        acc[...] = jnp.zeros_like(acc)

    x = proj[:, :qk]
    size = x.shape[0]
    marks = lane_marks(size, 3)
    lane = lax.broadcasted_iota(jnp.int32, (size, HV), 1)
    dens = jnp.zeros((size, HV), f32)
    for h in range(heads):
        v = proj[:, qk + h * HV : qk + (h + 1) * HV]
        left, right = split_state(acc[h])
        state = jnp.concatenate(
            [jnp.concatenate([left, right], axis=1), jnp.zeros((FL - FS, 2 * HV), bf16)], axis=0
        )
        state_out[0, h] = state
        _, _, fq = features_wide(x, wide[0, h], wide[1, h], rows)
        fq = fq.astype(bf16) * rows[3:4].astype(bf16)
        ext = mm(fq, state)
        num = num_in[:, h * HV : (h + 1) * HV] + ext[:, :HV]
        den = den_in[:, h : h + 1] + ext[:, HV : HV + 1] + ext[:, HV + 2 : HV + 3]
        heads_out[:, h * HV : (h + 1) * HV] = (num * (1.0 / den)).astype(bf16)
        num_out[:, h * HV : (h + 1) * HV] = num
        dens = jnp.where(lane == h, den, dens)
        tall_k = features_tall(x, tall[2, h], tall[3, h], columns)
        acc[h] += mm(tall_k, jnp.concatenate([v, marks], axis=1))
    den_out[...] = dens


def grad_tail_kernel(ids, proj, dheads, num, den, tall, columns, dnum_out, out, acc):
    at, last = pl.program_id(0), pl.num_programs(0) - 1
    heads = out.shape[0]
    qk = heads * 2 * FEAT

    @pl.when(at == 0)
    def _():
        acc[...] = jnp.zeros_like(acc)

    x = proj[:, :qk]
    size = x.shape[0]
    lane = lax.broadcasted_iota(jnp.int32, (size, HV), 1)
    for h in range(heads):
        d = den[:, h : h + 1]
        g = dheads[:, h * HV : (h + 1) * HV].astype(f32)
        inverse = 1.0 / d
        dnum = (g * inverse).astype(bf16)
        dden = -jnp.sum(g * num[:, h * HV : (h + 1) * HV], axis=1, keepdims=True) * (
            inverse * inverse
        )
        high = dden.astype(bf16)
        low = (dden - high.astype(f32)).astype(bf16)
        side = jnp.where(
            (lane == 0) | (lane == 2), high.astype(f32), jnp.where(lane == 1, low.astype(f32), 0.0)
        ).astype(bf16)
        dnum_out[:, h * 2 * HV : h * 2 * HV + HV] = dnum
        dnum_out[:, h * 2 * HV + HV : (h + 1) * 2 * HV] = side

    @pl.when(ids[at] == ids[0])
    def _():
        for h in range(heads):
            tall_q = features_tall(x, tall[0, h], tall[1, h], columns)
            acc[h] += mm(tall_q, dnum_out[:, h * 2 * HV : (h + 1) * 2 * HV])

    @pl.when(at == last)
    def _():
        for h in range(heads):
            left, right = split_state(acc[h])
            out[h, :, :HV] = left
            out[h, :, HV:] = right


def local_kernel(ids, proj, dnum_in, state_in, wide, moves, rows, out):
    heads = moves.shape[1]
    qk = heads * 2 * FEAT
    x = proj[:, :qk]
    size = x.shape[0]
    row = lax.broadcasted_iota(jnp.int32, (size, size), 0)
    col = lax.broadcasted_iota(jnp.int32, (size, size), 1)
    marks = lane_marks(size, 2)
    weight = rows[2:3] * rows[3:4]
    total = jnp.zeros((size, qk), f32)
    for h in range(heads):
        v = proj[:, qk + h * HV : qk + (h + 1) * HV]
        dn = dnum_in[:, h * 2 * HV : (h + 1) * 2 * HV]
        q1, q2, _ = features_wide(x, wide[0, h], wide[1, h], rows)
        kq = mm(x, moves[0, h]).astype(bf16)
        qk_moved = mm(x, moves[1, h]).astype(bf16)
        s = mm_nt(x, kq) * FEAT**-0.5
        st = mm_nt(kq, x) * FEAT**-0.5
        at_low = jnp.where(row <= col, 1.0 + st + 0.5 * st * st, 0.0).astype(bf16)
        v2 = jnp.concatenate([v, marks], axis=1)
        da = mm_nt(dn, v2)
        dat = mm_nt(v2, dn)
        draw = jnp.where(row >= col, da * (1.0 + s) * FEAT**-0.5, 0.0).astype(bf16)
        drawt = jnp.where(row <= col, dat * (1.0 + st) * FEAT**-0.5, 0.0).astype(bf16)
        wq = mm_nt(dn, state_in[0, h]) * weight
        total += (
            mm(draw, kq)
            + mm(drawt, qk_moved)
            + mm_nt((wq * q2).astype(bf16), wide[0, h])
            + mm_nt((wq * q1).astype(bf16), wide[1, h])
        )
        out[:, qk + h * HV : qk + (h + 1) * HV] = mm(at_low, dn[:, :HV])
    out[:, :qk] = total


def backward_kernel(ids, proj, dnum_in, local, incoming, wide, tall, rows, columns, out, acc):
    step, last = pl.program_id(0), pl.num_programs(0) - 1
    at = last - step
    heads = acc.shape[0]
    qk = heads * 2 * FEAT

    @pl.when(step == 0)
    def _():
        for h in range(heads):
            acc[h] = join_state(incoming[h], False)

    @pl.when((step > 0) & (ids[at] != ids[jnp.minimum(at + 1, last)]))
    def _():
        acc[...] = jnp.zeros_like(acc)

    x = proj[:, :qk]
    marks = lane_marks(x.shape[0], 3)
    weight = rows[2:3] * rows[3:4]
    twice = rows[3:4].astype(bf16)
    total = local[:, :qk]
    for h in range(heads):
        v = proj[:, qk + h * HV : qk + (h + 1) * HV]
        left, right = split_state(acc[h])
        dstate = jnp.concatenate(
            [jnp.concatenate([left, right], axis=1), jnp.zeros((FL - FS, 2 * HV), bf16)], axis=0
        )
        k1, k2, fk = features_wide(x, wide[2, h], wide[3, h], rows)
        fk = fk.astype(bf16) * twice
        wk = mm_nt(jnp.concatenate([v, marks], axis=1), dstate) * weight
        total += mm_nt((wk * k2).astype(bf16), wide[2, h]) + mm_nt(
            (wk * k1).astype(bf16), wide[3, h]
        )
        dv = local[:, qk + h * HV : qk + (h + 1) * HV] + mm(fk, dstate[:, :HV])
        out[:, qk + h * HV : qk + (h + 1) * HV] = dv.astype(bf16)
        tall_q = features_tall(x, tall[0, h], tall[1, h], columns)
        acc[h] += mm(tall_q, dnum_in[:, h * 2 * HV : (h + 1) * 2 * HV])
    out[:, :qk] = total.astype(bf16)


def whole_spec(array):
    zeros = (0,) * array.ndim
    return pl.BlockSpec(array.shape, lambda i, ids: zeros)


def attention_calls(blocks, block_len, heads, tables):
    wide, tall, moves, rows, columns = tables
    qk = heads * 2 * FEAT
    tokens = blocks * block_len
    state = (heads, FS, 2 * HV)

    def at_block(cols, reverse=False):
        if reverse:
            return pl.BlockSpec((block_len, cols), lambda i, ids: (blocks - 1 - i, 0))
        return pl.BlockSpec((block_len, cols), lambda i, ids: (i, 0))

    def states_spec(reverse=False):
        if reverse:
            return pl.BlockSpec((1, heads, FL, 2 * HV), lambda i, ids: (blocks - 1 - i, 0, 0, 0))
        return pl.BlockSpec((1, heads, FL, 2 * HV), lambda i, ids: (i, 0, 0, 0))

    def call(kernel, name, in_specs, out_specs, out_shape, flops, moved, carried=True):
        return pl.pallas_call(
            kernel,
            out_shape=out_shape,
            grid_spec=pltpu.PrefetchScalarGridSpec(
                num_scalar_prefetch=1,
                grid=(blocks,),
                in_specs=in_specs,
                out_specs=out_specs,
                scratch_shapes=[pltpu.VMEM(state, f32)] if carried else [],
            ),
            compiler_params=pltpu.CompilerParams(dimension_semantics=("arbitrary",)),
            cost_estimate=pl.CostEstimate(flops=flops, transcendentals=0, bytes_accessed=moved),
            name=name,
        )

    full_state = pl.BlockSpec(state, lambda i, ids: (0, 0, 0))
    proj_cols = qk + heads * HV

    def tail(ids, proj):
        return call(
            tail_kernel,
            "state_tail",
            [at_block(proj_cols), whole_spec(tall), whole_spec(columns)],
            full_state,
            jax.ShapeDtypeStruct(state, bf16),
            int(4e9),
            int(4e6),
        )(ids, proj, tall, columns)

    def inner(ids, proj):
        return call(
            inner_kernel,
            "attention_inner",
            [at_block(proj_cols), whole_spec(moves)],
            [at_block(heads * HV), at_block(HV)],
            [
                jax.ShapeDtypeStruct((tokens, heads * HV), f32),
                jax.ShapeDtypeStruct((tokens, HV), f32),
            ],
            int(4e9),
            int(4e6),
            False,
        )(ids, proj, moves)

    def forward(ids, proj, num, den, incoming):
        return call(
            forward_kernel,
            "attention_forward",
            [at_block(proj_cols), at_block(heads * HV), at_block(HV), full_state]
            + [whole_spec(t) for t in (wide, tall, rows, columns)],
            [at_block(heads * HV), at_block(heads * HV), at_block(HV), states_spec()],
            [
                jax.ShapeDtypeStruct((tokens, heads * HV), bf16),
                jax.ShapeDtypeStruct((tokens, heads * HV), f32),
                jax.ShapeDtypeStruct((tokens, HV), f32),
                jax.ShapeDtypeStruct((blocks, heads, FL, 2 * HV), bf16),
            ],
            int(6e9),
            int(2e7),
        )(ids, proj, num, den, incoming, wide, tall, rows, columns)

    def grad_tail(ids, proj, dheads, num, den):
        return call(
            grad_tail_kernel,
            "state_grad_tail",
            [at_block(proj_cols), at_block(heads * HV), at_block(heads * HV), at_block(HV)]
            + [whole_spec(tall), whole_spec(columns)],
            [at_block(heads * 2 * HV), full_state],
            [
                jax.ShapeDtypeStruct((tokens, heads * 2 * HV), bf16),
                jax.ShapeDtypeStruct(state, bf16),
            ],
            int(4e9),
            int(1e7),
        )(ids, proj, dheads, num, den, tall, columns)

    def local(ids, proj, dnum, states):
        return call(
            local_kernel,
            "attention_backward_local",
            [at_block(proj_cols), at_block(heads * 2 * HV), states_spec()]
            + [whole_spec(t) for t in (wide, moves, rows)],
            at_block(proj_cols),
            jax.ShapeDtypeStruct((tokens, proj_cols), f32),
            int(1.3e10),
            int(2e7),
            False,
        )(ids, proj, dnum, states, wide, moves, rows)

    def backward(ids, proj, dnum, partial, incoming):
        return call(
            backward_kernel,
            "attention_backward",
            [at_block(proj_cols, True), at_block(heads * 2 * HV, True)]
            + [at_block(proj_cols, True), full_state]
            + [whole_spec(t) for t in (wide, tall, rows, columns)],
            at_block(proj_cols, True),
            jax.ShapeDtypeStruct((tokens, proj_cols), bf16),
            int(1e10),
            int(2e7),
        )(ids, proj, dnum, partial, incoming, wide, tall, rows, columns)

    return tail, inner, forward, grad_tail, local, backward


def rows_dot(left, right):
    return lax.dot_general(left, right, (((0,), (0,)), ((), ())), preferred_element_type=f32)


def cols_dot(left, right):
    return lax.dot_general(left, right, (((1,), (1,)), ((), ())), preferred_element_type=f32)


def dot(left, right):
    return jnp.dot(left, right, preferred_element_type=f32)


def turn(value, axis, step):
    count = lax.axis_size(axis)
    return lax.ppermute(value, axis, [(i, (i + step) % count) for i in range(count)])


def tie(*values):
    return lax.optimization_barrier(values)


def put_rows(out, piece, at):
    return out.at[pl.ds(pl.multiple_of(at[0], 128), piece[0])]


def put_columns(out, piece, at):
    return out.at[:, pl.ds(pl.multiple_of(at[0], 128), piece[1])]


def place(pieces, offsets, shape, put=put_rows, dtype=None):
    count = len(pieces)
    kept = pieces[0].dtype
    dtype = dtype or kept
    wider = dtype != kept
    offsets = [at if isinstance(at, tuple) else (at,) for at in offsets]
    per = len(offsets[0])

    def kernel(offs, *refs):
        out = refs[count]
        held = refs[count + 1 : 2 * count + 1]
        sent = refs[2 * count + 1 : 3 * count + 1] if wider else held
        sems = refs[-1]

        def bring(j):
            return pltpu.make_async_copy(refs[j], held[j], sems.at[0, j])

        def send(j):
            at = [jnp.maximum(offs[j * per + i], 0) for i in range(per)]
            return pltpu.make_async_copy(sent[j], put(out, pieces[j].shape, at), sems.at[1, j])

        def each(action):
            for j in range(count):

                @pl.when(offs[j * per] >= 0)
                def _(j=j):
                    action(j)

        def forward(j):
            bring(j).wait()
            if wider:
                sent[j][...] = held[j][...].astype(dtype)
            send(j).start()

        each(lambda j: bring(j).start())
        each(forward)
        each(lambda j: send(j).wait())

    anywhere = pl.BlockSpec(memory_space=pl.ANY)
    size = int(np.prod(shape))
    buffers = [pltpu.VMEM(piece.shape, kept) for piece in pieces]
    if wider:
        buffers += [pltpu.VMEM(piece.shape, dtype) for piece in pieces]
    return pl.pallas_call(
        kernel,
        out_shape=jax.ShapeDtypeStruct(shape, dtype),
        grid_spec=pltpu.PrefetchScalarGridSpec(
            num_scalar_prefetch=1,
            grid=(1,),
            in_specs=[anywhere] * count,
            out_specs=anywhere,
            scratch_shapes=buffers + [pltpu.SemaphoreType.DMA((2, count))],
        ),
        cost_estimate=pl.CostEstimate(flops=0, transcendentals=0, bytes_accessed=4 * size),
        name="place",
    )(jnp.stack([jnp.asarray(o, jnp.int32) for at in offsets for o in at]), *pieces)


def swap(value, mask):
    count = lax.axis_size("seq")
    return lax.ppermute(value, "seq", [(i, i ^ mask) for i in range(count)])


def gather_start(part):
    half = part.shape[0] // 2
    if lax.axis_size("seq") != 8 or half % 128:
        return [lax.all_gather(part, "seq", axis=0, tiled=True)]
    top, low = part[:half], part[half:]
    return [top, low, swap(top, 2), swap(low, 4), swap(top, 4), swap(low, 2)]


def gather_next(held):
    return held if len(held) == 1 else held + [swap(held[2], 4), swap(held[3], 2)]


def gather_last(held):
    if len(held) == 1:
        return held[0]
    count, mine = lax.axis_size("seq"), lax.axis_index("seq")
    half, width = held[0].shape
    places = [(0, 0), (0, 1), (2, 0), (4, 1), (4, 0), (2, 1), (6, 0), (6, 1)]
    pieces = dict(zip(places, held))
    pieces |= {(mask | 1, side): swap(piece, 1) for (mask, side), piece in pieces.items()}
    offsets = [((mine ^ mask) * 2 + side) * half for mask, side in pieces]
    return place(list(pieces.values()), offsets, (2 * half * count, width))


def gather_columns(block, axis):
    count, mine = lax.axis_size(axis), lax.axis_index(axis)
    width = block.shape[1]
    pieces = [block] + [turn(block, axis, step) for step in range(1, count)]
    offsets = [((mine - step) % count) * width for step in range(count)]
    return place(pieces, offsets, (block.shape[0], width * count), put_columns)


def rows_sent(value):
    count, mine = lax.axis_size("head"), lax.axis_index("head")
    rows, width = value.shape[0] // count, value.shape[1]

    def block(k):
        return lax.dynamic_slice_in_dim(value, ((mine + k) % count) * rows, rows, 0)

    pieces = [block(0)] + [turn(block(k), "head", k) for k in range(1, count)]
    return pieces, [((mine - k) % count) * width for k in range(count)]


def columns_sent(value):
    count, mine = lax.axis_size("head"), lax.axis_index("head")
    rows, width = value.shape[0], value.shape[1] // count

    def block(k):
        return lax.dynamic_slice_in_dim(value, ((mine + k) % count) * width, width, 1)

    pieces = [block(0)] + [turn(block(k), "head", k) for k in range(1, count)]
    return pieces, [((mine - k) % count) * rows for k in range(count)]


def along(value, step):
    count = lax.axis_size("head")
    pairs = [(i, i + step) for i in range(count) if 0 <= i + step < count]
    return lax.ppermute(value, "head", pairs)


def sum_parts(parts, far, low=None, high=None):
    count = lax.axis_size("head")
    up, down = parts[-far % count], parts[far]
    if low is not None:
        up = (up.astype(f32) + low.astype(f32)).astype(bf16)
        down = (down.astype(f32) + high.astype(f32)).astype(bf16)
    return up, down


def sum_send(up, down, far):
    count = lax.axis_size("head")
    return (
        lax.ppermute(up, "head", [(i, i + 1) for i in range(count - far)]),
        lax.ppermute(down, "head", [(i, i - 1) for i in range(far, count)]),
    )


def sum_step(parts, far, low=None, high=None):
    return sum_send(*sum_parts(parts, far, low, high), far)


def join_line(own, from_low, from_high, dtype=None):
    count, mine = lax.axis_size("head"), lax.axis_index("head")
    rows = own.shape[0]
    pieces, offsets = [own], [mine * rows]
    for far, (low, high) in enumerate(zip(from_low, from_high), 1):
        pieces += [low, high]
        offsets.append((mine - far) * rows)
        offsets.append(jnp.where(mine + far < count, (mine + far) * rows, -1))
    return place(pieces, offsets, (rows * count, own.shape[1]), dtype=dtype)


def neighbour_sums(tail, all_ids, step, reach):
    count, mine = lax.axis_size("seq"), lax.axis_index("seq")
    theirs, own = (all_ids[:, -1], all_ids[:, 0]) if step > 0 else (all_ids[:, 0], all_ids[:, -1])
    own = lax.dynamic_index_in_dim(own, mine, 0, keepdims=False)
    total = jnp.zeros(tail.shape, f32)
    for k in range(1, min(reach, count - 1) + 1):
        pairs = [(i, i + k * step) for i in range(count) if 0 <= i + k * step < count]
        got = lax.ppermute(tail, "seq", pairs)
        at = mine - k * step
        other = lax.dynamic_index_in_dim(theirs, jnp.clip(at, 0, count - 1), 0, keepdims=False)
        use = (at >= 0) & (at < count) & (other == own)
        total = total + jnp.where(use, got.astype(f32), 0.0)
    return total


def body(tokens, seq_ids, gain_attn, w_qk, w_v, w_out, gain_mlp, w_gate, w_up, w_down, cotangent):
    zc, z = lax.axis_size("head"), lax.axis_index("head")
    token_count, width = tokens.shape
    blocks = seq_ids.shape[0]
    block_len = token_count // blocks
    heads_here = w_v.shape[1] // HV
    qk_cols = w_qk.shape[1]
    share = token_count // zc
    reach = -(-(MAX_BLOCKS - 1) // blocks)

    small = jnp.pad(seq_ids.astype(bf16), (0, gain_attn.shape[0] - blocks))
    small = jnp.stack([gain_attn, gain_mlp, small])
    small = lax.all_gather(small, "seq", axis=1, tiled=True).astype(f32)
    gain_one, gain_two = small[0], small[1]
    all_ids = small[2].reshape(lax.axis_size("seq"), gain_attn.shape[0])[:, :blocks]
    qkv_part = jnp.concatenate([w_qk, w_v], axis=1)
    full_qkv = lax.all_gather(qkv_part, "seq", axis=0, tiled=True)
    full_both = lax.all_gather(
        jnp.concatenate([w_gate, w_up], axis=1), "seq", axis=0, tiled=True
    )
    out_rows = gather_columns(w_out, "head")

    inputs = tokens.astype(f32)
    scale_one = lax.rsqrt(jnp.mean(inputs * inputs, axis=-1, keepdims=True) + epsilon)
    normed = (inputs * scale_one * gain_one).astype(bf16)
    qkv_blocks = {k: turn(qkv_part, "head", k) for k in range(1, zc)}
    full_qkv, normed, out_rows, qkv_blocks[1], qkv_blocks[zc - 1] = tie(
        full_qkv, normed, out_rows, qkv_blocks[1], qkv_blocks[zc - 1]
    )
    full_out = lax.all_gather(out_rows, "seq", axis=0, tiled=True)
    proj = dot(normed, full_qkv).astype(bf16)
    tables = selection_tables(heads_here)
    tail_call, inner_call, forward_call, grad_tail_call, local_call, backward_call = (
        attention_calls(blocks, block_len, heads_here, tables)
    )
    tail, qkv_blocks[2] = tie(tail_call(seq_ids, proj), qkv_blocks[2])
    qkv_rows = place(
        [qkv_part] + [qkv_blocks[k] for k in range(1, zc)],
        [((z - k) % zc) * qkv_part.shape[1] for k in range(zc)],
        (qkv_part.shape[0], qkv_part.shape[1] * zc),
        put_columns,
    )
    incoming = neighbour_sums(tail, all_ids, 1, reach)
    inner = inner_call(seq_ids, tie(proj, tail)[0])
    incoming, *inner = tie(incoming, *inner)
    head_rows, numerator, denominator, states = forward_call(seq_ids, proj, *inner, incoming)
    down_held = gather_start(tie(w_down, head_rows)[0])
    all_qkv = lax.all_gather(qkv_rows, "seq", axis=0, tiled=True)

    heads_own = place(*rows_sent(head_rows), (share, heads_here * HV * zc), put_columns)
    own_in = lax.dynamic_slice_in_dim(tokens, z * share, share, 0).astype(f32)
    residual = own_in + dot(heads_own, full_out)
    scale_two = lax.rsqrt(jnp.mean(residual * residual, axis=-1, keepdims=True) + epsilon)
    normed_own = (residual * scale_two * gain_two).astype(bf16)

    normed_own, *down_held = tie(normed_own, *down_held)
    full_down = gather_last(gather_next(down_held))
    order = [0] + sorted(range(1, zc), key=lambda k: min(k, zc - k))
    hidden = w_gate.shape[1]
    normed_parts, cot_parts, act_parts, both_parts = [], [], [], []
    backs = {}
    got_first, first_own, later = tie(turn(normed_own, "head", order[1]), normed_own, normed_own)
    arrivals = {0: first_own, order[1]: got_first}
    for k in order[2:]:
        arrivals[k] = turn(later, "head", k)
    for k in order:
        normed_two = arrivals[k]
        owner = (z - k) % zc
        cot = lax.dynamic_slice_in_dim(cotangent, owner * share, share, 0)
        pre = dot(normed_two, full_both)
        gate_pre, up_pre = pre[:, :hidden], pre[:, hidden:]
        gate_sigmoid = jax.nn.sigmoid(gate_pre)
        active = (gate_pre * gate_sigmoid * up_pre).astype(bf16)
        grad_active = dot(cot, full_down)
        grad_gate = grad_active * up_pre * gate_sigmoid * (1.0 + gate_pre * (1.0 - gate_sigmoid))
        grad_upper = grad_active * gate_pre * gate_sigmoid
        grad_both = jnp.concatenate([grad_gate.astype(bf16), grad_upper.astype(bf16)], axis=1)
        backs[k] = cols_dot(grad_both, full_both)
        if k:
            backs[k] = backs[k].astype(bf16)
        if k != order[-1]:
            following = order[order.index(k) + 1]
            arrivals[following], backs[k] = tie(arrivals[following], backs[k])
        normed_parts.append(normed_two)
        cot_parts.append(cot)
        act_parts.append(active)
        both_parts.append(grad_both)
    low = high = None
    for far in range(zc - 1, 2, -1):
        low, high = sum_step(backs, far, low, high)
    up, down = sum_parts(backs, 2, low, high)
    up, down, normed_parts[0], both_parts[0], cot_parts[0], *act_parts = tie(
        up, down, normed_parts[0], both_parts[0], cot_parts[0], *act_parts
    )
    low, high = sum_send(up, down, 2)
    both_grad = rows_dot(jnp.concatenate(normed_parts), jnp.concatenate(both_parts)).astype(bf16)
    low, high, act_parts[0], both_grad = tie(low, high, act_parts[0], both_grad)
    both_shard = lax.psum_scatter(both_grad, "seq", scatter_dimension=0, tiled=True)
    up, down = sum_parts(backs, 1, low, high)
    up, down, *act_parts = tie(up, down, *act_parts)
    low, high = sum_send(up, down, 1)
    outs = {k: cols_dot(active, full_down) for k, active in zip(order, act_parts)}
    outs = {k: out.astype(bf16) if k else out for k, out in outs.items()}
    down_grad = rows_dot(jnp.concatenate(cot_parts), jnp.concatenate(act_parts)).astype(bf16)
    tied = tie(backs[0], low, high, all_qkv, down_grad, *[outs[k] for k in order])
    grad_normed = tied[0] + tied[1].astype(f32) + tied[2].astype(f32)
    all_qkv, down_grad = tied[3:5]
    down_shard = lax.psum_scatter(down_grad, "seq", scatter_dimension=0, tiled=True)
    outs = dict(zip(order, tied[5:]))

    cot_own = lax.dynamic_slice_in_dim(cotangent, z * share, share, 0).astype(f32)
    weighted = grad_normed * gain_two
    grad_mid = (
        cot_own
        + scale_two * weighted
        - residual * scale_two**3 * jnp.mean(weighted * residual, axis=-1, keepdims=True)
    )
    gain_two_term = jnp.sum(grad_normed * residual * scale_two, axis=0)
    grad_branch = grad_mid.astype(bf16)
    grad_heads = cols_dot(grad_branch, full_out).astype(bf16)
    pieces, offsets = columns_sent(grad_heads)
    pieces[1], heads_own = tie(pieces[1], heads_own)
    out_grad = rows_dot(heads_own, grad_branch).astype(bf16)
    pieces[2], out_grad = tie(pieces[2], out_grad)
    grad_heads = place(pieces, offsets, (token_count, grad_heads.shape[1] // zc))
    grad_heads, low, high = tie(grad_heads, *sum_step(outs, zc - 1))
    low, high = sum_step(outs, 2, low, high)
    dnum, head_part = grad_tail_call(seq_ids, proj, grad_heads, numerator, denominator)
    outgoing = neighbour_sums(head_part, all_ids, -1, reach)
    partial = local_call(seq_ids, proj, dnum, states)
    outgoing, low, high, partial = tie(outgoing, low, high, partial)
    low, high = sum_step(outs, 1, low, high)
    grad_qkv = backward_call(seq_ids, proj, dnum, partial, outgoing)
    grad_qkv, low, high, both_shard, out_grad = tie(grad_qkv, low, high, both_shard, out_grad)
    out_part = lax.psum_scatter(out_grad, "seq", scatter_dimension=0, tiled=True)
    result_own = (residual + outs[0] + low.astype(f32) + high.astype(f32)).astype(bf16)
    qkv_grad = rows_dot(normed, grad_qkv)

    own_pieces, own_columns = rows_sent(grad_qkv)
    own_pieces[1], result_own = tie(own_pieces[1], result_own)
    res_low, res_high = [along(result_own, 1)], [along(result_own, -1)]
    own_qkv = place(own_pieces, own_columns, (share, grad_qkv.shape[1] * zc), put_columns)
    grad_norm_one = cols_dot(own_qkv, all_qkv)
    grad_norm_one, res_low[0], res_high[0], down_shard = tie(
        grad_norm_one, res_low[0], res_high[0], down_shard
    )
    own_scale = lax.dynamic_slice_in_dim(scale_one, z * share, share, 0)
    weighted_one = grad_norm_one * gain_one
    grad_own = (
        grad_mid
        + own_scale * weighted_one
        - own_in * own_scale**3 * jnp.mean(weighted_one * own_in, axis=-1, keepdims=True)
    )
    gain_one_term = jnp.sum(grad_norm_one * own_in * own_scale, axis=0)
    tok_own, gain_one_term = tie(grad_own.astype(bf16), gain_one_term)
    out_cols = w_out.shape[1]
    tok_low, tok_high = [along(tok_own, 1)], [along(tok_own, -1)]
    tok_low[0], out_part = tie(tok_low[0], out_part)
    out_shard = lax.dynamic_slice_in_dim(out_part, z * out_cols, out_cols, 1).astype(f32)
    for far in range(2, zc):
        res_low.append(along(res_low[-1], 1))
        res_high.append(along(res_high[-1], -1))
        tok_low.append(along(tok_low[-1], 1))
        tok_high.append(along(tok_high[-1], -1))
    got = []
    for k in range(1, zc):
        block = lax.dynamic_slice_in_dim(out_part, ((z + k) % zc) * out_cols, out_cols, 1)
        got.append(turn(tie(block, tok_low[1])[0], "head", k))

    def scatter(grad):
        return lax.psum_scatter(grad, "seq", scatter_dimension=0, tiled=True)

    down_shard = down_shard.astype(f32)
    both_shard = both_shard.astype(f32)
    gain_terms = jnp.pad(jnp.stack([gain_one_term, gain_two_term], axis=1), ((0, 0), (0, 126)))
    last = scatter(jnp.concatenate([qkv_grad, gain_terms], axis=1).astype(bf16)).astype(f32)
    gain_own = last[:, -128:-126].T[None]
    gain_parts = [gain_own] + [turn(gain_own, "head", k) for k in range(1, zc)]
    tok_low[-1], tok_high[-1], *tied = tie(tok_low[-1], tok_high[-1], *gain_parts, *got)
    gain_parts, got = tied[:zc], tied[zc:]
    for part in got:
        out_shard = out_shard + part.astype(f32)
    gain_all = jnp.zeros((zc,) + gain_own.shape[1:], f32)
    for k, part in enumerate(gain_parts):
        gain_all = lax.dynamic_update_slice_in_dim(gain_all, part, (z - k) % zc, 0)
    gain_sums = jnp.sum(gain_all, axis=0)
    grad_tokens = join_line(tok_own, tok_low, tok_high, f32)
    result = join_line(result_own, res_low, res_high)
    return (
        result,
        grad_tokens,
        last[:, :qk_cols],
        last[:, qk_cols:-128],
        out_shard,
        both_shard[:, :hidden],
        both_shard[:, hidden:],
        down_shard,
        gain_sums[0],
        gain_sums[1],
    )


def solution(mesh):
    return jax.shard_map(
        body,
        mesh=mesh,
        in_specs=(
            P("seq", None),
            P("seq"),
            P("seq"),
            P("seq", "head"),
            P("seq", "head"),
            P("seq", "head"),
            P("seq"),
            P("seq", "head"),
            P("seq", "head"),
            P("seq", "head"),
            P("seq", None),
        ),
        out_specs=(
            P("seq", None),
            P("seq", None),
            P("seq", "head"),
            P("seq", "head"),
            P("seq", "head"),
            P("seq", "head"),
            P("seq", "head"),
            P("seq", "head"),
            P("seq"),
            P("seq"),
        ),
        check_vma=False,
    )
```

```python
import math

import jax
import jax.numpy as jnp
import numpy as np
from jax import lax
from jax.experimental import pallas as pl
from jax.experimental.pallas import tpu as pltpu
from jax.sharding import PartitionSpec as P

FEAT = 16
HV = 128
MAX_BLOCKS = 16


epsilon = 1e-06
bf16 = jnp.bfloat16
f32 = jnp.float32


FS = 160
FL = 256


def selection_tables(heads):
    pairs = [(a, b) for a in range(FEAT) for b in range(a, FEAT)]
    first = np.zeros((FEAT, FL), np.float32)
    second = np.zeros((FEAT, FL), np.float32)
    one_a, one_b = np.zeros(FL, np.float32), np.zeros(FL, np.float32)
    scale, twice = np.zeros(FL, np.float32), np.ones(FL, np.float32)
    one_a[0] = one_b[0] = scale[0] = 1.0
    for a in range(FEAT):
        first[a, 1 + a] = 1.0
        one_b[1 + a] = 1.0
        scale[1 + a] = 1.0 / FEAT**0.25
    for at, (a, b) in enumerate(pairs):
        at += 1 + FEAT
        first[a, at] = second[b, at] = 1.0
        scale[at] = 1.0 / (math.sqrt(2.0) * FEAT**0.5)
        twice[at] = 1.0 if a == b else 2.0
    cols = heads * 2 * FEAT
    wide = np.zeros((4, heads, cols, FL), np.float32)
    moves = np.zeros((2, heads, cols, cols), np.float32)
    for h in range(heads):
        q0, k0 = h * 2 * FEAT, h * 2 * FEAT + FEAT
        wide[0, h, q0:k0], wide[1, h, q0:k0] = first, second
        wide[2, h, k0 : k0 + FEAT], wide[3, h, k0 : k0 + FEAT] = first, second
        for a in range(FEAT):
            moves[0, h, k0 + a, q0 + a] = 1.0
            moves[1, h, q0 + a, k0 + a] = 1.0
    tall = np.swapaxes(wide, 2, 3)[:, :, :FS]
    rows = np.zeros((8, FL), np.float32)
    rows[0], rows[1], rows[2], rows[3] = one_a, one_b, scale, twice
    columns = np.repeat(rows[:3, :FS, None], cols, axis=2)
    return (
        jnp.asarray(wide, bf16),
        jnp.asarray(np.ascontiguousarray(tall), bf16),
        jnp.asarray(moves, bf16),
        jnp.asarray(rows, f32),
        jnp.asarray(columns, f32),
    )


def mm(left, right):
    return lax.dot_general(left, right, (((1,), (0,)), ((), ())), preferred_element_type=f32)


def mm_nt(left, right):
    return lax.dot_general(left, right, (((1,), (1,)), ((), ())), preferred_element_type=f32)


def lane_marks(rows, lanes):
    lane = lax.broadcasted_iota(jnp.int32, (rows, HV), 1)
    return (lane < lanes).astype(bf16)


def features_wide(x, first, second, rows):
    one = mm(x, first) + rows[0:1]
    two = mm(x, second) + rows[1:2]
    return one, two, (one * two) * rows[2:3]


def features_tall(x, first, second, columns):
    one = mm_nt(first, x) + columns[0]
    two = mm_nt(second, x) + columns[1]
    return ((one * two) * columns[2]).astype(bf16)


def split_state(state):
    left, right = state[:, :HV], state[:, HV:]
    lane = lax.broadcasted_iota(jnp.int32, right.shape, 1)
    high = right.astype(bf16)
    low = (right - high.astype(f32)).astype(bf16)
    return left.astype(bf16), jnp.where(lane == 2, low, high)


def join_state(state, both):
    right = state[:, HV:]
    lane = lax.broadcasted_iota(jnp.int32, right.shape, 1)
    whole = right[:, 0:1] + right[:, 2:3]
    if both:
        new = jnp.where(lane < 3, whole, 0.0)
    else:
        new = jnp.where(lane == 1, right, jnp.where(lane < 3, whole, 0.0))
    return jnp.concatenate([state[:, :HV], new], axis=1)


def tail_kernel(ids, proj, tall, columns, out, acc):
    at, last = pl.program_id(0), pl.num_programs(0) - 1
    heads = out.shape[0]
    qk = heads * 2 * FEAT

    @pl.when(at == 0)
    def _():
        acc[...] = jnp.zeros_like(acc)

    @pl.when(ids[at] == ids[last])
    def _():
        x = proj[:, :qk]
        marks = lane_marks(x.shape[0], 3)
        for h in range(heads):
            tall_k = features_tall(x, tall[2, h], tall[3, h], columns)
            v = proj[:, qk + h * HV : qk + (h + 1) * HV]
            acc[h] += mm(tall_k, jnp.concatenate([v, marks], axis=1))

    @pl.when(at == last)
    def _():
        for h in range(heads):
            left, right = split_state(acc[h])
            out[h, :, :HV] = left
            out[h, :, HV:] = right


def inner_kernel(ids, proj, moves, num_out, den_out):
    heads = moves.shape[1]
    qk = heads * 2 * FEAT
    x = proj[:, :qk]
    size = x.shape[0]
    row = lax.broadcasted_iota(jnp.int32, (size, size), 0)
    col = lax.broadcasted_iota(jnp.int32, (size, size), 1)
    lane = lax.broadcasted_iota(jnp.int32, (size, HV), 1)
    dens = jnp.zeros((size, HV), f32)
    for h in range(heads):
        v = proj[:, qk + h * HV : qk + (h + 1) * HV]
        moved = mm(x, moves[0, h]).astype(bf16)
        s = mm_nt(x, moved) * FEAT**-0.5
        a = jnp.where(row >= col, 1.0 + s + 0.5 * s * s, 0.0)
        num_out[:, h * HV : (h + 1) * HV] = mm(a.astype(bf16), v)
        dens = jnp.where(lane == h, jnp.sum(a, axis=1, keepdims=True), dens)
    den_out[...] = dens


def forward_kernel(
    ids, proj, num_in, den_in, incoming, wide, tall, rows, columns, heads_out, num_out, den_out, state_out, acc
):
    at = pl.program_id(0)
    heads = acc.shape[0]
    qk = heads * 2 * FEAT

    @pl.when(at == 0)
    def _():
        for h in range(heads):
            acc[h] = join_state(incoming[h], True)

    @pl.when((at > 0) & (ids[at] != ids[jnp.maximum(at - 1, 0)]))
    def _():
        acc[...] = jnp.zeros_like(acc)

    x = proj[:, :qk]
    size = x.shape[0]
    marks = lane_marks(size, 3)
    lane = lax.broadcasted_iota(jnp.int32, (size, HV), 1)
    dens = jnp.zeros((size, HV), f32)
    for h in range(heads):
        v = proj[:, qk + h * HV : qk + (h + 1) * HV]
        left, right = split_state(acc[h])
        state = jnp.concatenate(
            [jnp.concatenate([left, right], axis=1), jnp.zeros((FL - FS, 2 * HV), bf16)], axis=0
        )
        state_out[0, h] = state
        _, _, fq = features_wide(x, wide[0, h], wide[1, h], rows)
        fq = fq.astype(bf16) * rows[3:4].astype(bf16)
        ext = mm(fq, state)
        num = num_in[:, h * HV : (h + 1) * HV] + ext[:, :HV]
        den = den_in[:, h : h + 1] + ext[:, HV : HV + 1] + ext[:, HV + 2 : HV + 3]
        heads_out[:, h * HV : (h + 1) * HV] = (num * (1.0 / den)).astype(bf16)
        num_out[:, h * HV : (h + 1) * HV] = num
        dens = jnp.where(lane == h, den, dens)
        tall_k = features_tall(x, tall[2, h], tall[3, h], columns)
        acc[h] += mm(tall_k, jnp.concatenate([v, marks], axis=1))
    den_out[...] = dens


def grad_tail_kernel(ids, proj, dheads, num, den, tall, columns, dnum_out, out, acc):
    at, last = pl.program_id(0), pl.num_programs(0) - 1
    heads = out.shape[0]
    qk = heads * 2 * FEAT

    @pl.when(at == 0)
    def _():
        acc[...] = jnp.zeros_like(acc)

    x = proj[:, :qk]
    size = x.shape[0]
    lane = lax.broadcasted_iota(jnp.int32, (size, HV), 1)
    for h in range(heads):
        d = den[:, h : h + 1]
        g = dheads[:, h * HV : (h + 1) * HV].astype(f32)
        inverse = 1.0 / d
        dnum = (g * inverse).astype(bf16)
        dden = -jnp.sum(g * num[:, h * HV : (h + 1) * HV], axis=1, keepdims=True) * (
            inverse * inverse
        )
        high = dden.astype(bf16)
        low = (dden - high.astype(f32)).astype(bf16)
        side = jnp.where(
            (lane == 0) | (lane == 2), high.astype(f32), jnp.where(lane == 1, low.astype(f32), 0.0)
        ).astype(bf16)
        dnum_out[:, h * 2 * HV : h * 2 * HV + HV] = dnum
        dnum_out[:, h * 2 * HV + HV : (h + 1) * 2 * HV] = side

    @pl.when(ids[at] == ids[0])
    def _():
        for h in range(heads):
            tall_q = features_tall(x, tall[0, h], tall[1, h], columns)
            acc[h] += mm(tall_q, dnum_out[:, h * 2 * HV : (h + 1) * 2 * HV])

    @pl.when(at == last)
    def _():
        for h in range(heads):
            left, right = split_state(acc[h])
            out[h, :, :HV] = left
            out[h, :, HV:] = right


def local_kernel(ids, proj, dnum_in, state_in, wide, moves, rows, out):
    heads = moves.shape[1]
    qk = heads * 2 * FEAT
    x = proj[:, :qk]
    size = x.shape[0]
    row = lax.broadcasted_iota(jnp.int32, (size, size), 0)
    col = lax.broadcasted_iota(jnp.int32, (size, size), 1)
    marks = lane_marks(size, 2)
    weight = rows[2:3] * rows[3:4]
    total = jnp.zeros((size, qk), f32)
    for h in range(heads):
        v = proj[:, qk + h * HV : qk + (h + 1) * HV]
        dn = dnum_in[:, h * 2 * HV : (h + 1) * 2 * HV]
        q1, q2, _ = features_wide(x, wide[0, h], wide[1, h], rows)
        kq = mm(x, moves[0, h]).astype(bf16)
        qk_moved = mm(x, moves[1, h]).astype(bf16)
        s = mm_nt(x, kq) * FEAT**-0.5
        st = mm_nt(kq, x) * FEAT**-0.5
        at_low = jnp.where(row <= col, 1.0 + st + 0.5 * st * st, 0.0).astype(bf16)
        v2 = jnp.concatenate([v, marks], axis=1)
        da = mm_nt(dn, v2)
        dat = mm_nt(v2, dn)
        draw = jnp.where(row >= col, da * (1.0 + s) * FEAT**-0.5, 0.0).astype(bf16)
        drawt = jnp.where(row <= col, dat * (1.0 + st) * FEAT**-0.5, 0.0).astype(bf16)
        wq = mm_nt(dn, state_in[0, h]) * weight
        total += (
            mm(draw, kq)
            + mm(drawt, qk_moved)
            + mm_nt((wq * q2).astype(bf16), wide[0, h])
            + mm_nt((wq * q1).astype(bf16), wide[1, h])
        )
        out[:, qk + h * HV : qk + (h + 1) * HV] = mm(at_low, dn[:, :HV])
    out[:, :qk] = total


def backward_kernel(ids, proj, dnum_in, local, incoming, wide, tall, rows, columns, out, acc):
    step, last = pl.program_id(0), pl.num_programs(0) - 1
    at = last - step
    heads = acc.shape[0]
    qk = heads * 2 * FEAT

    @pl.when(step == 0)
    def _():
        for h in range(heads):
            acc[h] = join_state(incoming[h], False)

    @pl.when((step > 0) & (ids[at] != ids[jnp.minimum(at + 1, last)]))
    def _():
        acc[...] = jnp.zeros_like(acc)

    x = proj[:, :qk]
    marks = lane_marks(x.shape[0], 3)
    weight = rows[2:3] * rows[3:4]
    twice = rows[3:4].astype(bf16)
    total = local[:, :qk]
    for h in range(heads):
        v = proj[:, qk + h * HV : qk + (h + 1) * HV]
        left, right = split_state(acc[h])
        dstate = jnp.concatenate(
            [jnp.concatenate([left, right], axis=1), jnp.zeros((FL - FS, 2 * HV), bf16)], axis=0
        )
        k1, k2, fk = features_wide(x, wide[2, h], wide[3, h], rows)
        fk = fk.astype(bf16) * twice
        wk = mm_nt(jnp.concatenate([v, marks], axis=1), dstate) * weight
        total += mm_nt((wk * k2).astype(bf16), wide[2, h]) + mm_nt(
            (wk * k1).astype(bf16), wide[3, h]
        )
        dv = local[:, qk + h * HV : qk + (h + 1) * HV] + mm(fk, dstate[:, :HV])
        out[:, qk + h * HV : qk + (h + 1) * HV] = dv.astype(bf16)
        tall_q = features_tall(x, tall[0, h], tall[1, h], columns)
        acc[h] += mm(tall_q, dnum_in[:, h * 2 * HV : (h + 1) * 2 * HV])
    out[:, :qk] = total.astype(bf16)


def whole_spec(array):
    zeros = (0,) * array.ndim
    return pl.BlockSpec(array.shape, lambda i, ids: zeros)


def attention_calls(blocks, block_len, heads, tables):
    wide, tall, moves, rows, columns = tables
    qk = heads * 2 * FEAT
    tokens = blocks * block_len
    state = (heads, FS, 2 * HV)

    def at_block(cols, reverse=False):
        if reverse:
            return pl.BlockSpec((block_len, cols), lambda i, ids: (blocks - 1 - i, 0))
        return pl.BlockSpec((block_len, cols), lambda i, ids: (i, 0))

    def states_spec(reverse=False):
        if reverse:
            return pl.BlockSpec((1, heads, FL, 2 * HV), lambda i, ids: (blocks - 1 - i, 0, 0, 0))
        return pl.BlockSpec((1, heads, FL, 2 * HV), lambda i, ids: (i, 0, 0, 0))

    def call(kernel, name, in_specs, out_specs, out_shape, flops, moved, carried=True):
        return pl.pallas_call(
            kernel,
            out_shape=out_shape,
            grid_spec=pltpu.PrefetchScalarGridSpec(
                num_scalar_prefetch=1,
                grid=(blocks,),
                in_specs=in_specs,
                out_specs=out_specs,
                scratch_shapes=[pltpu.VMEM(state, f32)] if carried else [],
            ),
            compiler_params=pltpu.CompilerParams(dimension_semantics=("arbitrary",)),
            cost_estimate=pl.CostEstimate(flops=flops, transcendentals=0, bytes_accessed=moved),
            name=name,
        )

    full_state = pl.BlockSpec(state, lambda i, ids: (0, 0, 0))
    proj_cols = qk + heads * HV

    def tail(ids, proj):
        return call(
            tail_kernel,
            "state_tail",
            [at_block(proj_cols), whole_spec(tall), whole_spec(columns)],
            full_state,
            jax.ShapeDtypeStruct(state, bf16),
            int(4e9),
            int(4e6),
        )(ids, proj, tall, columns)

    def inner(ids, proj):
        return call(
            inner_kernel,
            "attention_inner",
            [at_block(proj_cols), whole_spec(moves)],
            [at_block(heads * HV), at_block(HV)],
            [
                jax.ShapeDtypeStruct((tokens, heads * HV), f32),
                jax.ShapeDtypeStruct((tokens, HV), f32),
            ],
            int(4e9),
            int(4e6),
            False,
        )(ids, proj, moves)

    def forward(ids, proj, num, den, incoming):
        return call(
            forward_kernel,
            "attention_forward",
            [at_block(proj_cols), at_block(heads * HV), at_block(HV), full_state]
            + [whole_spec(t) for t in (wide, tall, rows, columns)],
            [at_block(heads * HV), at_block(heads * HV), at_block(HV), states_spec()],
            [
                jax.ShapeDtypeStruct((tokens, heads * HV), bf16),
                jax.ShapeDtypeStruct((tokens, heads * HV), f32),
                jax.ShapeDtypeStruct((tokens, HV), f32),
                jax.ShapeDtypeStruct((blocks, heads, FL, 2 * HV), bf16),
            ],
            int(6e9),
            int(2e7),
        )(ids, proj, num, den, incoming, wide, tall, rows, columns)

    def grad_tail(ids, proj, dheads, num, den):
        return call(
            grad_tail_kernel,
            "state_grad_tail",
            [at_block(proj_cols), at_block(heads * HV), at_block(heads * HV), at_block(HV)]
            + [whole_spec(tall), whole_spec(columns)],
            [at_block(heads * 2 * HV), full_state],
            [
                jax.ShapeDtypeStruct((tokens, heads * 2 * HV), bf16),
                jax.ShapeDtypeStruct(state, bf16),
            ],
            int(4e9),
            int(1e7),
        )(ids, proj, dheads, num, den, tall, columns)

    def local(ids, proj, dnum, states):
        return call(
            local_kernel,
            "attention_backward_local",
            [at_block(proj_cols), at_block(heads * 2 * HV), states_spec()]
            + [whole_spec(t) for t in (wide, moves, rows)],
            at_block(proj_cols),
            jax.ShapeDtypeStruct((tokens, proj_cols), f32),
            int(1.3e10),
            int(2e7),
            False,
        )(ids, proj, dnum, states, wide, moves, rows)

    def backward(ids, proj, dnum, partial, incoming):
        return call(
            backward_kernel,
            "attention_backward",
            [at_block(proj_cols, True), at_block(heads * 2 * HV, True)]
            + [at_block(proj_cols, True), full_state]
            + [whole_spec(t) for t in (wide, tall, rows, columns)],
            at_block(proj_cols, True),
            jax.ShapeDtypeStruct((tokens, proj_cols), bf16),
            int(1e10),
            int(2e7),
        )(ids, proj, dnum, partial, incoming, wide, tall, rows, columns)

    return tail, inner, forward, grad_tail, local, backward


def rows_dot(left, right):
    return lax.dot_general(left, right, (((0,), (0,)), ((), ())), preferred_element_type=f32)


def cols_dot(left, right):
    return lax.dot_general(left, right, (((1,), (1,)), ((), ())), preferred_element_type=f32)


def dot(left, right):
    return jnp.dot(left, right, preferred_element_type=f32)


def turn(value, axis, step):
    count = lax.axis_size(axis)
    return lax.ppermute(value, axis, [(i, (i + step) % count) for i in range(count)])


def tie(*values):
    return lax.optimization_barrier(values)


def put_rows(out, piece, at):
    return out.at[pl.ds(pl.multiple_of(at[0], 128), piece[0])]


def put_columns(out, piece, at):
    return out.at[:, pl.ds(pl.multiple_of(at[0], 128), piece[1])]


def place(pieces, offsets, shape, put=put_rows, dtype=None, base=None):
    count = len(pieces)
    kept = pieces[0].dtype
    dtype = dtype or kept
    wider = dtype != kept
    offsets = [at if isinstance(at, tuple) else (at,) for at in offsets]
    per = len(offsets[0])

    given = count + (base is not None)

    def kernel(offs, *refs):
        out = refs[given]
        held = refs[given + 1 : given + count + 1]
        sent = refs[given + count + 1 : given + 2 * count + 1] if wider else held
        sems = refs[-1]

        def bring(j):
            return pltpu.make_async_copy(refs[j], held[j], sems.at[0, j])

        def send(j):
            at = [jnp.maximum(offs[j * per + i], 0) for i in range(per)]
            return pltpu.make_async_copy(sent[j], put(out, pieces[j].shape, at), sems.at[1, j])

        def each(action):
            for j in range(count):

                @pl.when(offs[j * per] >= 0)
                def _(j=j):
                    action(j)

        def forward(j):
            bring(j).wait()
            if wider:
                sent[j][...] = held[j][...].astype(dtype)
            send(j).start()

        each(lambda j: bring(j).start())
        each(forward)
        each(lambda j: send(j).wait())

    anywhere = pl.BlockSpec(memory_space=pl.ANY)
    size = int(np.prod(shape))
    buffers = [pltpu.VMEM(piece.shape, kept) for piece in pieces]
    if wider:
        buffers += [pltpu.VMEM(piece.shape, dtype) for piece in pieces]
    return pl.pallas_call(
        kernel,
        out_shape=jax.ShapeDtypeStruct(shape, dtype),
        grid_spec=pltpu.PrefetchScalarGridSpec(
            num_scalar_prefetch=1,
            grid=(1,),
            in_specs=[anywhere] * given,
            out_specs=anywhere,
            scratch_shapes=buffers + [pltpu.SemaphoreType.DMA((2, count))],
        ),
        cost_estimate=pl.CostEstimate(flops=0, transcendentals=0, bytes_accessed=4 * size),
        input_output_aliases={} if base is None else {given: 0},
        name="place",
    )(
        jnp.stack([jnp.asarray(o, jnp.int32) for at in offsets for o in at]),
        *pieces,
        *([] if base is None else [base]),
    )


def swap(value, mask):
    count = lax.axis_size("seq")
    return lax.ppermute(value, "seq", [(i, i ^ mask) for i in range(count)])


def gather_start(part):
    half = part.shape[0] // 2
    if lax.axis_size("seq") != 8 or half % 128:
        return [lax.all_gather(part, "seq", axis=0, tiled=True)]
    top, low = part[:half], part[half:]
    return [top, low, swap(top, 2), swap(low, 4), swap(top, 4), swap(low, 2)]


def gather_next(held):
    return held if len(held) == 1 else held + [swap(held[2], 4), swap(held[3], 2)]


def gather_last(held):
    if len(held) == 1:
        return held[0]
    count, mine = lax.axis_size("seq"), lax.axis_index("seq")
    half, width = held[0].shape
    places = [(0, 0), (0, 1), (2, 0), (4, 1), (4, 0), (2, 1), (6, 0), (6, 1)]
    pieces = dict(zip(places, held))
    pieces |= {(mask | 1, side): swap(piece, 1) for (mask, side), piece in pieces.items()}
    offsets = [((mine ^ mask) * 2 + side) * half for mask, side in pieces]
    return place(list(pieces.values()), offsets, (2 * half * count, width))


def gather_columns(block, axis):
    count, mine = lax.axis_size(axis), lax.axis_index(axis)
    width = block.shape[1]
    pieces = [block] + [turn(block, axis, step) for step in range(1, count)]
    offsets = [((mine - step) % count) * width for step in range(count)]
    return place(pieces, offsets, (block.shape[0], width * count), put_columns)


def rows_sent(value):
    count, mine = lax.axis_size("head"), lax.axis_index("head")
    rows, width = value.shape[0] // count, value.shape[1]

    def block(k):
        return lax.dynamic_slice_in_dim(value, ((mine + k) % count) * rows, rows, 0)

    pieces = [block(0)] + [turn(block(k), "head", k) for k in range(1, count)]
    return pieces, [((mine - k) % count) * width for k in range(count)]


def columns_sent(value):
    count, mine = lax.axis_size("head"), lax.axis_index("head")
    rows, width = value.shape[0], value.shape[1] // count

    def block(k):
        return lax.dynamic_slice_in_dim(value, ((mine + k) % count) * width, width, 1)

    pieces = [block(0)] + [turn(block(k), "head", k) for k in range(1, count)]
    return pieces, [((mine - k) % count) * rows for k in range(count)]


def along(value, step):
    count = lax.axis_size("head")
    pairs = [(i, i + step) for i in range(count) if 0 <= i + step < count]
    return lax.ppermute(value, "head", pairs)


def sum_parts(parts, far, low=None, high=None):
    count = lax.axis_size("head")
    up, down = parts[-far % count], parts[far]
    if low is not None:
        up = (up.astype(f32) + low.astype(f32)).astype(bf16)
        down = (down.astype(f32) + high.astype(f32)).astype(bf16)
    return up, down


def sum_send(up, down, far):
    count = lax.axis_size("head")
    return (
        lax.ppermute(up, "head", [(i, i + 1) for i in range(count - far)]),
        lax.ppermute(down, "head", [(i, i - 1) for i in range(far, count)]),
    )


def sum_step(parts, far, low=None, high=None):
    return sum_send(*sum_parts(parts, far, low, high), far)


def join_line(own, from_low, from_high, dtype=None):
    count, mine = lax.axis_size("head"), lax.axis_index("head")
    rows = own.shape[0]
    pieces, offsets = [own], [mine * rows]
    for far, (low, high) in enumerate(zip(from_low, from_high), 1):
        pieces += [low, high]
        offsets.append((mine - far) * rows)
        offsets.append(jnp.where(mine + far < count, (mine + far) * rows, -1))
    return place(pieces, offsets, (rows * count, own.shape[1]), dtype=dtype)


def neighbour_sums(tail, all_ids, step, reach):
    count, mine = lax.axis_size("seq"), lax.axis_index("seq")
    theirs, own = (all_ids[:, -1], all_ids[:, 0]) if step > 0 else (all_ids[:, 0], all_ids[:, -1])
    own = lax.dynamic_index_in_dim(own, mine, 0, keepdims=False)
    total = jnp.zeros(tail.shape, f32)
    for k in range(1, min(reach, count - 1) + 1):
        pairs = [(i, i + k * step) for i in range(count) if 0 <= i + k * step < count]
        got = lax.ppermute(tail, "seq", pairs)
        at = mine - k * step
        other = lax.dynamic_index_in_dim(theirs, jnp.clip(at, 0, count - 1), 0, keepdims=False)
        use = (at >= 0) & (at < count) & (other == own)
        total = total + jnp.where(use, got.astype(f32), 0.0)
    return total


def body(tokens, seq_ids, gain_attn, w_qk, w_v, w_out, gain_mlp, w_gate, w_up, w_down, cotangent):
    zc, z = lax.axis_size("head"), lax.axis_index("head")
    token_count, width = tokens.shape
    blocks = seq_ids.shape[0]
    block_len = token_count // blocks
    heads_here = w_v.shape[1] // HV
    qk_cols = w_qk.shape[1]
    share = token_count // zc
    reach = -(-(MAX_BLOCKS - 1) // blocks)

    small = jnp.pad(seq_ids.astype(bf16), (0, gain_attn.shape[0] - blocks))
    small = jnp.stack([gain_attn, gain_mlp, small])
    small = lax.all_gather(small, "seq", axis=1, tiled=True).astype(f32)
    gain_one, gain_two = small[0], small[1]
    all_ids = small[2].reshape(lax.axis_size("seq"), gain_attn.shape[0])[:, :blocks]
    qkv_part = jnp.concatenate([w_qk, w_v], axis=1)
    full_qkv = lax.all_gather(qkv_part, "seq", axis=0, tiled=True)
    full_both = lax.all_gather(
        jnp.concatenate([w_gate, w_up], axis=1), "seq", axis=0, tiled=True
    )
    out_rows = gather_columns(w_out, "head")

    inputs = tokens.astype(f32)
    scale_one = lax.rsqrt(jnp.mean(inputs * inputs, axis=-1, keepdims=True) + epsilon)
    normed = (inputs * scale_one * gain_one).astype(bf16)
    qkv_blocks = {k: turn(qkv_part, "head", k) for k in range(1, zc)}
    full_qkv, normed, out_rows, qkv_blocks[1], qkv_blocks[zc - 1] = tie(
        full_qkv, normed, out_rows, qkv_blocks[1], qkv_blocks[zc - 1]
    )
    full_out = lax.all_gather(out_rows, "seq", axis=0, tiled=True)
    proj = dot(normed, full_qkv).astype(bf16)
    tables = selection_tables(heads_here)
    tail_call, inner_call, forward_call, grad_tail_call, local_call, backward_call = (
        attention_calls(blocks, block_len, heads_here, tables)
    )
    tail, qkv_blocks[2] = tie(tail_call(seq_ids, proj), qkv_blocks[2])
    qkv_rows = place(
        [qkv_part] + [qkv_blocks[k] for k in range(1, zc)],
        [((z - k) % zc) * qkv_part.shape[1] for k in range(zc)],
        (qkv_part.shape[0], qkv_part.shape[1] * zc),
        put_columns,
    )
    incoming = neighbour_sums(tail, all_ids, 1, reach)
    inner = inner_call(seq_ids, tie(proj, tail)[0])
    incoming, *inner = tie(incoming, *inner)
    head_rows, numerator, denominator, states = forward_call(seq_ids, proj, *inner, incoming)
    down_held = gather_start(tie(w_down, head_rows)[0])
    all_qkv = lax.all_gather(qkv_rows, "seq", axis=0, tiled=True)

    heads_own = place(*rows_sent(head_rows), (share, heads_here * HV * zc), put_columns)
    own_in = lax.dynamic_slice_in_dim(tokens, z * share, share, 0).astype(f32)
    residual = own_in + dot(heads_own, full_out)
    scale_two = lax.rsqrt(jnp.mean(residual * residual, axis=-1, keepdims=True) + epsilon)
    normed_own = (residual * scale_two * gain_two).astype(bf16)

    normed_own, *down_held = tie(normed_own, *down_held)
    full_down = gather_last(gather_next(down_held))
    order = [0] + sorted(range(1, zc), key=lambda k: min(k, zc - k))
    hidden = w_gate.shape[1]
    normed_parts, cot_parts, act_parts, both_parts = [], [], [], []
    backs = {}
    got_first, first_own, later = tie(turn(normed_own, "head", order[1]), normed_own, normed_own)
    arrivals = {0: first_own, order[1]: got_first}
    for k in order[2:]:
        arrivals[k] = turn(later, "head", k)
    for k in order:
        normed_two = arrivals[k]
        owner = (z - k) % zc
        cot = lax.dynamic_slice_in_dim(cotangent, owner * share, share, 0)
        pre = dot(normed_two, full_both)
        gate_pre, up_pre = pre[:, :hidden], pre[:, hidden:]
        gate_sigmoid = jax.nn.sigmoid(gate_pre)
        active = (gate_pre * gate_sigmoid * up_pre).astype(bf16)
        grad_active = dot(cot, full_down)
        grad_gate = grad_active * up_pre * gate_sigmoid * (1.0 + gate_pre * (1.0 - gate_sigmoid))
        grad_upper = grad_active * gate_pre * gate_sigmoid
        grad_both = jnp.concatenate([grad_gate.astype(bf16), grad_upper.astype(bf16)], axis=1)
        backs[k] = cols_dot(grad_both, full_both)
        if k:
            backs[k] = backs[k].astype(bf16)
        if k != order[-1]:
            following = order[order.index(k) + 1]
            arrivals[following], backs[k] = tie(arrivals[following], backs[k])
        normed_parts.append(normed_two)
        cot_parts.append(cot)
        act_parts.append(active)
        both_parts.append(grad_both)
    low = high = None
    for far in range(zc - 1, 2, -1):
        low, high = sum_step(backs, far, low, high)
    up, down = sum_parts(backs, 2, low, high)
    up, down, normed_parts[0], both_parts[0], cot_parts[0], *act_parts = tie(
        up, down, normed_parts[0], both_parts[0], cot_parts[0], *act_parts
    )
    low, high = sum_send(up, down, 2)
    both_grad = rows_dot(jnp.concatenate(normed_parts), jnp.concatenate(both_parts)).astype(bf16)
    low, high, act_parts[0], both_grad = tie(low, high, act_parts[0], both_grad)
    both_shard = lax.psum_scatter(both_grad, "seq", scatter_dimension=0, tiled=True)
    up, down = sum_parts(backs, 1, low, high)
    up, down, *act_parts = tie(up, down, *act_parts)
    low, high = sum_send(up, down, 1)
    outs = {k: cols_dot(active, full_down) for k, active in zip(order, act_parts)}
    outs = {k: out.astype(bf16) if k else out for k, out in outs.items()}
    down_grad = rows_dot(jnp.concatenate(cot_parts), jnp.concatenate(act_parts)).astype(bf16)
    tied = tie(backs[0], low, high, all_qkv, down_grad, *[outs[k] for k in order])
    grad_normed = tied[0] + tied[1].astype(f32) + tied[2].astype(f32)
    all_qkv, down_grad = tied[3:5]
    down_shard = lax.psum_scatter(down_grad, "seq", scatter_dimension=0, tiled=True)
    outs = dict(zip(order, tied[5:]))

    cot_own = lax.dynamic_slice_in_dim(cotangent, z * share, share, 0).astype(f32)
    weighted = grad_normed * gain_two
    grad_mid = (
        cot_own
        + scale_two * weighted
        - residual * scale_two**3 * jnp.mean(weighted * residual, axis=-1, keepdims=True)
    )
    gain_two_term = jnp.sum(grad_normed * residual * scale_two, axis=0)
    grad_branch = grad_mid.astype(bf16)
    grad_heads = cols_dot(grad_branch, full_out).astype(bf16)
    pieces, offsets = columns_sent(grad_heads)
    pieces[1], heads_own = tie(pieces[1], heads_own)
    out_grad = rows_dot(heads_own, grad_branch).astype(bf16)
    pieces[2], out_grad = tie(pieces[2], out_grad)
    grad_heads = place(pieces, offsets, (token_count, grad_heads.shape[1] // zc))
    grad_heads, low, high = tie(grad_heads, *sum_step(outs, zc - 1))
    grad_heads, up, down = tie(grad_heads, *sum_parts(outs, 2, low, high))
    low, high = sum_send(up, down, 2)
    dnum, head_part = grad_tail_call(seq_ids, proj, grad_heads, numerator, denominator)
    outgoing = neighbour_sums(head_part, all_ids, -1, reach)
    low, high = sum_step(outs, 1, low, high)
    partial = local_call(seq_ids, proj, dnum, states)
    outgoing, low, high, partial = tie(outgoing, low, high, partial)
    result_own = (residual + outs[0] + low.astype(f32) + high.astype(f32)).astype(bf16)
    res_low, res_high = [along(result_own, 1)], [along(result_own, -1)]
    grad_qkv = backward_call(seq_ids, proj, dnum, partial, outgoing)
    grad_qkv, res_low[0], res_high[0], both_shard, out_grad = tie(
        grad_qkv, res_low[0], res_high[0], both_shard, out_grad
    )
    out_part = lax.psum_scatter(out_grad, "seq", scatter_dimension=0, tiled=True)
    qkv_grad = rows_dot(normed, grad_qkv)

    own_pieces, own_columns = rows_sent(grad_qkv)
    own_pieces[1], res_low[0], res_high[0] = tie(own_pieces[1], res_low[0], res_high[0])
    res_low.append(along(res_low[0], 1))
    res_high.append(along(res_high[0], -1))
    own_qkv = place(own_pieces, own_columns, (share, grad_qkv.shape[1] * zc), put_columns)
    grad_norm_one = cols_dot(own_qkv, all_qkv)
    grad_norm_one, res_low[1], res_high[1], down_shard = tie(
        grad_norm_one, res_low[1], res_high[1], down_shard
    )
    own_scale = lax.dynamic_slice_in_dim(scale_one, z * share, share, 0)
    weighted_one = grad_norm_one * gain_one
    grad_own = (
        grad_mid
        + own_scale * weighted_one
        - own_in * own_scale**3 * jnp.mean(weighted_one * own_in, axis=-1, keepdims=True)
    )
    gain_one_term = jnp.sum(grad_norm_one * own_in * own_scale, axis=0)
    tok_own, gain_one_term = tie(grad_own.astype(bf16), gain_one_term)
    out_cols = w_out.shape[1]
    tok_low, tok_high = [along(tok_own, 1)], [along(tok_own, -1)]
    for far in range(3, zc):
        res_low.append(along(res_low[-1], 1))
        res_high.append(along(res_high[-1], -1))
    tok_low[0], tok_high[0], res_low[-1], res_high[-1], out_part = tie(
        tok_low[0], tok_high[0], res_low[-1], res_high[-1], out_part
    )
    out_shard = lax.dynamic_slice_in_dim(out_part, z * out_cols, out_cols, 1).astype(f32)
    for k in range(1, zc):
        block = lax.dynamic_slice_in_dim(out_part, ((z + k) % zc) * out_cols, out_cols, 1)
        out_shard = out_shard + turn(block, "head", k).astype(f32)
    for far in range(2, zc):
        tok_low.append(along(tok_low[-1], 1))
        tok_high.append(along(tok_high[-1], -1))
    near_low, near_high = tok_low[:-1], tok_high[:-1]
    near_low[-1], out_shard = tie(near_low[-1], out_shard)

    def scatter(grad):
        return lax.psum_scatter(grad, "seq", scatter_dimension=0, tiled=True)

    down_shard = down_shard.astype(f32)
    both_shard = both_shard.astype(f32)
    gain_terms = jnp.pad(jnp.stack([gain_one_term, gain_two_term], axis=1), ((0, 0), (0, 126)))
    last = scatter(jnp.concatenate([qkv_grad, gain_terms], axis=1).astype(bf16)).astype(f32)
    gain_own = last[:, -128:-126].T[None]
    gain_parts = [gain_own] + [turn(gain_own, "head", k) for k in range(1, zc)]
    tok_low[-1], tok_high[-1], *gain_parts = tie(tok_low[-1], tok_high[-1], *gain_parts)
    gain_all = jnp.zeros((zc,) + gain_own.shape[1:], f32)
    for k, part in enumerate(gain_parts):
        gain_all = lax.dynamic_update_slice_in_dim(gain_all, part, (z - k) % zc, 0)
    gain_sums = jnp.sum(gain_all, axis=0)
    grad_tokens = join_line(tok_own, near_low, near_high, f32)
    grad_tokens = place(
        [tok_low[-1], tok_high[-1]],
        [(z - zc + 1) * share, jnp.where(z == 0, (zc - 1) * share, -1)],
        grad_tokens.shape,
        dtype=f32,
        base=grad_tokens,
    )
    result = join_line(result_own, res_low, res_high)
    return (
        result,
        grad_tokens,
        last[:, :qk_cols],
        last[:, qk_cols:-128],
        out_shard,
        both_shard[:, :hidden],
        both_shard[:, hidden:],
        down_shard,
        gain_sums[0],
        gain_sums[1],
    )


def solution(mesh):
    return jax.shard_map(
        body,
        mesh=mesh,
        in_specs=(
            P("seq", None),
            P("seq"),
            P("seq"),
            P("seq", "head"),
            P("seq", "head"),
            P("seq", "head"),
            P("seq"),
            P("seq", "head"),
            P("seq", "head"),
            P("seq", "head"),
            P("seq", None),
        ),
        out_specs=(
            P("seq", None),
            P("seq", None),
            P("seq", "head"),
            P("seq", "head"),
            P("seq", "head"),
            P("seq", "head"),
            P("seq", "head"),
            P("seq", "head"),
            P("seq"),
            P("seq"),
        ),
        check_vma=False,
    )
```

```python
import math

import jax
import jax.numpy as jnp
import numpy as np
from jax import lax
from jax.experimental import pallas as pl
from jax.experimental.pallas import tpu as pltpu
from jax.sharding import PartitionSpec as P

FEAT = 16
HV = 128
MAX_BLOCKS = 16


epsilon = 1e-06
bf16 = jnp.bfloat16
f32 = jnp.float32


FS = 160
FL = 256


def selection_tables(heads):
    pairs = [(a, b) for a in range(FEAT) for b in range(a, FEAT)]
    first = np.zeros((FEAT, FL), np.float32)
    second = np.zeros((FEAT, FL), np.float32)
    one_a, one_b = np.zeros(FL, np.float32), np.zeros(FL, np.float32)
    scale, twice = np.zeros(FL, np.float32), np.ones(FL, np.float32)
    one_a[0] = one_b[0] = scale[0] = 1.0
    for a in range(FEAT):
        first[a, 1 + a] = 1.0
        one_b[1 + a] = 1.0
        scale[1 + a] = 1.0 / FEAT**0.25
    for at, (a, b) in enumerate(pairs):
        at += 1 + FEAT
        first[a, at] = second[b, at] = 1.0
        scale[at] = 1.0 / (math.sqrt(2.0) * FEAT**0.5)
        twice[at] = 1.0 if a == b else 2.0
    cols = heads * 2 * FEAT
    wide = np.zeros((4, heads, cols, FL), np.float32)
    for h in range(heads):
        q0, k0 = h * 2 * FEAT, h * 2 * FEAT + FEAT
        wide[0, h, q0:k0], wide[1, h, q0:k0] = first, second
        wide[2, h, k0 : k0 + FEAT], wide[3, h, k0 : k0 + FEAT] = first, second
    tall = np.swapaxes(wide, 2, 3)[:, :, :FS].reshape(4, heads * FS, cols)
    rows = np.zeros((8, FL), np.float32)
    rows[0], rows[1], rows[2], rows[3] = one_a, one_b, scale, twice
    columns = np.repeat(rows[:3, :FS, None], cols, axis=2)
    return (
        jnp.asarray(wide, bf16),
        jnp.asarray(np.ascontiguousarray(tall), bf16),
        jnp.asarray(rows, f32),
        jnp.asarray(columns, f32),
    )


def mm(left, right):
    return lax.dot_general(left, right, (((1,), (0,)), ((), ())), preferred_element_type=f32)


def mm_nt(left, right):
    return lax.dot_general(left, right, (((1,), (1,)), ((), ())), preferred_element_type=f32)


def lane_marks(rows, lanes):
    lane = lax.broadcasted_iota(jnp.int32, (rows, HV), 1)
    return (lane < lanes).astype(bf16)


def features_wide(x, first, second, rows):
    one = mm(x, first) + rows[0:1]
    two = mm(x, second) + rows[1:2]
    return one, two, (one * two) * rows[2:3]


def features_tall(x, tall, first, columns):
    one, two = mm_nt(tall[first], x), mm_nt(tall[first + 1], x)
    parts = [slice(at, at + FS) for at in range(0, one.shape[0], FS)]
    return [
        ((one[at] + columns[0]) * (two[at] + columns[1]) * columns[2]).astype(bf16) for at in parts
    ]


def neighbours(x):
    lane = lax.broadcasted_iota(jnp.int32, x.shape, 1)
    wide = x.astype(f32)
    size = x.shape[1]
    from_k, from_q = pltpu.roll(wide, size - FEAT, 1), pltpu.roll(wide, FEAT, 1)
    pairs = []
    for at in range(0, size, 2 * FEAT):
        in_q = (lane >= at) & (lane < at + FEAT)
        in_k = (lane >= at + FEAT) & (lane < at + 2 * FEAT)
        pairs.append(
            (jnp.where(in_q, from_k, 0.0).astype(bf16), jnp.where(in_k, from_q, 0.0).astype(bf16))
        )
    return pairs


def split_state(state):
    left, right = state[:, :HV], state[:, HV:]
    lane = lax.broadcasted_iota(jnp.int32, right.shape, 1)
    high = right.astype(bf16)
    low = (right - high.astype(f32)).astype(bf16)
    return left.astype(bf16), jnp.where(lane == 2, low, high)


def join_state(state, both):
    right = state[:, HV:]
    lane = lax.broadcasted_iota(jnp.int32, right.shape, 1)
    whole = right[:, 0:1] + right[:, 2:3]
    if both:
        new = jnp.where(lane < 3, whole, 0.0)
    else:
        new = jnp.where(lane == 1, right, jnp.where(lane < 3, whole, 0.0))
    return jnp.concatenate([state[:, :HV], new], axis=1)


def tail_kernel(ids, proj, tall, columns, out, acc):
    at, last = pl.program_id(0), pl.num_programs(0) - 1
    heads = out.shape[0]
    qk = heads * 2 * FEAT

    @pl.when(at == 0)
    def _():
        acc[...] = jnp.zeros_like(acc)

    @pl.when(ids[at] == ids[last])
    def _():
        x = proj[:, :qk]
        marks = lane_marks(x.shape[0], 3)
        tall_k = features_tall(x, tall, 2, columns)
        for h in range(heads):
            v = proj[:, qk + h * HV : qk + (h + 1) * HV]
            acc[h] += mm(tall_k[h], jnp.concatenate([v, marks], axis=1))

    @pl.when(at == last)
    def _():
        for h in range(heads):
            left, right = split_state(acc[h])
            out[h, :, :HV] = left
            out[h, :, HV:] = right


def inner_kernel(ids, proj, num_out, den_out):
    heads = num_out.shape[1] // HV
    qk = heads * 2 * FEAT
    x = proj[:, :qk]
    pairs = neighbours(x)
    size = x.shape[0]
    row = lax.broadcasted_iota(jnp.int32, (size, size), 0)
    col = lax.broadcasted_iota(jnp.int32, (size, size), 1)
    lane = lax.broadcasted_iota(jnp.int32, (size, HV), 1)
    dens = jnp.zeros((size, HV), f32)
    for h in range(heads):
        v = proj[:, qk + h * HV : qk + (h + 1) * HV]
        s = mm_nt(x, pairs[h][0]) * FEAT**-0.5
        a = jnp.where(row >= col, 1.0 + s + 0.5 * s * s, 0.0)
        num_out[:, h * HV : (h + 1) * HV] = mm(a.astype(bf16), v)
        dens = jnp.where(lane == h, jnp.sum(a, axis=1, keepdims=True), dens)
    den_out[...] = dens


def forward_kernel(
    ids, proj, num_in, den_in, incoming, wide, tall, rows, columns, heads_out, num_out, den_out, state_out, acc
):
    at = pl.program_id(0)
    heads = acc.shape[0]
    qk = heads * 2 * FEAT

    @pl.when(at == 0)
    def _():
        for h in range(heads):
            acc[h] = join_state(incoming[h], True)

    @pl.when((at > 0) & (ids[at] != ids[jnp.maximum(at - 1, 0)]))
    def _():
        acc[...] = jnp.zeros_like(acc)

    x = proj[:, :qk]
    size = x.shape[0]
    marks = lane_marks(size, 3)
    lane = lax.broadcasted_iota(jnp.int32, (size, HV), 1)
    tall_k = features_tall(x, tall, 2, columns)
    dens = jnp.zeros((size, HV), f32)
    for h in range(heads):
        v = proj[:, qk + h * HV : qk + (h + 1) * HV]
        left, right = split_state(acc[h])
        state = jnp.concatenate(
            [jnp.concatenate([left, right], axis=1), jnp.zeros((FL - FS, 2 * HV), bf16)], axis=0
        )
        state_out[0, h] = state
        _, _, fq = features_wide(x, wide[0, h], wide[1, h], rows)
        fq = fq.astype(bf16) * rows[3:4].astype(bf16)
        ext = mm(fq, state)
        num = num_in[:, h * HV : (h + 1) * HV] + ext[:, :HV]
        den = den_in[:, h : h + 1] + ext[:, HV : HV + 1] + ext[:, HV + 2 : HV + 3]
        heads_out[:, h * HV : (h + 1) * HV] = (num * (1.0 / den)).astype(bf16)
        num_out[:, h * HV : (h + 1) * HV] = num
        dens = jnp.where(lane == h, den, dens)
        acc[h] += mm(tall_k[h], jnp.concatenate([v, marks], axis=1))
    den_out[...] = dens


def grad_tail_kernel(ids, proj, dheads, num, den, tall, columns, dnum_out, out, acc):
    at, last = pl.program_id(0), pl.num_programs(0) - 1
    heads = out.shape[0]
    qk = heads * 2 * FEAT

    @pl.when(at == 0)
    def _():
        acc[...] = jnp.zeros_like(acc)

    x = proj[:, :qk]
    size = x.shape[0]
    lane = lax.broadcasted_iota(jnp.int32, (size, HV), 1)
    for h in range(heads):
        d = den[:, h : h + 1]
        g = dheads[:, h * HV : (h + 1) * HV].astype(f32)
        inverse = 1.0 / d
        dnum = (g * inverse).astype(bf16)
        dden = -jnp.sum(g * num[:, h * HV : (h + 1) * HV], axis=1, keepdims=True) * (
            inverse * inverse
        )
        high = dden.astype(bf16)
        low = (dden - high.astype(f32)).astype(bf16)
        side = jnp.where(
            (lane == 0) | (lane == 2), high.astype(f32), jnp.where(lane == 1, low.astype(f32), 0.0)
        ).astype(bf16)
        dnum_out[:, h * 2 * HV : h * 2 * HV + HV] = dnum
        dnum_out[:, h * 2 * HV + HV : (h + 1) * 2 * HV] = side

    @pl.when(ids[at] == ids[0])
    def _():
        tall_q = features_tall(x, tall, 0, columns)
        for h in range(heads):
            acc[h] += mm(tall_q[h], dnum_out[:, h * 2 * HV : (h + 1) * 2 * HV])

    @pl.when(at == last)
    def _():
        for h in range(heads):
            left, right = split_state(acc[h])
            out[h, :, :HV] = left
            out[h, :, HV:] = right


def local_kernel(ids, proj, dnum_in, state_in, wide, rows, out):
    heads = wide.shape[1]
    qk = heads * 2 * FEAT
    x = proj[:, :qk]
    pairs = neighbours(x)
    size = x.shape[0]
    row = lax.broadcasted_iota(jnp.int32, (size, size), 0)
    col = lax.broadcasted_iota(jnp.int32, (size, size), 1)
    marks = lane_marks(size, 2)
    weight = rows[2:3] * rows[3:4]
    total = jnp.zeros((size, qk), f32)
    for h in range(heads):
        v = proj[:, qk + h * HV : qk + (h + 1) * HV]
        dn = dnum_in[:, h * 2 * HV : (h + 1) * 2 * HV]
        q1, q2, _ = features_wide(x, wide[0, h], wide[1, h], rows)
        kq, qk_moved = pairs[h]
        s = mm_nt(x, kq) * FEAT**-0.5
        st = mm_nt(kq, x) * FEAT**-0.5
        at_low = jnp.where(row <= col, 1.0 + st + 0.5 * st * st, 0.0).astype(bf16)
        v2 = jnp.concatenate([v, marks], axis=1)
        da = mm_nt(dn, v2)
        dat = mm_nt(v2, dn)
        draw = jnp.where(row >= col, da * (1.0 + s) * FEAT**-0.5, 0.0).astype(bf16)
        drawt = jnp.where(row <= col, dat * (1.0 + st) * FEAT**-0.5, 0.0).astype(bf16)
        wq = mm_nt(dn, state_in[0, h]) * weight
        total += (
            mm(draw, kq)
            + mm(drawt, qk_moved)
            + mm_nt((wq * q2).astype(bf16), wide[0, h])
            + mm_nt((wq * q1).astype(bf16), wide[1, h])
        )
        out[:, qk + h * HV : qk + (h + 1) * HV] = mm(at_low, dn[:, :HV])
    out[:, :qk] = total


def backward_kernel(ids, proj, dnum_in, local, incoming, wide, tall, rows, columns, out, acc):
    step, last = pl.program_id(0), pl.num_programs(0) - 1
    at = last - step
    heads = acc.shape[0]
    qk = heads * 2 * FEAT

    @pl.when(step == 0)
    def _():
        for h in range(heads):
            acc[h] = join_state(incoming[h], False)

    @pl.when((step > 0) & (ids[at] != ids[jnp.minimum(at + 1, last)]))
    def _():
        acc[...] = jnp.zeros_like(acc)

    x = proj[:, :qk]
    marks = lane_marks(x.shape[0], 3)
    weight = rows[2:3] * rows[3:4]
    twice = rows[3:4].astype(bf16)
    tall_q = features_tall(x, tall, 0, columns)
    total = local[:, :qk]
    for h in range(heads):
        v = proj[:, qk + h * HV : qk + (h + 1) * HV]
        left, right = split_state(acc[h])
        dstate = jnp.concatenate(
            [jnp.concatenate([left, right], axis=1), jnp.zeros((FL - FS, 2 * HV), bf16)], axis=0
        )
        k1, k2, fk = features_wide(x, wide[2, h], wide[3, h], rows)
        fk = fk.astype(bf16) * twice
        wk = mm_nt(jnp.concatenate([v, marks], axis=1), dstate) * weight
        total += mm_nt((wk * k2).astype(bf16), wide[2, h]) + mm_nt(
            (wk * k1).astype(bf16), wide[3, h]
        )
        dv = local[:, qk + h * HV : qk + (h + 1) * HV] + mm(fk, dstate[:, :HV])
        out[:, qk + h * HV : qk + (h + 1) * HV] = dv.astype(bf16)
        acc[h] += mm(tall_q[h], dnum_in[:, h * 2 * HV : (h + 1) * 2 * HV])
    out[:, :qk] = total.astype(bf16)


def whole_spec(array):
    zeros = (0,) * array.ndim
    return pl.BlockSpec(array.shape, lambda i, ids: zeros)


def attention_calls(blocks, block_len, heads, tables):
    wide, tall, rows, columns = tables
    qk = heads * 2 * FEAT
    tokens = blocks * block_len
    state = (heads, FS, 2 * HV)

    def at_block(cols, reverse=False):
        if reverse:
            return pl.BlockSpec((block_len, cols), lambda i, ids: (blocks - 1 - i, 0))
        return pl.BlockSpec((block_len, cols), lambda i, ids: (i, 0))

    def states_spec(reverse=False):
        if reverse:
            return pl.BlockSpec((1, heads, FL, 2 * HV), lambda i, ids: (blocks - 1 - i, 0, 0, 0))
        return pl.BlockSpec((1, heads, FL, 2 * HV), lambda i, ids: (i, 0, 0, 0))

    def call(kernel, name, in_specs, out_specs, out_shape, flops, moved, carried=True):
        return pl.pallas_call(
            kernel,
            out_shape=out_shape,
            grid_spec=pltpu.PrefetchScalarGridSpec(
                num_scalar_prefetch=1,
                grid=(blocks,),
                in_specs=in_specs,
                out_specs=out_specs,
                scratch_shapes=[pltpu.VMEM(state, f32)] if carried else [],
            ),
            compiler_params=pltpu.CompilerParams(dimension_semantics=("arbitrary",)),
            cost_estimate=pl.CostEstimate(flops=flops, transcendentals=0, bytes_accessed=moved),
            name=name,
        )

    full_state = pl.BlockSpec(state, lambda i, ids: (0, 0, 0))
    proj_cols = qk + heads * HV

    def tail(ids, proj):
        return call(
            tail_kernel,
            "state_tail",
            [at_block(proj_cols), whole_spec(tall), whole_spec(columns)],
            full_state,
            jax.ShapeDtypeStruct(state, bf16),
            int(4e9),
            int(4e6),
        )(ids, proj, tall, columns)

    def inner(ids, proj):
        return call(
            inner_kernel,
            "attention_inner",
            [at_block(proj_cols)],
            [at_block(heads * HV), at_block(HV)],
            [
                jax.ShapeDtypeStruct((tokens, heads * HV), f32),
                jax.ShapeDtypeStruct((tokens, HV), f32),
            ],
            int(4e9),
            int(4e6),
            False,
        )(ids, proj)

    def forward(ids, proj, num, den, incoming):
        return call(
            forward_kernel,
            "attention_forward",
            [at_block(proj_cols), at_block(heads * HV), at_block(HV), full_state]
            + [whole_spec(t) for t in (wide, tall, rows, columns)],
            [at_block(heads * HV), at_block(heads * HV), at_block(HV), states_spec()],
            [
                jax.ShapeDtypeStruct((tokens, heads * HV), bf16),
                jax.ShapeDtypeStruct((tokens, heads * HV), f32),
                jax.ShapeDtypeStruct((tokens, HV), f32),
                jax.ShapeDtypeStruct((blocks, heads, FL, 2 * HV), bf16),
            ],
            int(6e9),
            int(2e7),
        )(ids, proj, num, den, incoming, wide, tall, rows, columns)

    def grad_tail(ids, proj, dheads, num, den):
        return call(
            grad_tail_kernel,
            "state_grad_tail",
            [at_block(proj_cols), at_block(heads * HV), at_block(heads * HV), at_block(HV)]
            + [whole_spec(tall), whole_spec(columns)],
            [at_block(heads * 2 * HV), full_state],
            [
                jax.ShapeDtypeStruct((tokens, heads * 2 * HV), bf16),
                jax.ShapeDtypeStruct(state, bf16),
            ],
            int(4e9),
            int(1e7),
        )(ids, proj, dheads, num, den, tall, columns)

    def local(ids, proj, dnum, states):
        return call(
            local_kernel,
            "attention_backward_local",
            [at_block(proj_cols), at_block(heads * 2 * HV), states_spec()]
            + [whole_spec(t) for t in (wide, rows)],
            at_block(proj_cols),
            jax.ShapeDtypeStruct((tokens, proj_cols), f32),
            int(1.3e10),
            int(2e7),
            False,
        )(ids, proj, dnum, states, wide, rows)

    def backward(ids, proj, dnum, partial, incoming):
        return call(
            backward_kernel,
            "attention_backward",
            [at_block(proj_cols, True), at_block(heads * 2 * HV, True)]
            + [at_block(proj_cols, True), full_state]
            + [whole_spec(t) for t in (wide, tall, rows, columns)],
            at_block(proj_cols, True),
            jax.ShapeDtypeStruct((tokens, proj_cols), bf16),
            int(1e10),
            int(2e7),
        )(ids, proj, dnum, partial, incoming, wide, tall, rows, columns)

    return tail, inner, forward, grad_tail, local, backward


def rows_dot(left, right):
    return lax.dot_general(left, right, (((0,), (0,)), ((), ())), preferred_element_type=f32)


def cols_dot(left, right):
    return lax.dot_general(left, right, (((1,), (1,)), ((), ())), preferred_element_type=f32)


def dot(left, right):
    return jnp.dot(left, right, preferred_element_type=f32)


def turn(value, axis, step):
    count = lax.axis_size(axis)
    return lax.ppermute(value, axis, [(i, (i + step) % count) for i in range(count)])


def tie(*values):
    return lax.optimization_barrier(values)


def put_rows(out, piece, at):
    return out.at[pl.ds(pl.multiple_of(at[0], 128), piece[0])]


def put_columns(out, piece, at):
    return out.at[:, pl.ds(pl.multiple_of(at[0], 128), piece[1])]


def place(pieces, offsets, shape, put=put_rows, dtype=None, base=None):
    count = len(pieces)
    kept = pieces[0].dtype
    dtype = dtype or kept
    wider = dtype != kept
    offsets = [at if isinstance(at, tuple) else (at,) for at in offsets]
    per = len(offsets[0])

    given = count + (base is not None)

    def kernel(offs, *refs):
        out = refs[given]
        held = refs[given + 1 : given + count + 1]
        sent = refs[given + count + 1 : given + 2 * count + 1] if wider else held
        sems = refs[-1]

        def bring(j):
            return pltpu.make_async_copy(refs[j], held[j], sems.at[0, j])

        def send(j):
            at = [jnp.maximum(offs[j * per + i], 0) for i in range(per)]
            return pltpu.make_async_copy(sent[j], put(out, pieces[j].shape, at), sems.at[1, j])

        def each(action):
            for j in range(count):

                @pl.when(offs[j * per] >= 0)
                def _(j=j):
                    action(j)

        def forward(j):
            bring(j).wait()
            if wider:
                sent[j][...] = held[j][...].astype(dtype)
            send(j).start()

        each(lambda j: bring(j).start())
        each(forward)
        each(lambda j: send(j).wait())

    anywhere = pl.BlockSpec(memory_space=pl.ANY)
    size = int(np.prod(shape))
    buffers = [pltpu.VMEM(piece.shape, kept) for piece in pieces]
    if wider:
        buffers += [pltpu.VMEM(piece.shape, dtype) for piece in pieces]
    return pl.pallas_call(
        kernel,
        out_shape=jax.ShapeDtypeStruct(shape, dtype),
        grid_spec=pltpu.PrefetchScalarGridSpec(
            num_scalar_prefetch=1,
            grid=(1,),
            in_specs=[anywhere] * given,
            out_specs=anywhere,
            scratch_shapes=buffers + [pltpu.SemaphoreType.DMA((2, count))],
        ),
        cost_estimate=pl.CostEstimate(flops=0, transcendentals=0, bytes_accessed=4 * size),
        input_output_aliases={} if base is None else {given: 0},
        name="place",
    )(
        jnp.stack([jnp.asarray(o, jnp.int32) for at in offsets for o in at]),
        *pieces,
        *([] if base is None else [base]),
    )


def swap(value, mask):
    count = lax.axis_size("seq")
    return lax.ppermute(value, "seq", [(i, i ^ mask) for i in range(count)])


def gather_start(part):
    half = part.shape[0] // 2
    if lax.axis_size("seq") != 8 or half % 128:
        return [lax.all_gather(part, "seq", axis=0, tiled=True)]
    top, low = part[:half], part[half:]
    return [top, low, swap(top, 2), swap(low, 4), swap(top, 4), swap(low, 2)]


def gather_next(held):
    return held if len(held) == 1 else held + [swap(held[2], 4), swap(held[3], 2)]


def gather_last(held):
    if len(held) == 1:
        return held[0]
    count, mine = lax.axis_size("seq"), lax.axis_index("seq")
    half, width = held[0].shape
    places = [(0, 0), (0, 1), (2, 0), (4, 1), (4, 0), (2, 1), (6, 0), (6, 1)]
    pieces = dict(zip(places, held))
    pieces |= {(mask | 1, side): swap(piece, 1) for (mask, side), piece in pieces.items()}
    offsets = [((mine ^ mask) * 2 + side) * half for mask, side in pieces]
    return place(list(pieces.values()), offsets, (2 * half * count, width))


def gather_columns(block, axis):
    count, mine = lax.axis_size(axis), lax.axis_index(axis)
    width = block.shape[1]
    pieces = [block] + [turn(block, axis, step) for step in range(1, count)]
    offsets = [((mine - step) % count) * width for step in range(count)]
    return place(pieces, offsets, (block.shape[0], width * count), put_columns)


def rows_sent(value):
    count, mine = lax.axis_size("head"), lax.axis_index("head")
    rows, width = value.shape[0] // count, value.shape[1]

    def block(k):
        return lax.dynamic_slice_in_dim(value, ((mine + k) % count) * rows, rows, 0)

    pieces = [block(0)] + [turn(block(k), "head", k) for k in range(1, count)]
    return pieces, [((mine - k) % count) * width for k in range(count)]


def columns_sent(value):
    count, mine = lax.axis_size("head"), lax.axis_index("head")
    rows, width = value.shape[0], value.shape[1] // count

    def block(k):
        return lax.dynamic_slice_in_dim(value, ((mine + k) % count) * width, width, 1)

    pieces = [block(0)] + [turn(block(k), "head", k) for k in range(1, count)]
    return pieces, [((mine - k) % count) * rows for k in range(count)]


def along(value, step):
    count = lax.axis_size("head")
    pairs = [(i, i + step) for i in range(count) if 0 <= i + step < count]
    return lax.ppermute(value, "head", pairs)


def sum_parts(parts, far, low=None, high=None):
    count = lax.axis_size("head")
    up, down = parts[-far % count], parts[far]
    if low is not None:
        up = (up.astype(f32) + low.astype(f32)).astype(bf16)
        down = (down.astype(f32) + high.astype(f32)).astype(bf16)
    return up, down


def sum_send(up, down, far):
    count = lax.axis_size("head")
    return (
        lax.ppermute(up, "head", [(i, i + 1) for i in range(count - far)]),
        lax.ppermute(down, "head", [(i, i - 1) for i in range(far, count)]),
    )


def sum_step(parts, far, low=None, high=None):
    return sum_send(*sum_parts(parts, far, low, high), far)


def join_line(own, from_low, from_high, dtype=None):
    count, mine = lax.axis_size("head"), lax.axis_index("head")
    rows = own.shape[0]
    pieces, offsets = [own], [mine * rows]
    for far, (low, high) in enumerate(zip(from_low, from_high), 1):
        pieces += [low, high]
        offsets.append((mine - far) * rows)
        offsets.append(jnp.where(mine + far < count, (mine + far) * rows, -1))
    return place(pieces, offsets, (rows * count, own.shape[1]), dtype=dtype)


def neighbour_sums(tail, all_ids, step, reach):
    count, mine = lax.axis_size("seq"), lax.axis_index("seq")
    theirs, own = (all_ids[:, -1], all_ids[:, 0]) if step > 0 else (all_ids[:, 0], all_ids[:, -1])
    own = lax.dynamic_index_in_dim(own, mine, 0, keepdims=False)
    total = jnp.zeros(tail.shape, f32)
    for k in range(1, min(reach, count - 1) + 1):
        pairs = [(i, i + k * step) for i in range(count) if 0 <= i + k * step < count]
        got = lax.ppermute(tail, "seq", pairs)
        at = mine - k * step
        other = lax.dynamic_index_in_dim(theirs, jnp.clip(at, 0, count - 1), 0, keepdims=False)
        use = (at >= 0) & (at < count) & (other == own)
        total = total + jnp.where(use, got.astype(f32), 0.0)
    return total


def body(tokens, seq_ids, gain_attn, w_qk, w_v, w_out, gain_mlp, w_gate, w_up, w_down, cotangent):
    zc, z = lax.axis_size("head"), lax.axis_index("head")
    token_count, width = tokens.shape
    blocks = seq_ids.shape[0]
    block_len = token_count // blocks
    heads_here = w_v.shape[1] // HV
    qk_cols = w_qk.shape[1]
    share = token_count // zc
    reach = -(-(MAX_BLOCKS - 1) // blocks)

    small = jnp.pad(seq_ids.astype(bf16), (0, gain_attn.shape[0] - blocks))
    small = jnp.stack([gain_attn, gain_mlp, small])
    small = lax.all_gather(small, "seq", axis=1, tiled=True).astype(f32)
    gain_one, gain_two = small[0], small[1]
    all_ids = small[2].reshape(lax.axis_size("seq"), gain_attn.shape[0])[:, :blocks]
    qkv_part = jnp.concatenate([w_qk, w_v], axis=1)
    full_qkv = lax.all_gather(qkv_part, "seq", axis=0, tiled=True)
    full_both = lax.all_gather(
        jnp.concatenate([w_gate, w_up], axis=1), "seq", axis=0, tiled=True
    )
    out_rows = gather_columns(w_out, "head")

    inputs = tokens.astype(f32)
    scale_one = lax.rsqrt(jnp.mean(inputs * inputs, axis=-1, keepdims=True) + epsilon)
    normed = (inputs * scale_one * gain_one).astype(bf16)
    qkv_blocks = {k: turn(qkv_part, "head", k) for k in range(1, zc)}
    full_qkv, normed, out_rows, qkv_blocks[1], qkv_blocks[zc - 1] = tie(
        full_qkv, normed, out_rows, qkv_blocks[1], qkv_blocks[zc - 1]
    )
    full_out = lax.all_gather(out_rows, "seq", axis=0, tiled=True)
    proj = dot(normed, full_qkv).astype(bf16)
    tables = selection_tables(heads_here)
    tail_call, inner_call, forward_call, grad_tail_call, local_call, backward_call = (
        attention_calls(blocks, block_len, heads_here, tables)
    )
    tail, qkv_blocks[2] = tie(tail_call(seq_ids, proj), qkv_blocks[2])
    qkv_rows = place(
        [qkv_part] + [qkv_blocks[k] for k in range(1, zc)],
        [((z - k) % zc) * qkv_part.shape[1] for k in range(zc)],
        (qkv_part.shape[0], qkv_part.shape[1] * zc),
        put_columns,
    )
    incoming = neighbour_sums(tail, all_ids, 1, reach)
    inner = inner_call(seq_ids, tie(proj, tail)[0])
    incoming, *inner = tie(incoming, *inner)
    head_rows, numerator, denominator, states = forward_call(seq_ids, proj, *inner, incoming)
    down_held = gather_start(tie(w_down, head_rows)[0])
    all_qkv = lax.all_gather(qkv_rows, "seq", axis=0, tiled=True)

    heads_own = place(*rows_sent(head_rows), (share, heads_here * HV * zc), put_columns)
    own_in = lax.dynamic_slice_in_dim(tokens, z * share, share, 0).astype(f32)
    residual = own_in + dot(heads_own, full_out)
    scale_two = lax.rsqrt(jnp.mean(residual * residual, axis=-1, keepdims=True) + epsilon)
    normed_own = (residual * scale_two * gain_two).astype(bf16)

    normed_own, *down_held = tie(normed_own, *down_held)
    full_down = gather_last(gather_next(down_held))
    order = [0] + sorted(range(1, zc), key=lambda k: min(k, zc - k))
    hidden = w_gate.shape[1]
    normed_parts, cot_parts, act_parts, both_parts = [], [], [], []
    backs = {}
    got_first, first_own, later = tie(turn(normed_own, "head", order[1]), normed_own, normed_own)
    arrivals = {0: first_own, order[1]: got_first}
    for k in order[2:]:
        arrivals[k] = turn(later, "head", k)
    for k in order:
        normed_two = arrivals[k]
        owner = (z - k) % zc
        cot = lax.dynamic_slice_in_dim(cotangent, owner * share, share, 0)
        pre = dot(normed_two, full_both)
        gate_pre, up_pre = pre[:, :hidden], pre[:, hidden:]
        gate_sigmoid = jax.nn.sigmoid(gate_pre)
        active = (gate_pre * gate_sigmoid * up_pre).astype(bf16)
        grad_active = dot(cot, full_down)
        grad_gate = grad_active * up_pre * gate_sigmoid * (1.0 + gate_pre * (1.0 - gate_sigmoid))
        grad_upper = grad_active * gate_pre * gate_sigmoid
        grad_both = jnp.concatenate([grad_gate.astype(bf16), grad_upper.astype(bf16)], axis=1)
        backs[k] = cols_dot(grad_both, full_both)
        if k:
            backs[k] = backs[k].astype(bf16)
        if k != order[-1]:
            following = order[order.index(k) + 1]
            arrivals[following], backs[k] = tie(arrivals[following], backs[k])
        normed_parts.append(normed_two)
        cot_parts.append(cot)
        act_parts.append(active)
        both_parts.append(grad_both)
    low = high = None
    for far in range(zc - 1, 2, -1):
        low, high = sum_step(backs, far, low, high)
    up, down = sum_parts(backs, 2, low, high)
    up, down, normed_parts[0], both_parts[0], cot_parts[0], *act_parts = tie(
        up, down, normed_parts[0], both_parts[0], cot_parts[0], *act_parts
    )
    low, high = sum_send(up, down, 2)
    both_grad = rows_dot(jnp.concatenate(normed_parts), jnp.concatenate(both_parts)).astype(bf16)
    low, high, act_parts[0], both_grad = tie(low, high, act_parts[0], both_grad)
    both_shard = lax.psum_scatter(both_grad, "seq", scatter_dimension=0, tiled=True)
    up, down = sum_parts(backs, 1, low, high)
    up, down, *act_parts = tie(up, down, *act_parts)
    low, high = sum_send(up, down, 1)
    outs = {k: cols_dot(active, full_down) for k, active in zip(order, act_parts)}
    outs = {k: out.astype(bf16) if k else out for k, out in outs.items()}
    down_grad = rows_dot(jnp.concatenate(cot_parts), jnp.concatenate(act_parts)).astype(bf16)
    tied = tie(backs[0], low, high, all_qkv, down_grad, *[outs[k] for k in order])
    grad_normed = tied[0] + tied[1].astype(f32) + tied[2].astype(f32)
    all_qkv, down_grad = tied[3:5]
    down_shard = lax.psum_scatter(down_grad, "seq", scatter_dimension=0, tiled=True)
    outs = dict(zip(order, tied[5:]))

    cot_own = lax.dynamic_slice_in_dim(cotangent, z * share, share, 0).astype(f32)
    weighted = grad_normed * gain_two
    grad_mid = (
        cot_own
        + scale_two * weighted
        - residual * scale_two**3 * jnp.mean(weighted * residual, axis=-1, keepdims=True)
    )
    gain_two_term = jnp.sum(grad_normed * residual * scale_two, axis=0)
    grad_branch = grad_mid.astype(bf16)
    grad_heads = cols_dot(grad_branch, full_out).astype(bf16)
    pieces, offsets = columns_sent(grad_heads)
    pieces[1], heads_own = tie(pieces[1], heads_own)
    out_grad = rows_dot(heads_own, grad_branch).astype(bf16)
    pieces[2], out_grad = tie(pieces[2], out_grad)
    grad_heads = place(pieces, offsets, (token_count, grad_heads.shape[1] // zc))
    grad_heads, low, high = tie(grad_heads, *sum_step(outs, zc - 1))
    grad_heads, up, down = tie(grad_heads, *sum_parts(outs, 2, low, high))
    low, high = sum_send(up, down, 2)
    dnum, head_part = grad_tail_call(seq_ids, proj, grad_heads, numerator, denominator)
    outgoing = neighbour_sums(head_part, all_ids, -1, reach)
    low, high = sum_step(outs, 1, low, high)
    partial = local_call(seq_ids, proj, dnum, states)
    outgoing, low, high, partial = tie(outgoing, low, high, partial)
    result_own = (residual + outs[0] + low.astype(f32) + high.astype(f32)).astype(bf16)
    res_low, res_high = [along(result_own, 1)], [along(result_own, -1)]
    grad_qkv = backward_call(seq_ids, proj, dnum, partial, outgoing)
    grad_qkv, res_low[0], res_high[0], both_shard, out_grad = tie(
        grad_qkv, res_low[0], res_high[0], both_shard, out_grad
    )
    out_part = lax.psum_scatter(out_grad, "seq", scatter_dimension=0, tiled=True)
    qkv_grad = rows_dot(normed, grad_qkv)

    own_pieces, own_columns = rows_sent(grad_qkv)
    own_pieces[1], res_low[0], res_high[0] = tie(own_pieces[1], res_low[0], res_high[0])
    res_low.append(along(res_low[0], 1))
    res_high.append(along(res_high[0], -1))
    own_qkv = place(own_pieces, own_columns, (share, grad_qkv.shape[1] * zc), put_columns)
    grad_norm_one = cols_dot(own_qkv, all_qkv)
    grad_norm_one, res_low[1], res_high[1], down_shard = tie(
        grad_norm_one, res_low[1], res_high[1], down_shard
    )
    own_scale = lax.dynamic_slice_in_dim(scale_one, z * share, share, 0)
    weighted_one = grad_norm_one * gain_one
    grad_own = (
        grad_mid
        + own_scale * weighted_one
        - own_in * own_scale**3 * jnp.mean(weighted_one * own_in, axis=-1, keepdims=True)
    )
    gain_one_term = jnp.sum(grad_norm_one * own_in * own_scale, axis=0)
    tok_own, gain_one_term = tie(grad_own.astype(bf16), gain_one_term)
    out_cols = w_out.shape[1]
    tok_low, tok_high = [along(tok_own, 1)], [along(tok_own, -1)]
    for far in range(3, zc):
        res_low.append(along(res_low[-1], 1))
        res_high.append(along(res_high[-1], -1))
    tok_low[0], tok_high[0], res_low[-1], res_high[-1], out_part = tie(
        tok_low[0], tok_high[0], res_low[-1], res_high[-1], out_part
    )
    out_shard = lax.dynamic_slice_in_dim(out_part, z * out_cols, out_cols, 1).astype(f32)
    for k in range(1, zc):
        block = lax.dynamic_slice_in_dim(out_part, ((z + k) % zc) * out_cols, out_cols, 1)
        out_shard = out_shard + turn(block, "head", k).astype(f32)
    for far in range(2, zc):
        tok_low.append(along(tok_low[-1], 1))
        tok_high.append(along(tok_high[-1], -1))
    near_low, near_high = tok_low[:-1], tok_high[:-1]
    near_low[-1], out_shard = tie(near_low[-1], out_shard)

    def scatter(grad):
        return lax.psum_scatter(grad, "seq", scatter_dimension=0, tiled=True)

    down_shard = down_shard.astype(f32)
    both_shard = both_shard.astype(f32)
    gain_terms = jnp.pad(jnp.stack([gain_one_term, gain_two_term], axis=1), ((0, 0), (0, 126)))
    last = scatter(jnp.concatenate([qkv_grad, gain_terms], axis=1).astype(bf16)).astype(f32)
    gain_own = last[:, -128:-126].T[None]
    gain_parts = [gain_own] + [turn(gain_own, "head", k) for k in range(1, zc)]
    tok_low[-1], tok_high[-1], *gain_parts = tie(tok_low[-1], tok_high[-1], *gain_parts)
    gain_all = jnp.zeros((zc,) + gain_own.shape[1:], f32)
    for k, part in enumerate(gain_parts):
        gain_all = lax.dynamic_update_slice_in_dim(gain_all, part, (z - k) % zc, 0)
    gain_sums = jnp.sum(gain_all, axis=0)
    grad_tokens = join_line(tok_own, near_low, near_high, f32)
    grad_tokens = place(
        [tok_low[-1], tok_high[-1]],
        [(z - zc + 1) * share, jnp.where(z == 0, (zc - 1) * share, -1)],
        grad_tokens.shape,
        dtype=f32,
        base=grad_tokens,
    )
    result = join_line(result_own, res_low, res_high)
    return (
        result,
        grad_tokens,
        last[:, :qk_cols],
        last[:, qk_cols:-128],
        out_shard,
        both_shard[:, :hidden],
        both_shard[:, hidden:],
        down_shard,
        gain_sums[0],
        gain_sums[1],
    )


def solution(mesh):
    return jax.shard_map(
        body,
        mesh=mesh,
        in_specs=(
            P("seq", None),
            P("seq"),
            P("seq"),
            P("seq", "head"),
            P("seq", "head"),
            P("seq", "head"),
            P("seq"),
            P("seq", "head"),
            P("seq", "head"),
            P("seq", "head"),
            P("seq", None),
        ),
        out_specs=(
            P("seq", None),
            P("seq", None),
            P("seq", "head"),
            P("seq", "head"),
            P("seq", "head"),
            P("seq", "head"),
            P("seq", "head"),
            P("seq", "head"),
            P("seq"),
            P("seq"),
        ),
        check_vma=False,
    )
```

```python
import math

import jax
import jax.numpy as jnp
import numpy as np
from jax import lax
from jax.experimental import pallas as pl
from jax.experimental.pallas import tpu as pltpu
from jax.sharding import PartitionSpec as P

FEAT = 16
HV = 128
MAX_BLOCKS = 16


epsilon = 1e-06
bf16 = jnp.bfloat16
f32 = jnp.float32


FS = 160
FL = 256


def selection_tables(heads):
    pairs = [(a, b) for a in range(FEAT) for b in range(a, FEAT)]
    first = np.zeros((FEAT, FL), np.float32)
    second = np.zeros((FEAT, FL), np.float32)
    one_a, one_b = np.zeros(FL, np.float32), np.zeros(FL, np.float32)
    scale, twice = np.zeros(FL, np.float32), np.ones(FL, np.float32)
    one_a[0] = one_b[0] = scale[0] = 1.0
    for a in range(FEAT):
        first[a, 1 + a] = 1.0
        one_b[1 + a] = 1.0
        scale[1 + a] = 1.0 / FEAT**0.25
    for at, (a, b) in enumerate(pairs):
        at += 1 + FEAT
        first[a, at] = second[b, at] = 1.0
        scale[at] = 1.0 / (math.sqrt(2.0) * FEAT**0.5)
        twice[at] = 1.0 if a == b else 2.0
    cols = heads * 2 * FEAT
    wide = np.zeros((4, heads, cols, FL), np.float32)
    for h in range(heads):
        q0, k0 = h * 2 * FEAT, h * 2 * FEAT + FEAT
        wide[0, h, q0:k0], wide[1, h, q0:k0] = first, second
        wide[2, h, k0 : k0 + FEAT], wide[3, h, k0 : k0 + FEAT] = first, second
    tall = np.swapaxes(wide, 2, 3)[:, :, :FS].reshape(4, heads * FS, cols)
    rows = np.zeros((8, FL), np.float32)
    rows[0], rows[1], rows[2], rows[3] = one_a, one_b, scale, twice
    columns = np.repeat(rows[:3, :FS, None], cols, axis=2)
    return (
        jnp.asarray(np.moveaxis(wide, 1, 2).reshape(4, cols, heads * FL), bf16),
        jnp.asarray(np.ascontiguousarray(tall), bf16),
        jnp.asarray(rows, f32),
        jnp.asarray(columns, f32),
    )


def mm(left, right):
    return lax.dot_general(left, right, (((1,), (0,)), ((), ())), preferred_element_type=f32)


def mm_nt(left, right):
    return lax.dot_general(left, right, (((1,), (1,)), ((), ())), preferred_element_type=f32)


def lane_marks(rows, lanes):
    lane = lax.broadcasted_iota(jnp.int32, (rows, HV), 1)
    return (lane < lanes).astype(bf16)


def features_wide(x, wide, first, rows):
    one, two = mm(x, wide[first]), mm(x, wide[first + 1])
    parts = []
    for at in range(0, one.shape[1], FL):
        factors = one[:, at : at + FL] + rows[0:1], two[:, at : at + FL] + rows[1:2]
        parts.append((*factors, factors[0] * factors[1] * rows[2:3]))
    return parts


def features_tall(x, tall, first, columns):
    one, two = mm_nt(tall[first], x), mm_nt(tall[first + 1], x)
    parts = [slice(at, at + FS) for at in range(0, one.shape[0], FS)]
    return [
        ((one[at] + columns[0]) * (two[at] + columns[1]) * columns[2]).astype(bf16) for at in parts
    ]


def neighbours(x):
    lane = lax.broadcasted_iota(jnp.int32, x.shape, 1)
    wide = x.astype(f32)
    size = x.shape[1]
    from_k, from_q = pltpu.roll(wide, size - FEAT, 1), pltpu.roll(wide, FEAT, 1)
    pairs = []
    for at in range(0, size, 2 * FEAT):
        in_q = (lane >= at) & (lane < at + FEAT)
        in_k = (lane >= at + FEAT) & (lane < at + 2 * FEAT)
        pairs.append(
            (jnp.where(in_q, from_k, 0.0).astype(bf16), jnp.where(in_k, from_q, 0.0).astype(bf16))
        )
    return pairs


def split_state(state):
    left, right = state[:, :HV], state[:, HV:]
    lane = lax.broadcasted_iota(jnp.int32, right.shape, 1)
    high = right.astype(bf16)
    low = (right - high.astype(f32)).astype(bf16)
    return left.astype(bf16), jnp.where(lane == 2, low, high)


def join_state(state, both):
    right = state[:, HV:]
    lane = lax.broadcasted_iota(jnp.int32, right.shape, 1)
    whole = right[:, 0:1] + right[:, 2:3]
    if both:
        new = jnp.where(lane < 3, whole, 0.0)
    else:
        new = jnp.where(lane == 1, right, jnp.where(lane < 3, whole, 0.0))
    return jnp.concatenate([state[:, :HV], new], axis=1)


def tail_kernel(ids, proj, tall, columns, out, acc):
    at, last = pl.program_id(0), pl.num_programs(0) - 1
    heads = out.shape[0]
    qk = heads * 2 * FEAT

    @pl.when(at == 0)
    def _():
        acc[...] = jnp.zeros_like(acc)

    @pl.when(ids[at] == ids[last])
    def _():
        x = proj[:, :qk]
        marks = lane_marks(x.shape[0], 3)
        tall_k = features_tall(x, tall, 2, columns)
        for h in range(heads):
            v = proj[:, qk + h * HV : qk + (h + 1) * HV]
            acc[h] += mm(tall_k[h], jnp.concatenate([v, marks], axis=1))

    @pl.when(at == last)
    def _():
        for h in range(heads):
            left, right = split_state(acc[h])
            out[h, :, :HV] = left
            out[h, :, HV:] = right


def inner_kernel(ids, proj, num_out, den_out):
    heads = num_out.shape[1] // HV
    qk = heads * 2 * FEAT
    x = proj[:, :qk]
    pairs = neighbours(x)
    size = x.shape[0]
    row = lax.broadcasted_iota(jnp.int32, (size, size), 0)
    col = lax.broadcasted_iota(jnp.int32, (size, size), 1)
    lane = lax.broadcasted_iota(jnp.int32, (size, HV), 1)
    dens = jnp.zeros((size, HV), f32)
    for h in range(heads):
        v = proj[:, qk + h * HV : qk + (h + 1) * HV]
        s = mm_nt(x, pairs[h][0]) * FEAT**-0.5
        a = jnp.where(row >= col, 1.0 + s + 0.5 * s * s, 0.0)
        num_out[:, h * HV : (h + 1) * HV] = mm(a.astype(bf16), v)
        dens = jnp.where(lane == h, jnp.sum(a, axis=1, keepdims=True), dens)
    den_out[...] = dens


def forward_kernel(
    ids, proj, num_in, den_in, incoming, wide, tall, rows, columns, heads_out, num_out, den_out, state_out, acc
):
    at = pl.program_id(0)
    heads = acc.shape[0]
    qk = heads * 2 * FEAT

    @pl.when(at == 0)
    def _():
        for h in range(heads):
            acc[h] = join_state(incoming[h], True)

    @pl.when((at > 0) & (ids[at] != ids[jnp.maximum(at - 1, 0)]))
    def _():
        acc[...] = jnp.zeros_like(acc)

    x = proj[:, :qk]
    size = x.shape[0]
    marks = lane_marks(size, 3)
    lane = lax.broadcasted_iota(jnp.int32, (size, HV), 1)
    tall_k = features_tall(x, tall, 2, columns)
    wide_q = features_wide(x, wide, 0, rows)
    dens = jnp.zeros((size, HV), f32)
    for h in range(heads):
        v = proj[:, qk + h * HV : qk + (h + 1) * HV]
        left, right = split_state(acc[h])
        state = jnp.concatenate(
            [jnp.concatenate([left, right], axis=1), jnp.zeros((FL - FS, 2 * HV), bf16)], axis=0
        )
        state_out[0, h] = state
        _, _, fq = wide_q[h]
        fq = fq.astype(bf16) * rows[3:4].astype(bf16)
        ext = mm(fq, state)
        num = num_in[:, h * HV : (h + 1) * HV] + ext[:, :HV]
        den = den_in[:, h : h + 1] + ext[:, HV : HV + 1] + ext[:, HV + 2 : HV + 3]
        heads_out[:, h * HV : (h + 1) * HV] = (num * (1.0 / den)).astype(bf16)
        num_out[:, h * HV : (h + 1) * HV] = num
        dens = jnp.where(lane == h, den, dens)
        acc[h] += mm(tall_k[h], jnp.concatenate([v, marks], axis=1))
    den_out[...] = dens


def grad_tail_kernel(ids, proj, dheads, num, den, tall, columns, dnum_out, out, acc):
    at, last = pl.program_id(0), pl.num_programs(0) - 1
    heads = out.shape[0]
    qk = heads * 2 * FEAT

    @pl.when(at == 0)
    def _():
        acc[...] = jnp.zeros_like(acc)

    x = proj[:, :qk]
    size = x.shape[0]
    lane = lax.broadcasted_iota(jnp.int32, (size, HV), 1)
    for h in range(heads):
        d = den[:, h : h + 1]
        g = dheads[:, h * HV : (h + 1) * HV].astype(f32)
        inverse = 1.0 / d
        dnum = (g * inverse).astype(bf16)
        dden = -jnp.sum(g * num[:, h * HV : (h + 1) * HV], axis=1, keepdims=True) * (
            inverse * inverse
        )
        high = dden.astype(bf16)
        low = (dden - high.astype(f32)).astype(bf16)
        side = jnp.where(
            (lane == 0) | (lane == 2), high.astype(f32), jnp.where(lane == 1, low.astype(f32), 0.0)
        ).astype(bf16)
        dnum_out[:, h * 2 * HV : h * 2 * HV + HV] = dnum
        dnum_out[:, h * 2 * HV + HV : (h + 1) * 2 * HV] = side

    @pl.when(ids[at] == ids[0])
    def _():
        tall_q = features_tall(x, tall, 0, columns)
        for h in range(heads):
            acc[h] += mm(tall_q[h], dnum_out[:, h * 2 * HV : (h + 1) * 2 * HV])

    @pl.when(at == last)
    def _():
        for h in range(heads):
            left, right = split_state(acc[h])
            out[h, :, :HV] = left
            out[h, :, HV:] = right


def local_kernel(ids, proj, dnum_in, state_in, wide, rows, out):
    heads = wide.shape[2] // FL
    qk = heads * 2 * FEAT
    x = proj[:, :qk]
    pairs = neighbours(x)
    wide_q, by_one, by_two = features_wide(x, wide, 0, rows), [], []
    size = x.shape[0]
    row = lax.broadcasted_iota(jnp.int32, (size, size), 0)
    col = lax.broadcasted_iota(jnp.int32, (size, size), 1)
    marks = lane_marks(size, 2)
    weight = rows[2:3] * rows[3:4]
    total = jnp.zeros((size, qk), f32)
    for h in range(heads):
        v = proj[:, qk + h * HV : qk + (h + 1) * HV]
        dn = dnum_in[:, h * 2 * HV : (h + 1) * 2 * HV]
        q1, q2, _ = wide_q[h]
        kq, qk_moved = pairs[h]
        s = mm_nt(x, kq) * FEAT**-0.5
        st = mm_nt(kq, x) * FEAT**-0.5
        at_low = jnp.where(row <= col, 1.0 + st + 0.5 * st * st, 0.0).astype(bf16)
        v2 = jnp.concatenate([v, marks], axis=1)
        da = mm_nt(dn, v2)
        dat = mm_nt(v2, dn)
        draw = jnp.where(row >= col, da * (1.0 + s) * FEAT**-0.5, 0.0).astype(bf16)
        drawt = jnp.where(row <= col, dat * (1.0 + st) * FEAT**-0.5, 0.0).astype(bf16)
        wq = mm_nt(dn, state_in[0, h]) * weight
        total += mm(draw, kq) + mm(drawt, qk_moved)
        by_two.append((wq * q2).astype(bf16))
        by_one.append((wq * q1).astype(bf16))
        out[:, qk + h * HV : qk + (h + 1) * HV] = mm(at_low, dn[:, :HV])
    total += mm_nt(jnp.concatenate(by_two, axis=1), wide[0])
    out[:, :qk] = total + mm_nt(jnp.concatenate(by_one, axis=1), wide[1])


def backward_kernel(ids, proj, dnum_in, local, incoming, wide, tall, rows, columns, out, acc):
    step, last = pl.program_id(0), pl.num_programs(0) - 1
    at = last - step
    heads = acc.shape[0]
    qk = heads * 2 * FEAT

    @pl.when(step == 0)
    def _():
        for h in range(heads):
            acc[h] = join_state(incoming[h], False)

    @pl.when((step > 0) & (ids[at] != ids[jnp.minimum(at + 1, last)]))
    def _():
        acc[...] = jnp.zeros_like(acc)

    x = proj[:, :qk]
    marks = lane_marks(x.shape[0], 3)
    weight = rows[2:3] * rows[3:4]
    twice = rows[3:4].astype(bf16)
    tall_q = features_tall(x, tall, 0, columns)
    wide_k, by_one, by_two = features_wide(x, wide, 2, rows), [], []
    total = local[:, :qk]
    for h in range(heads):
        v = proj[:, qk + h * HV : qk + (h + 1) * HV]
        left, right = split_state(acc[h])
        dstate = jnp.concatenate(
            [jnp.concatenate([left, right], axis=1), jnp.zeros((FL - FS, 2 * HV), bf16)], axis=0
        )
        k1, k2, fk = wide_k[h]
        fk = fk.astype(bf16) * twice
        wk = mm_nt(jnp.concatenate([v, marks], axis=1), dstate) * weight
        by_two.append((wk * k2).astype(bf16))
        by_one.append((wk * k1).astype(bf16))
        dv = local[:, qk + h * HV : qk + (h + 1) * HV] + mm(fk, dstate[:, :HV])
        out[:, qk + h * HV : qk + (h + 1) * HV] = dv.astype(bf16)
        acc[h] += mm(tall_q[h], dnum_in[:, h * 2 * HV : (h + 1) * 2 * HV])
    total += mm_nt(jnp.concatenate(by_two, axis=1), wide[2])
    total += mm_nt(jnp.concatenate(by_one, axis=1), wide[3])
    out[:, :qk] = total.astype(bf16)


def whole_spec(array):
    zeros = (0,) * array.ndim
    return pl.BlockSpec(array.shape, lambda i, ids: zeros)


def attention_calls(blocks, block_len, heads, tables):
    wide, tall, rows, columns = tables
    qk = heads * 2 * FEAT
    tokens = blocks * block_len
    state = (heads, FS, 2 * HV)

    def at_block(cols, reverse=False):
        if reverse:
            return pl.BlockSpec((block_len, cols), lambda i, ids: (blocks - 1 - i, 0))
        return pl.BlockSpec((block_len, cols), lambda i, ids: (i, 0))

    def states_spec(reverse=False):
        if reverse:
            return pl.BlockSpec((1, heads, FL, 2 * HV), lambda i, ids: (blocks - 1 - i, 0, 0, 0))
        return pl.BlockSpec((1, heads, FL, 2 * HV), lambda i, ids: (i, 0, 0, 0))

    def call(kernel, name, in_specs, out_specs, out_shape, flops, moved, carried=True):
        return pl.pallas_call(
            kernel,
            out_shape=out_shape,
            grid_spec=pltpu.PrefetchScalarGridSpec(
                num_scalar_prefetch=1,
                grid=(blocks,),
                in_specs=in_specs,
                out_specs=out_specs,
                scratch_shapes=[pltpu.VMEM(state, f32)] if carried else [],
            ),
            compiler_params=pltpu.CompilerParams(dimension_semantics=("arbitrary",)),
            cost_estimate=pl.CostEstimate(flops=flops, transcendentals=0, bytes_accessed=moved),
            name=name,
        )

    full_state = pl.BlockSpec(state, lambda i, ids: (0, 0, 0))
    proj_cols = qk + heads * HV

    def tail(ids, proj):
        return call(
            tail_kernel,
            "state_tail",
            [at_block(proj_cols), whole_spec(tall), whole_spec(columns)],
            full_state,
            jax.ShapeDtypeStruct(state, bf16),
            int(4e9),
            int(4e6),
        )(ids, proj, tall, columns)

    def inner(ids, proj):
        return call(
            inner_kernel,
            "attention_inner",
            [at_block(proj_cols)],
            [at_block(heads * HV), at_block(HV)],
            [
                jax.ShapeDtypeStruct((tokens, heads * HV), f32),
                jax.ShapeDtypeStruct((tokens, HV), f32),
            ],
            int(4e9),
            int(4e6),
            False,
        )(ids, proj)

    def forward(ids, proj, num, den, incoming):
        return call(
            forward_kernel,
            "attention_forward",
            [at_block(proj_cols), at_block(heads * HV), at_block(HV), full_state]
            + [whole_spec(t) for t in (wide, tall, rows, columns)],
            [at_block(heads * HV), at_block(heads * HV), at_block(HV), states_spec()],
            [
                jax.ShapeDtypeStruct((tokens, heads * HV), bf16),
                jax.ShapeDtypeStruct((tokens, heads * HV), f32),
                jax.ShapeDtypeStruct((tokens, HV), f32),
                jax.ShapeDtypeStruct((blocks, heads, FL, 2 * HV), bf16),
            ],
            int(6e9),
            int(2e7),
        )(ids, proj, num, den, incoming, wide, tall, rows, columns)

    def grad_tail(ids, proj, dheads, num, den):
        return call(
            grad_tail_kernel,
            "state_grad_tail",
            [at_block(proj_cols), at_block(heads * HV), at_block(heads * HV), at_block(HV)]
            + [whole_spec(tall), whole_spec(columns)],
            [at_block(heads * 2 * HV), full_state],
            [
                jax.ShapeDtypeStruct((tokens, heads * 2 * HV), bf16),
                jax.ShapeDtypeStruct(state, bf16),
            ],
            int(4e9),
            int(1e7),
        )(ids, proj, dheads, num, den, tall, columns)

    def local(ids, proj, dnum, states):
        return call(
            local_kernel,
            "attention_backward_local",
            [at_block(proj_cols), at_block(heads * 2 * HV), states_spec()]
            + [whole_spec(t) for t in (wide, rows)],
            at_block(proj_cols),
            jax.ShapeDtypeStruct((tokens, proj_cols), f32),
            int(1.3e10),
            int(2e7),
            False,
        )(ids, proj, dnum, states, wide, rows)

    def backward(ids, proj, dnum, partial, incoming):
        return call(
            backward_kernel,
            "attention_backward",
            [at_block(proj_cols, True), at_block(heads * 2 * HV, True)]
            + [at_block(proj_cols, True), full_state]
            + [whole_spec(t) for t in (wide, tall, rows, columns)],
            at_block(proj_cols, True),
            jax.ShapeDtypeStruct((tokens, proj_cols), bf16),
            int(1e10),
            int(2e7),
        )(ids, proj, dnum, partial, incoming, wide, tall, rows, columns)

    return tail, inner, forward, grad_tail, local, backward


def rows_dot(left, right):
    return lax.dot_general(left, right, (((0,), (0,)), ((), ())), preferred_element_type=f32)


def cols_dot(left, right):
    return lax.dot_general(left, right, (((1,), (1,)), ((), ())), preferred_element_type=f32)


def dot(left, right):
    return jnp.dot(left, right, preferred_element_type=f32)


def turn(value, axis, step):
    count = lax.axis_size(axis)
    return lax.ppermute(value, axis, [(i, (i + step) % count) for i in range(count)])


def tie(*values):
    return lax.optimization_barrier(values)


def put_rows(out, piece, at):
    return out.at[pl.ds(pl.multiple_of(at[0], 128), piece[0])]


def put_columns(out, piece, at):
    return out.at[:, pl.ds(pl.multiple_of(at[0], 128), piece[1])]


def place(pieces, offsets, shape, put=put_rows, dtype=None, base=None):
    count = len(pieces)
    kept = pieces[0].dtype
    dtype = dtype or kept
    wider = dtype != kept
    offsets = [at if isinstance(at, tuple) else (at,) for at in offsets]
    per = len(offsets[0])

    given = count + (base is not None)

    def kernel(offs, *refs):
        out = refs[given]
        held = refs[given + 1 : given + count + 1]
        sent = refs[given + count + 1 : given + 2 * count + 1] if wider else held
        sems = refs[-1]

        def bring(j):
            return pltpu.make_async_copy(refs[j], held[j], sems.at[0, j])

        def send(j):
            at = [jnp.maximum(offs[j * per + i], 0) for i in range(per)]
            return pltpu.make_async_copy(sent[j], put(out, pieces[j].shape, at), sems.at[1, j])

        def each(action):
            for j in range(count):

                @pl.when(offs[j * per] >= 0)
                def _(j=j):
                    action(j)

        def forward(j):
            bring(j).wait()
            if wider:
                sent[j][...] = held[j][...].astype(dtype)
            send(j).start()

        each(lambda j: bring(j).start())
        each(forward)
        each(lambda j: send(j).wait())

    anywhere = pl.BlockSpec(memory_space=pl.ANY)
    size = int(np.prod(shape))
    buffers = [pltpu.VMEM(piece.shape, kept) for piece in pieces]
    if wider:
        buffers += [pltpu.VMEM(piece.shape, dtype) for piece in pieces]
    return pl.pallas_call(
        kernel,
        out_shape=jax.ShapeDtypeStruct(shape, dtype),
        grid_spec=pltpu.PrefetchScalarGridSpec(
            num_scalar_prefetch=1,
            grid=(1,),
            in_specs=[anywhere] * given,
            out_specs=anywhere,
            scratch_shapes=buffers + [pltpu.SemaphoreType.DMA((2, count))],
        ),
        cost_estimate=pl.CostEstimate(flops=0, transcendentals=0, bytes_accessed=4 * size),
        input_output_aliases={} if base is None else {given: 0},
        name="place",
    )(
        jnp.stack([jnp.asarray(o, jnp.int32) for at in offsets for o in at]),
        *pieces,
        *([] if base is None else [base]),
    )


def swap(value, mask):
    count = lax.axis_size("seq")
    return lax.ppermute(value, "seq", [(i, i ^ mask) for i in range(count)])


def gather_start(part):
    half = part.shape[0] // 2
    if lax.axis_size("seq") != 8 or half % 128:
        return [lax.all_gather(part, "seq", axis=0, tiled=True)]
    top, low = part[:half], part[half:]
    return [top, low, swap(top, 2), swap(low, 4), swap(top, 4), swap(low, 2)]


def gather_next(held):
    return held if len(held) == 1 else held + [swap(held[2], 4), swap(held[3], 2)]


def gather_last(held):
    if len(held) == 1:
        return held[0]
    count, mine = lax.axis_size("seq"), lax.axis_index("seq")
    half, width = held[0].shape
    places = [(0, 0), (0, 1), (2, 0), (4, 1), (4, 0), (2, 1), (6, 0), (6, 1)]
    pieces = dict(zip(places, held))
    pieces |= {(mask | 1, side): swap(piece, 1) for (mask, side), piece in pieces.items()}
    offsets = [((mine ^ mask) * 2 + side) * half for mask, side in pieces]
    return place(list(pieces.values()), offsets, (2 * half * count, width))


def gather_columns(block, axis):
    count, mine = lax.axis_size(axis), lax.axis_index(axis)
    width = block.shape[1]
    pieces = [block] + [turn(block, axis, step) for step in range(1, count)]
    offsets = [((mine - step) % count) * width for step in range(count)]
    return place(pieces, offsets, (block.shape[0], width * count), put_columns)


def rows_sent(value):
    count, mine = lax.axis_size("head"), lax.axis_index("head")
    rows, width = value.shape[0] // count, value.shape[1]

    def block(k):
        return lax.dynamic_slice_in_dim(value, ((mine + k) % count) * rows, rows, 0)

    pieces = [block(0)] + [turn(block(k), "head", k) for k in range(1, count)]
    return pieces, [((mine - k) % count) * width for k in range(count)]


def columns_sent(value):
    count, mine = lax.axis_size("head"), lax.axis_index("head")
    rows, width = value.shape[0], value.shape[1] // count

    def block(k):
        return lax.dynamic_slice_in_dim(value, ((mine + k) % count) * width, width, 1)

    pieces = [block(0)] + [turn(block(k), "head", k) for k in range(1, count)]
    return pieces, [((mine - k) % count) * rows for k in range(count)]


def along(value, step):
    count = lax.axis_size("head")
    pairs = [(i, i + step) for i in range(count) if 0 <= i + step < count]
    return lax.ppermute(value, "head", pairs)


def sum_parts(parts, far, low=None, high=None):
    count = lax.axis_size("head")
    up, down = parts[-far % count], parts[far]
    if low is not None:
        up = (up.astype(f32) + low.astype(f32)).astype(bf16)
        down = (down.astype(f32) + high.astype(f32)).astype(bf16)
    return up, down


def sum_send(up, down, far):
    count = lax.axis_size("head")
    return (
        lax.ppermute(up, "head", [(i, i + 1) for i in range(count - far)]),
        lax.ppermute(down, "head", [(i, i - 1) for i in range(far, count)]),
    )


def sum_step(parts, far, low=None, high=None):
    return sum_send(*sum_parts(parts, far, low, high), far)


def join_line(own, from_low, from_high, dtype=None):
    count, mine = lax.axis_size("head"), lax.axis_index("head")
    rows = own.shape[0]
    pieces, offsets = [own], [mine * rows]
    for far, (low, high) in enumerate(zip(from_low, from_high), 1):
        pieces += [low, high]
        offsets.append((mine - far) * rows)
        offsets.append(jnp.where(mine + far < count, (mine + far) * rows, -1))
    return place(pieces, offsets, (rows * count, own.shape[1]), dtype=dtype)


def neighbour_sums(tail, all_ids, step, reach):
    count, mine = lax.axis_size("seq"), lax.axis_index("seq")
    theirs, own = (all_ids[:, -1], all_ids[:, 0]) if step > 0 else (all_ids[:, 0], all_ids[:, -1])
    own = lax.dynamic_index_in_dim(own, mine, 0, keepdims=False)
    total = jnp.zeros(tail.shape, f32)
    for k in range(1, min(reach, count - 1) + 1):
        pairs = [(i, i + k * step) for i in range(count) if 0 <= i + k * step < count]
        got = lax.ppermute(tail, "seq", pairs)
        at = mine - k * step
        other = lax.dynamic_index_in_dim(theirs, jnp.clip(at, 0, count - 1), 0, keepdims=False)
        use = (at >= 0) & (at < count) & (other == own)
        total = total + jnp.where(use, got.astype(f32), 0.0)
    return total


def body(tokens, seq_ids, gain_attn, w_qk, w_v, w_out, gain_mlp, w_gate, w_up, w_down, cotangent):
    zc, z = lax.axis_size("head"), lax.axis_index("head")
    token_count, width = tokens.shape
    blocks = seq_ids.shape[0]
    block_len = token_count // blocks
    heads_here = w_v.shape[1] // HV
    qk_cols = w_qk.shape[1]
    share = token_count // zc
    reach = -(-(MAX_BLOCKS - 1) // blocks)

    small = jnp.pad(seq_ids.astype(bf16), (0, gain_attn.shape[0] - blocks))
    small = jnp.stack([gain_attn, gain_mlp, small])
    small = lax.all_gather(small, "seq", axis=1, tiled=True).astype(f32)
    gain_one, gain_two = small[0], small[1]
    all_ids = small[2].reshape(lax.axis_size("seq"), gain_attn.shape[0])[:, :blocks]
    qkv_part = jnp.concatenate([w_qk, w_v], axis=1)
    full_qkv = lax.all_gather(qkv_part, "seq", axis=0, tiled=True)
    full_both = lax.all_gather(
        jnp.concatenate([w_gate, w_up], axis=1), "seq", axis=0, tiled=True
    )
    out_rows = gather_columns(w_out, "head")

    inputs = tokens.astype(f32)
    scale_one = lax.rsqrt(jnp.mean(inputs * inputs, axis=-1, keepdims=True) + epsilon)
    normed = (inputs * scale_one * gain_one).astype(bf16)
    qkv_blocks = {k: turn(qkv_part, "head", k) for k in range(1, zc)}
    full_qkv, normed, out_rows, qkv_blocks[1], qkv_blocks[zc - 1] = tie(
        full_qkv, normed, out_rows, qkv_blocks[1], qkv_blocks[zc - 1]
    )
    full_out = lax.all_gather(out_rows, "seq", axis=0, tiled=True)
    proj = dot(normed, full_qkv).astype(bf16)
    tables = selection_tables(heads_here)
    tail_call, inner_call, forward_call, grad_tail_call, local_call, backward_call = (
        attention_calls(blocks, block_len, heads_here, tables)
    )
    tail, qkv_blocks[2] = tie(tail_call(seq_ids, proj), qkv_blocks[2])
    qkv_rows = place(
        [qkv_part] + [qkv_blocks[k] for k in range(1, zc)],
        [((z - k) % zc) * qkv_part.shape[1] for k in range(zc)],
        (qkv_part.shape[0], qkv_part.shape[1] * zc),
        put_columns,
    )
    incoming = neighbour_sums(tail, all_ids, 1, reach)
    inner = inner_call(seq_ids, tie(proj, tail)[0])
    incoming, *inner = tie(incoming, *inner)
    head_rows, numerator, denominator, states = forward_call(seq_ids, proj, *inner, incoming)
    down_held = gather_start(tie(w_down, head_rows)[0])
    all_qkv = lax.all_gather(qkv_rows, "seq", axis=0, tiled=True)

    heads_own = place(*rows_sent(head_rows), (share, heads_here * HV * zc), put_columns)
    own_in = lax.dynamic_slice_in_dim(tokens, z * share, share, 0).astype(f32)
    residual = own_in + dot(heads_own, full_out)
    scale_two = lax.rsqrt(jnp.mean(residual * residual, axis=-1, keepdims=True) + epsilon)
    normed_own = (residual * scale_two * gain_two).astype(bf16)

    normed_own, *down_held = tie(normed_own, *down_held)
    full_down = gather_last(gather_next(down_held))
    order = [0] + sorted(range(1, zc), key=lambda k: min(k, zc - k))
    hidden = w_gate.shape[1]
    normed_parts, cot_parts, act_parts, both_parts = [], [], [], []
    backs = {}
    got_first, first_own, later = tie(turn(normed_own, "head", order[1]), normed_own, normed_own)
    arrivals = {0: first_own, order[1]: got_first}
    for k in order[2:]:
        arrivals[k] = turn(later, "head", k)
    for k in order:
        normed_two = arrivals[k]
        owner = (z - k) % zc
        cot = lax.dynamic_slice_in_dim(cotangent, owner * share, share, 0)
        pre = dot(normed_two, full_both)
        gate_pre, up_pre = pre[:, :hidden], pre[:, hidden:]
        gate_sigmoid = jax.nn.sigmoid(gate_pre)
        active = (gate_pre * gate_sigmoid * up_pre).astype(bf16)
        grad_active = dot(cot, full_down)
        grad_gate = grad_active * up_pre * gate_sigmoid * (1.0 + gate_pre * (1.0 - gate_sigmoid))
        grad_upper = grad_active * gate_pre * gate_sigmoid
        grad_both = jnp.concatenate([grad_gate.astype(bf16), grad_upper.astype(bf16)], axis=1)
        backs[k] = cols_dot(grad_both, full_both)
        if k:
            backs[k] = backs[k].astype(bf16)
        if k != order[-1]:
            following = order[order.index(k) + 1]
            arrivals[following], backs[k] = tie(arrivals[following], backs[k])
        normed_parts.append(normed_two)
        cot_parts.append(cot)
        act_parts.append(active)
        both_parts.append(grad_both)
    low = high = None
    for far in range(zc - 1, 2, -1):
        low, high = sum_step(backs, far, low, high)
    up, down = sum_parts(backs, 2, low, high)
    up, down, normed_parts[0], both_parts[0], cot_parts[0], *act_parts = tie(
        up, down, normed_parts[0], both_parts[0], cot_parts[0], *act_parts
    )
    low, high = sum_send(up, down, 2)
    both_grad = rows_dot(jnp.concatenate(normed_parts), jnp.concatenate(both_parts)).astype(bf16)
    low, high, act_parts[0], both_grad = tie(low, high, act_parts[0], both_grad)
    both_shard = lax.psum_scatter(both_grad, "seq", scatter_dimension=0, tiled=True)
    up, down = sum_parts(backs, 1, low, high)
    up, down, *act_parts = tie(up, down, *act_parts)
    low, high = sum_send(up, down, 1)
    outs = {k: cols_dot(active, full_down) for k, active in zip(order, act_parts)}
    outs = {k: out.astype(bf16) if k else out for k, out in outs.items()}
    down_grad = rows_dot(jnp.concatenate(cot_parts), jnp.concatenate(act_parts)).astype(bf16)
    tied = tie(backs[0], low, high, all_qkv, down_grad, *[outs[k] for k in order])
    grad_normed = tied[0] + tied[1].astype(f32) + tied[2].astype(f32)
    all_qkv, down_grad = tied[3:5]
    down_shard = lax.psum_scatter(down_grad, "seq", scatter_dimension=0, tiled=True)
    outs = dict(zip(order, tied[5:]))

    cot_own = lax.dynamic_slice_in_dim(cotangent, z * share, share, 0).astype(f32)
    weighted = grad_normed * gain_two
    grad_mid = (
        cot_own
        + scale_two * weighted
        - residual * scale_two**3 * jnp.mean(weighted * residual, axis=-1, keepdims=True)
    )
    gain_two_term = jnp.sum(grad_normed * residual * scale_two, axis=0)
    grad_branch = grad_mid.astype(bf16)
    grad_heads = cols_dot(grad_branch, full_out).astype(bf16)
    pieces, offsets = columns_sent(grad_heads)
    pieces[1], heads_own = tie(pieces[1], heads_own)
    out_grad = rows_dot(heads_own, grad_branch).astype(bf16)
    pieces[2], out_grad = tie(pieces[2], out_grad)
    grad_heads = place(pieces, offsets, (token_count, grad_heads.shape[1] // zc))
    grad_heads, low, high = tie(grad_heads, *sum_step(outs, zc - 1))
    grad_heads, up, down = tie(grad_heads, *sum_parts(outs, 2, low, high))
    low, high = sum_send(up, down, 2)
    dnum, head_part = grad_tail_call(seq_ids, proj, grad_heads, numerator, denominator)
    outgoing = neighbour_sums(head_part, all_ids, -1, reach)
    low, high = sum_step(outs, 1, low, high)
    partial = local_call(seq_ids, proj, dnum, states)
    outgoing, low, high, partial = tie(outgoing, low, high, partial)
    result_own = (residual + outs[0] + low.astype(f32) + high.astype(f32)).astype(bf16)
    res_low, res_high = [along(result_own, 1)], [along(result_own, -1)]
    grad_qkv = backward_call(seq_ids, proj, dnum, partial, outgoing)
    grad_qkv, res_low[0], res_high[0], both_shard, out_grad = tie(
        grad_qkv, res_low[0], res_high[0], both_shard, out_grad
    )
    out_part = lax.psum_scatter(out_grad, "seq", scatter_dimension=0, tiled=True)
    qkv_grad = rows_dot(normed, grad_qkv)

    own_pieces, own_columns = rows_sent(grad_qkv)
    own_pieces[1], res_low[0], res_high[0] = tie(own_pieces[1], res_low[0], res_high[0])
    res_low.append(along(res_low[0], 1))
    res_high.append(along(res_high[0], -1))
    own_qkv = place(own_pieces, own_columns, (share, grad_qkv.shape[1] * zc), put_columns)
    grad_norm_one = cols_dot(own_qkv, all_qkv)
    grad_norm_one, res_low[1], res_high[1], down_shard = tie(
        grad_norm_one, res_low[1], res_high[1], down_shard
    )
    own_scale = lax.dynamic_slice_in_dim(scale_one, z * share, share, 0)
    weighted_one = grad_norm_one * gain_one
    grad_own = (
        grad_mid
        + own_scale * weighted_one
        - own_in * own_scale**3 * jnp.mean(weighted_one * own_in, axis=-1, keepdims=True)
    )
    gain_one_term = jnp.sum(grad_norm_one * own_in * own_scale, axis=0)
    tok_own, gain_one_term = tie(grad_own.astype(bf16), gain_one_term)
    out_cols = w_out.shape[1]
    tok_low, tok_high = [along(tok_own, 1)], [along(tok_own, -1)]
    for far in range(3, zc):
        res_low.append(along(res_low[-1], 1))
        res_high.append(along(res_high[-1], -1))
    tok_low[0], tok_high[0], res_low[-1], res_high[-1], out_part = tie(
        tok_low[0], tok_high[0], res_low[-1], res_high[-1], out_part
    )
    out_shard = lax.dynamic_slice_in_dim(out_part, z * out_cols, out_cols, 1).astype(f32)
    for k in range(1, zc):
        block = lax.dynamic_slice_in_dim(out_part, ((z + k) % zc) * out_cols, out_cols, 1)
        out_shard = out_shard + turn(block, "head", k).astype(f32)
    for far in range(2, zc):
        tok_low.append(along(tok_low[-1], 1))
        tok_high.append(along(tok_high[-1], -1))
    near_low, near_high = tok_low[:-1], tok_high[:-1]
    near_low[-1], out_shard = tie(near_low[-1], out_shard)

    def scatter(grad):
        return lax.psum_scatter(grad, "seq", scatter_dimension=0, tiled=True)

    down_shard = down_shard.astype(f32)
    both_shard = both_shard.astype(f32)
    gain_terms = jnp.pad(jnp.stack([gain_one_term, gain_two_term], axis=1), ((0, 0), (0, 126)))
    last = scatter(jnp.concatenate([qkv_grad, gain_terms], axis=1).astype(bf16)).astype(f32)
    gain_own = last[:, -128:-126].T[None]
    gain_parts = [gain_own] + [turn(gain_own, "head", k) for k in range(1, zc)]
    tok_low[-1], tok_high[-1], *gain_parts = tie(tok_low[-1], tok_high[-1], *gain_parts)
    gain_all = jnp.zeros((zc,) + gain_own.shape[1:], f32)
    for k, part in enumerate(gain_parts):
        gain_all = lax.dynamic_update_slice_in_dim(gain_all, part, (z - k) % zc, 0)
    gain_sums = jnp.sum(gain_all, axis=0)
    grad_tokens = join_line(tok_own, near_low, near_high, f32)
    grad_tokens = place(
        [tok_low[-1], tok_high[-1]],
        [(z - zc + 1) * share, jnp.where(z == 0, (zc - 1) * share, -1)],
        grad_tokens.shape,
        dtype=f32,
        base=grad_tokens,
    )
    result = join_line(result_own, res_low, res_high)
    return (
        result,
        grad_tokens,
        last[:, :qk_cols],
        last[:, qk_cols:-128],
        out_shard,
        both_shard[:, :hidden],
        both_shard[:, hidden:],
        down_shard,
        gain_sums[0],
        gain_sums[1],
    )


def solution(mesh):
    return jax.shard_map(
        body,
        mesh=mesh,
        in_specs=(
            P("seq", None),
            P("seq"),
            P("seq"),
            P("seq", "head"),
            P("seq", "head"),
            P("seq", "head"),
            P("seq"),
            P("seq", "head"),
            P("seq", "head"),
            P("seq", "head"),
            P("seq", None),
        ),
        out_specs=(
            P("seq", None),
            P("seq", None),
            P("seq", "head"),
            P("seq", "head"),
            P("seq", "head"),
            P("seq", "head"),
            P("seq", "head"),
            P("seq", "head"),
            P("seq"),
            P("seq"),
        ),
        check_vma=False,
    )
```

```python
import math

import jax
import jax.numpy as jnp
import numpy as np
from jax import lax
from jax.experimental import pallas as pl
from jax.experimental.pallas import tpu as pltpu
from jax.sharding import PartitionSpec as P

FEAT = 16
HV = 128
MAX_BLOCKS = 16


epsilon = 1e-06
bf16 = jnp.bfloat16
f32 = jnp.float32


FS = 160
FL = 256


def selection_tables(heads):
    pairs = [(a, b) for a in range(FEAT) for b in range(a, FEAT)]
    first = np.zeros((FEAT, FL), np.float32)
    second = np.zeros((FEAT, FL), np.float32)
    one_a, one_b = np.zeros(FL, np.float32), np.zeros(FL, np.float32)
    scale, twice = np.zeros(FL, np.float32), np.ones(FL, np.float32)
    one_a[0] = one_b[0] = scale[0] = 1.0
    for a in range(FEAT):
        first[a, 1 + a] = 1.0
        one_b[1 + a] = 1.0
        scale[1 + a] = 1.0 / FEAT**0.25
    for at, (a, b) in enumerate(pairs):
        at += 1 + FEAT
        first[a, at] = second[b, at] = 1.0
        scale[at] = 1.0 / (math.sqrt(2.0) * FEAT**0.5)
        twice[at] = 1.0 if a == b else 2.0
    cols = heads * 2 * FEAT
    wide = np.zeros((4, heads, cols, FL), np.float32)
    for h in range(heads):
        q0, k0 = h * 2 * FEAT, h * 2 * FEAT + FEAT
        wide[0, h, q0:k0], wide[1, h, q0:k0] = first, second
        wide[2, h, k0 : k0 + FEAT], wide[3, h, k0 : k0 + FEAT] = first, second
    tall = np.swapaxes(wide, 2, 3)[:, :, :FS].reshape(4, heads * FS, cols)
    rows = np.zeros((8, FL), np.float32)
    rows[0], rows[1], rows[2], rows[3] = one_a, one_b, scale, twice
    columns = np.repeat(rows[:3, :FS, None], cols, axis=2)
    return (
        jnp.asarray(wide, bf16),
        jnp.asarray(np.ascontiguousarray(tall), bf16),
        jnp.asarray(rows, f32),
        jnp.asarray(columns, f32),
    )


def mm(left, right):
    return lax.dot_general(left, right, (((1,), (0,)), ((), ())), preferred_element_type=f32)


def mm_nt(left, right):
    return lax.dot_general(left, right, (((1,), (1,)), ((), ())), preferred_element_type=f32)


def lane_marks(rows, lanes):
    lane = lax.broadcasted_iota(jnp.int32, (rows, HV), 1)
    return (lane < lanes).astype(bf16)


def features_wide(x, first, second, rows):
    one = mm(x, first) + rows[0:1]
    two = mm(x, second) + rows[1:2]
    return one, two, (one * two) * rows[2:3]


def features_tall(x, tall, first, columns):
    one, two = mm_nt(tall[first], x), mm_nt(tall[first + 1], x)
    parts = [slice(at, at + FS) for at in range(0, one.shape[0], FS)]
    return [
        ((one[at] + columns[0]) * (two[at] + columns[1]) * columns[2]).astype(bf16) for at in parts
    ]


def neighbours(x):
    lane = lax.broadcasted_iota(jnp.int32, x.shape, 1)
    wide = x.astype(f32)
    size = x.shape[1]
    from_k, from_q = pltpu.roll(wide, size - FEAT, 1), pltpu.roll(wide, FEAT, 1)
    pairs = []
    for at in range(0, size, 2 * FEAT):
        in_q = (lane >= at) & (lane < at + FEAT)
        in_k = (lane >= at + FEAT) & (lane < at + 2 * FEAT)
        pairs.append(
            (jnp.where(in_q, from_k, 0.0).astype(bf16), jnp.where(in_k, from_q, 0.0).astype(bf16))
        )
    return pairs


def split_state(state):
    left, right = state[:, :HV], state[:, HV:]
    lane = lax.broadcasted_iota(jnp.int32, right.shape, 1)
    high = right.astype(bf16)
    low = (right - high.astype(f32)).astype(bf16)
    return left.astype(bf16), jnp.where(lane == 2, low, high)


def join_state(state, both):
    right = state[:, HV:]
    lane = lax.broadcasted_iota(jnp.int32, right.shape, 1)
    whole = right[:, 0:1] + right[:, 2:3]
    if both:
        new = jnp.where(lane < 3, whole, 0.0)
    else:
        new = jnp.where(lane == 1, right, jnp.where(lane < 3, whole, 0.0))
    return jnp.concatenate([state[:, :HV], new], axis=1)


def tail_kernel(ids, proj, tall, columns, out, acc):
    at, last = pl.program_id(0), pl.num_programs(0) - 1
    heads = out.shape[0]
    qk = heads * 2 * FEAT

    @pl.when(at == 0)
    def _():
        acc[...] = jnp.zeros_like(acc)

    @pl.when(ids[at] == ids[last])
    def _():
        x = proj[:, :qk]
        marks = lane_marks(x.shape[0], 3)
        tall_k = features_tall(x, tall, 2, columns)
        for h in range(heads):
            v = proj[:, qk + h * HV : qk + (h + 1) * HV]
            acc[h] += mm(tall_k[h], jnp.concatenate([v, marks], axis=1))

    @pl.when(at == last)
    def _():
        for h in range(heads):
            left, right = split_state(acc[h])
            out[h, :, :HV] = left
            out[h, :, HV:] = right


def inner_kernel(ids, proj, num_out, den_out):
    heads = num_out.shape[1] // HV
    qk = heads * 2 * FEAT
    x = proj[:, :qk]
    pairs = neighbours(x)
    size = x.shape[0]
    row = lax.broadcasted_iota(jnp.int32, (size, size), 0)
    col = lax.broadcasted_iota(jnp.int32, (size, size), 1)
    lane = lax.broadcasted_iota(jnp.int32, (size, HV), 1)
    dens = jnp.zeros((size, HV), f32)
    for h in range(heads):
        v = proj[:, qk + h * HV : qk + (h + 1) * HV]
        s = mm_nt(x, pairs[h][0]) * FEAT**-0.5
        a = jnp.where(row >= col, 1.0 + s + 0.5 * s * s, 0.0)
        num_out[:, h * HV : (h + 1) * HV] = mm(a.astype(bf16), v)
        dens = jnp.where(lane == h, jnp.sum(a, axis=1, keepdims=True), dens)
    den_out[...] = dens


def forward_kernel(
    ids, proj, num_in, den_in, incoming, wide, tall, rows, columns, heads_out, num_out, den_out, state_out, acc
):
    at = pl.program_id(0)
    heads = acc.shape[0]
    qk = heads * 2 * FEAT

    @pl.when(at == 0)
    def _():
        for h in range(heads):
            acc[h] = join_state(incoming[h], True)

    @pl.when((at > 0) & (ids[at] != ids[jnp.maximum(at - 1, 0)]))
    def _():
        acc[...] = jnp.zeros_like(acc)

    x = proj[:, :qk]
    size = x.shape[0]
    marks = lane_marks(size, 3)
    lane = lax.broadcasted_iota(jnp.int32, (size, HV), 1)
    tall_k = features_tall(x, tall, 2, columns)
    dens = jnp.zeros((size, HV), f32)
    for h in range(heads):
        v = proj[:, qk + h * HV : qk + (h + 1) * HV]
        left, right = split_state(acc[h])
        state = jnp.concatenate(
            [jnp.concatenate([left, right], axis=1), jnp.zeros((FL - FS, 2 * HV), bf16)], axis=0
        )
        state_out[0, h] = state
        _, _, fq = features_wide(x, wide[0, h], wide[1, h], rows)
        fq = fq.astype(bf16) * rows[3:4].astype(bf16)
        ext = mm(fq, state)
        num = num_in[:, h * HV : (h + 1) * HV] + ext[:, :HV]
        den = den_in[:, h : h + 1] + ext[:, HV : HV + 1] + ext[:, HV + 2 : HV + 3]
        heads_out[:, h * HV : (h + 1) * HV] = (num * (1.0 / den)).astype(bf16)
        num_out[:, h * HV : (h + 1) * HV] = num
        dens = jnp.where(lane == h, den, dens)
        acc[h] += mm(tall_k[h], jnp.concatenate([v, marks], axis=1))
    den_out[...] = dens


def grad_tail_kernel(ids, proj, dheads, num, den, tall, columns, dnum_out, out, acc):
    at, last = pl.program_id(0), pl.num_programs(0) - 1
    heads = out.shape[0]
    qk = heads * 2 * FEAT

    @pl.when(at == 0)
    def _():
        acc[...] = jnp.zeros_like(acc)

    x = proj[:, :qk]
    size = x.shape[0]
    lane = lax.broadcasted_iota(jnp.int32, (size, HV), 1)
    both = []
    for h in range(heads):
        d = den[:, h : h + 1]
        g = dheads[:, h * HV : (h + 1) * HV].astype(f32)
        inverse = 1.0 / d
        dnum = (g * inverse).astype(bf16)
        dden = -jnp.sum(g * num[:, h * HV : (h + 1) * HV], axis=1, keepdims=True) * (
            inverse * inverse
        )
        high = dden.astype(bf16)
        low = (dden - high.astype(f32)).astype(bf16)
        side = jnp.where(
            (lane == 0) | (lane == 2), high.astype(f32), jnp.where(lane == 1, low.astype(f32), 0.0)
        ).astype(bf16)
        both.append(jnp.concatenate([dnum, side], axis=1))
        dnum_out[:, h * 2 * HV : (h + 1) * 2 * HV] = both[h]

    @pl.when(ids[at] == ids[0])
    def _():
        tall_q = features_tall(x, tall, 0, columns)
        for h in range(heads):
            acc[h] += mm(tall_q[h], both[h])

    @pl.when(at == last)
    def _():
        for h in range(heads):
            left, right = split_state(acc[h])
            out[h, :, :HV] = left
            out[h, :, HV:] = right


def local_kernel(ids, proj, dnum_in, state_in, wide, rows, out):
    heads = wide.shape[1]
    qk = heads * 2 * FEAT
    x = proj[:, :qk]
    pairs = neighbours(x)
    size = x.shape[0]
    row = lax.broadcasted_iota(jnp.int32, (size, size), 0)
    col = lax.broadcasted_iota(jnp.int32, (size, size), 1)
    marks = lane_marks(size, 2)
    weight = rows[2:3] * rows[3:4]
    total = jnp.zeros((size, qk), f32)
    for h in range(heads):
        v = proj[:, qk + h * HV : qk + (h + 1) * HV]
        dn = dnum_in[:, h * 2 * HV : (h + 1) * 2 * HV]
        q1, q2, _ = features_wide(x, wide[0, h], wide[1, h], rows)
        kq, qk_moved = pairs[h]
        s = mm_nt(x, kq) * FEAT**-0.5
        st = mm_nt(kq, x) * FEAT**-0.5
        at_low = jnp.where(row <= col, 1.0 + st + 0.5 * st * st, 0.0).astype(bf16)
        v2 = jnp.concatenate([v, marks], axis=1)
        da = mm_nt(dn, v2)
        dat = mm_nt(v2, dn)
        draw = jnp.where(row >= col, da * (1.0 + s) * FEAT**-0.5, 0.0).astype(bf16)
        drawt = jnp.where(row <= col, dat * (1.0 + st) * FEAT**-0.5, 0.0).astype(bf16)
        wq = mm_nt(dn, state_in[0, h]) * weight
        total += (
            mm(draw, kq)
            + mm(drawt, qk_moved)
            + mm_nt((wq * q2).astype(bf16), wide[0, h])
            + mm_nt((wq * q1).astype(bf16), wide[1, h])
        )
        out[:, qk + h * HV : qk + (h + 1) * HV] = mm(at_low, dn[:, :HV])
    out[:, :qk] = total


def backward_kernel(ids, proj, dnum_in, local, incoming, wide, tall, rows, columns, out, acc):
    step, last = pl.program_id(0), pl.num_programs(0) - 1
    at = last - step
    heads = acc.shape[0]
    qk = heads * 2 * FEAT

    @pl.when(step == 0)
    def _():
        for h in range(heads):
            acc[h] = join_state(incoming[h], False)

    @pl.when((step > 0) & (ids[at] != ids[jnp.minimum(at + 1, last)]))
    def _():
        acc[...] = jnp.zeros_like(acc)

    x = proj[:, :qk]
    marks = lane_marks(x.shape[0], 3)
    weight = rows[2:3] * rows[3:4]
    twice = rows[3:4].astype(bf16)
    tall_q = features_tall(x, tall, 0, columns)
    total = local[:, :qk]
    for h in range(heads):
        v = proj[:, qk + h * HV : qk + (h + 1) * HV]
        left, right = split_state(acc[h])
        dstate = jnp.concatenate(
            [jnp.concatenate([left, right], axis=1), jnp.zeros((FL - FS, 2 * HV), bf16)], axis=0
        )
        k1, k2, fk = features_wide(x, wide[2, h], wide[3, h], rows)
        fk = fk.astype(bf16) * twice
        wk = mm_nt(jnp.concatenate([v, marks], axis=1), dstate) * weight
        total += mm_nt((wk * k2).astype(bf16), wide[2, h]) + mm_nt(
            (wk * k1).astype(bf16), wide[3, h]
        )
        dv = local[:, qk + h * HV : qk + (h + 1) * HV] + mm(fk, dstate[:, :HV])
        out[:, qk + h * HV : qk + (h + 1) * HV] = dv.astype(bf16)
        acc[h] += mm(tall_q[h], dnum_in[:, h * 2 * HV : (h + 1) * 2 * HV])
    out[:, :qk] = total.astype(bf16)


def whole_spec(array):
    zeros = (0,) * array.ndim
    return pl.BlockSpec(array.shape, lambda i, ids: zeros)


def attention_calls(blocks, block_len, heads, tables):
    wide, tall, rows, columns = tables
    qk = heads * 2 * FEAT
    tokens = blocks * block_len
    state = (heads, FS, 2 * HV)

    def at_block(cols, reverse=False):
        if reverse:
            return pl.BlockSpec((block_len, cols), lambda i, ids: (blocks - 1 - i, 0))
        return pl.BlockSpec((block_len, cols), lambda i, ids: (i, 0))

    def states_spec(reverse=False):
        if reverse:
            return pl.BlockSpec((1, heads, FL, 2 * HV), lambda i, ids: (blocks - 1 - i, 0, 0, 0))
        return pl.BlockSpec((1, heads, FL, 2 * HV), lambda i, ids: (i, 0, 0, 0))

    def call(kernel, name, in_specs, out_specs, out_shape, flops, moved, carried=True):
        return pl.pallas_call(
            kernel,
            out_shape=out_shape,
            grid_spec=pltpu.PrefetchScalarGridSpec(
                num_scalar_prefetch=1,
                grid=(blocks,),
                in_specs=in_specs,
                out_specs=out_specs,
                scratch_shapes=[pltpu.VMEM(state, f32)] if carried else [],
            ),
            compiler_params=pltpu.CompilerParams(dimension_semantics=("arbitrary",)),
            cost_estimate=pl.CostEstimate(flops=flops, transcendentals=0, bytes_accessed=moved),
            name=name,
        )

    full_state = pl.BlockSpec(state, lambda i, ids: (0, 0, 0))
    proj_cols = qk + heads * HV

    def tail(ids, proj):
        return call(
            tail_kernel,
            "state_tail",
            [at_block(proj_cols), whole_spec(tall), whole_spec(columns)],
            full_state,
            jax.ShapeDtypeStruct(state, bf16),
            int(4e9),
            int(4e6),
        )(ids, proj, tall, columns)

    def inner(ids, proj):
        return call(
            inner_kernel,
            "attention_inner",
            [at_block(proj_cols)],
            [at_block(heads * HV), at_block(HV)],
            [
                jax.ShapeDtypeStruct((tokens, heads * HV), f32),
                jax.ShapeDtypeStruct((tokens, HV), f32),
            ],
            int(4e9),
            int(4e6),
            False,
        )(ids, proj)

    def forward(ids, proj, num, den, incoming):
        return call(
            forward_kernel,
            "attention_forward",
            [at_block(proj_cols), at_block(heads * HV), at_block(HV), full_state]
            + [whole_spec(t) for t in (wide, tall, rows, columns)],
            [at_block(heads * HV), at_block(heads * HV), at_block(HV), states_spec()],
            [
                jax.ShapeDtypeStruct((tokens, heads * HV), bf16),
                jax.ShapeDtypeStruct((tokens, heads * HV), f32),
                jax.ShapeDtypeStruct((tokens, HV), f32),
                jax.ShapeDtypeStruct((blocks, heads, FL, 2 * HV), bf16),
            ],
            int(6e9),
            int(2e7),
        )(ids, proj, num, den, incoming, wide, tall, rows, columns)

    def grad_tail(ids, proj, dheads, num, den):
        return call(
            grad_tail_kernel,
            "state_grad_tail",
            [at_block(proj_cols), at_block(heads * HV), at_block(heads * HV), at_block(HV)]
            + [whole_spec(tall), whole_spec(columns)],
            [at_block(heads * 2 * HV), full_state],
            [
                jax.ShapeDtypeStruct((tokens, heads * 2 * HV), bf16),
                jax.ShapeDtypeStruct(state, bf16),
            ],
            int(4e9),
            int(1e7),
        )(ids, proj, dheads, num, den, tall, columns)

    def local(ids, proj, dnum, states):
        return call(
            local_kernel,
            "attention_backward_local",
            [at_block(proj_cols), at_block(heads * 2 * HV), states_spec()]
            + [whole_spec(t) for t in (wide, rows)],
            at_block(proj_cols),
            jax.ShapeDtypeStruct((tokens, proj_cols), f32),
            int(1.3e10),
            int(2e7),
            False,
        )(ids, proj, dnum, states, wide, rows)

    def backward(ids, proj, dnum, partial, incoming):
        return call(
            backward_kernel,
            "attention_backward",
            [at_block(proj_cols, True), at_block(heads * 2 * HV, True)]
            + [at_block(proj_cols, True), full_state]
            + [whole_spec(t) for t in (wide, tall, rows, columns)],
            at_block(proj_cols, True),
            jax.ShapeDtypeStruct((tokens, proj_cols), bf16),
            int(1e10),
            int(2e7),
        )(ids, proj, dnum, partial, incoming, wide, tall, rows, columns)

    return tail, inner, forward, grad_tail, local, backward


def rows_dot(left, right):
    return lax.dot_general(left, right, (((0,), (0,)), ((), ())), preferred_element_type=f32)


def cols_dot(left, right):
    return lax.dot_general(left, right, (((1,), (1,)), ((), ())), preferred_element_type=f32)


def dot(left, right):
    return jnp.dot(left, right, preferred_element_type=f32)


def turn(value, axis, step):
    count = lax.axis_size(axis)
    return lax.ppermute(value, axis, [(i, (i + step) % count) for i in range(count)])


def tie(*values):
    return lax.optimization_barrier(values)


def put_rows(out, piece, at):
    return out.at[pl.ds(pl.multiple_of(at[0], 128), piece[0])]


def put_columns(out, piece, at):
    return out.at[:, pl.ds(pl.multiple_of(at[0], 128), piece[1])]


def place(pieces, offsets, shape, put=put_rows, dtype=None, base=None):
    count = len(pieces)
    kept = pieces[0].dtype
    dtype = dtype or kept
    wider = dtype != kept
    offsets = [at if isinstance(at, tuple) else (at,) for at in offsets]
    per = len(offsets[0])

    given = count + (base is not None)

    def kernel(offs, *refs):
        out = refs[given]
        held = refs[given + 1 : given + count + 1]
        sent = refs[given + count + 1 : given + 2 * count + 1] if wider else held
        sems = refs[-1]

        def bring(j):
            return pltpu.make_async_copy(refs[j], held[j], sems.at[0, j])

        def send(j):
            at = [jnp.maximum(offs[j * per + i], 0) for i in range(per)]
            return pltpu.make_async_copy(sent[j], put(out, pieces[j].shape, at), sems.at[1, j])

        def each(action):
            for j in range(count):

                @pl.when(offs[j * per] >= 0)
                def _(j=j):
                    action(j)

        def forward(j):
            bring(j).wait()
            if wider:
                sent[j][...] = held[j][...].astype(dtype)
            send(j).start()

        each(lambda j: bring(j).start())
        each(forward)
        each(lambda j: send(j).wait())

    anywhere = pl.BlockSpec(memory_space=pl.ANY)
    size = int(np.prod(shape))
    buffers = [pltpu.VMEM(piece.shape, kept) for piece in pieces]
    if wider:
        buffers += [pltpu.VMEM(piece.shape, dtype) for piece in pieces]
    return pl.pallas_call(
        kernel,
        out_shape=jax.ShapeDtypeStruct(shape, dtype),
        grid_spec=pltpu.PrefetchScalarGridSpec(
            num_scalar_prefetch=1,
            grid=(1,),
            in_specs=[anywhere] * given,
            out_specs=anywhere,
            scratch_shapes=buffers + [pltpu.SemaphoreType.DMA((2, count))],
        ),
        cost_estimate=pl.CostEstimate(flops=0, transcendentals=0, bytes_accessed=4 * size),
        input_output_aliases={} if base is None else {given: 0},
        name="place",
    )(
        jnp.stack([jnp.asarray(o, jnp.int32) for at in offsets for o in at]),
        *pieces,
        *([] if base is None else [base]),
    )


def swap(value, mask):
    count = lax.axis_size("seq")
    return lax.ppermute(value, "seq", [(i, i ^ mask) for i in range(count)])


def gather_start(part):
    half = part.shape[0] // 2
    if lax.axis_size("seq") != 8 or half % 128:
        return [lax.all_gather(part, "seq", axis=0, tiled=True)]
    top, low = part[:half], part[half:]
    return [top, low, swap(top, 2), swap(low, 4), swap(top, 4), swap(low, 2)]


def gather_next(held):
    return held if len(held) == 1 else held + [swap(held[2], 4), swap(held[3], 2)]


def gather_last(held):
    if len(held) == 1:
        return held[0]
    count, mine = lax.axis_size("seq"), lax.axis_index("seq")
    half, width = held[0].shape
    places = [(0, 0), (0, 1), (2, 0), (4, 1), (4, 0), (2, 1), (6, 0), (6, 1)]
    pieces = dict(zip(places, held))
    pieces |= {(mask | 1, side): swap(piece, 1) for (mask, side), piece in pieces.items()}
    offsets = [((mine ^ mask) * 2 + side) * half for mask, side in pieces]
    return place(list(pieces.values()), offsets, (2 * half * count, width))


def gather_columns(block, axis):
    count, mine = lax.axis_size(axis), lax.axis_index(axis)
    width = block.shape[1]
    pieces = [block] + [turn(block, axis, step) for step in range(1, count)]
    offsets = [((mine - step) % count) * width for step in range(count)]
    return place(pieces, offsets, (block.shape[0], width * count), put_columns)


def rows_sent(value):
    count, mine = lax.axis_size("head"), lax.axis_index("head")
    rows, width = value.shape[0] // count, value.shape[1]

    def block(k):
        return lax.dynamic_slice_in_dim(value, ((mine + k) % count) * rows, rows, 0)

    pieces = [block(0)] + [turn(block(k), "head", k) for k in range(1, count)]
    return pieces, [((mine - k) % count) * width for k in range(count)]


def columns_sent(value):
    count, mine = lax.axis_size("head"), lax.axis_index("head")
    rows, width = value.shape[0], value.shape[1] // count

    def block(k):
        return lax.dynamic_slice_in_dim(value, ((mine + k) % count) * width, width, 1)

    pieces = [block(0)] + [turn(block(k), "head", k) for k in range(1, count)]
    return pieces, [((mine - k) % count) * rows for k in range(count)]


def along(value, step):
    count = lax.axis_size("head")
    pairs = [(i, i + step) for i in range(count) if 0 <= i + step < count]
    return lax.ppermute(value, "head", pairs)


def sum_parts(parts, far, low=None, high=None):
    count = lax.axis_size("head")
    up, down = parts[-far % count], parts[far]
    if low is not None:
        up = (up.astype(f32) + low.astype(f32)).astype(bf16)
        down = (down.astype(f32) + high.astype(f32)).astype(bf16)
    return up, down


def sum_send(up, down, far):
    count = lax.axis_size("head")
    return (
        lax.ppermute(up, "head", [(i, i + 1) for i in range(count - far)]),
        lax.ppermute(down, "head", [(i, i - 1) for i in range(far, count)]),
    )


def sum_step(parts, far, low=None, high=None):
    return sum_send(*sum_parts(parts, far, low, high), far)


def join_line(own, from_low, from_high, dtype=None):
    count, mine = lax.axis_size("head"), lax.axis_index("head")
    rows = own.shape[0]
    pieces, offsets = [own], [mine * rows]
    for far, (low, high) in enumerate(zip(from_low, from_high), 1):
        pieces += [low, high]
        offsets.append((mine - far) * rows)
        offsets.append(jnp.where(mine + far < count, (mine + far) * rows, -1))
    return place(pieces, offsets, (rows * count, own.shape[1]), dtype=dtype)


def neighbour_sums(tail, all_ids, step, reach):
    count, mine = lax.axis_size("seq"), lax.axis_index("seq")
    theirs, own = (all_ids[:, -1], all_ids[:, 0]) if step > 0 else (all_ids[:, 0], all_ids[:, -1])
    own = lax.dynamic_index_in_dim(own, mine, 0, keepdims=False)
    total = jnp.zeros(tail.shape, f32)
    for k in range(1, min(reach, count - 1) + 1):
        pairs = [(i, i + k * step) for i in range(count) if 0 <= i + k * step < count]
        got = lax.ppermute(tail, "seq", pairs)
        at = mine - k * step
        other = lax.dynamic_index_in_dim(theirs, jnp.clip(at, 0, count - 1), 0, keepdims=False)
        use = (at >= 0) & (at < count) & (other == own)
        total = total + jnp.where(use, got.astype(f32), 0.0)
    return total


def body(tokens, seq_ids, gain_attn, w_qk, w_v, w_out, gain_mlp, w_gate, w_up, w_down, cotangent):
    zc, z = lax.axis_size("head"), lax.axis_index("head")
    token_count, width = tokens.shape
    blocks = seq_ids.shape[0]
    block_len = token_count // blocks
    heads_here = w_v.shape[1] // HV
    qk_cols = w_qk.shape[1]
    share = token_count // zc
    reach = -(-(MAX_BLOCKS - 1) // blocks)

    small = jnp.pad(seq_ids.astype(bf16), (0, gain_attn.shape[0] - blocks))
    small = jnp.stack([gain_attn, gain_mlp, small])
    small = lax.all_gather(small, "seq", axis=1, tiled=True).astype(f32)
    gain_one, gain_two = small[0], small[1]
    all_ids = small[2].reshape(lax.axis_size("seq"), gain_attn.shape[0])[:, :blocks]
    qkv_part = jnp.concatenate([w_qk, w_v], axis=1)
    full_qkv = lax.all_gather(qkv_part, "seq", axis=0, tiled=True)
    full_both = lax.all_gather(
        jnp.concatenate([w_gate, w_up], axis=1), "seq", axis=0, tiled=True
    )
    out_rows = gather_columns(w_out, "head")

    inputs = tokens.astype(f32)
    scale_one = lax.rsqrt(jnp.mean(inputs * inputs, axis=-1, keepdims=True) + epsilon)
    normed = (inputs * scale_one * gain_one).astype(bf16)
    qkv_blocks = {k: turn(qkv_part, "head", k) for k in range(1, zc)}
    full_qkv, normed, out_rows, qkv_blocks[1], qkv_blocks[zc - 1] = tie(
        full_qkv, normed, out_rows, qkv_blocks[1], qkv_blocks[zc - 1]
    )
    full_out = lax.all_gather(out_rows, "seq", axis=0, tiled=True)
    proj = dot(normed, full_qkv).astype(bf16)
    tables = selection_tables(heads_here)
    tail_call, inner_call, forward_call, grad_tail_call, local_call, backward_call = (
        attention_calls(blocks, block_len, heads_here, tables)
    )
    tail, qkv_blocks[2] = tie(tail_call(seq_ids, proj), qkv_blocks[2])
    qkv_rows = place(
        [qkv_part] + [qkv_blocks[k] for k in range(1, zc)],
        [((z - k) % zc) * qkv_part.shape[1] for k in range(zc)],
        (qkv_part.shape[0], qkv_part.shape[1] * zc),
        put_columns,
    )
    incoming = neighbour_sums(tail, all_ids, 1, reach)
    inner = inner_call(seq_ids, tie(proj, tail)[0])
    incoming, *inner = tie(incoming, *inner)
    head_rows, numerator, denominator, states = forward_call(seq_ids, proj, *inner, incoming)
    down_held = gather_start(tie(w_down, head_rows)[0])
    all_qkv = lax.all_gather(qkv_rows, "seq", axis=0, tiled=True)

    heads_own = place(*rows_sent(head_rows), (share, heads_here * HV * zc), put_columns)
    own_in = lax.dynamic_slice_in_dim(tokens, z * share, share, 0).astype(f32)
    residual = own_in + dot(heads_own, full_out)
    scale_two = lax.rsqrt(jnp.mean(residual * residual, axis=-1, keepdims=True) + epsilon)
    normed_own = (residual * scale_two * gain_two).astype(bf16)

    normed_own, *down_held = tie(normed_own, *down_held)
    full_down = gather_last(gather_next(down_held))
    order = [0] + sorted(range(1, zc), key=lambda k: min(k, zc - k))
    hidden = w_gate.shape[1]
    normed_parts, cot_parts, act_parts, both_parts = [], [], [], []
    backs = {}
    got_first, first_own, later = tie(turn(normed_own, "head", order[1]), normed_own, normed_own)
    arrivals = {0: first_own, order[1]: got_first}
    for k in order[2:]:
        arrivals[k] = turn(later, "head", k)
    for k in order:
        normed_two = arrivals[k]
        owner = (z - k) % zc
        cot = lax.dynamic_slice_in_dim(cotangent, owner * share, share, 0)
        pre = dot(normed_two, full_both)
        gate_pre, up_pre = pre[:, :hidden], pre[:, hidden:]
        gate_sigmoid = jax.nn.sigmoid(gate_pre)
        active = (gate_pre * gate_sigmoid * up_pre).astype(bf16)
        grad_active = dot(cot, full_down)
        grad_gate = grad_active * up_pre * gate_sigmoid * (1.0 + gate_pre * (1.0 - gate_sigmoid))
        grad_upper = grad_active * gate_pre * gate_sigmoid
        grad_both = jnp.concatenate([grad_gate.astype(bf16), grad_upper.astype(bf16)], axis=1)
        backs[k] = cols_dot(grad_both, full_both)
        if k:
            backs[k] = backs[k].astype(bf16)
        if k != order[-1]:
            following = order[order.index(k) + 1]
            arrivals[following], backs[k] = tie(arrivals[following], backs[k])
        normed_parts.append(normed_two)
        cot_parts.append(cot)
        act_parts.append(active)
        both_parts.append(grad_both)
    low = high = None
    for far in range(zc - 1, 2, -1):
        low, high = sum_step(backs, far, low, high)
    up, down = sum_parts(backs, 2, low, high)
    up, down, normed_parts[0], both_parts[0], cot_parts[0], *act_parts = tie(
        up, down, normed_parts[0], both_parts[0], cot_parts[0], *act_parts
    )
    low, high = sum_send(up, down, 2)
    both_grad = rows_dot(jnp.concatenate(normed_parts), jnp.concatenate(both_parts)).astype(bf16)
    low, high, act_parts[0], both_grad = tie(low, high, act_parts[0], both_grad)
    both_shard = lax.psum_scatter(both_grad, "seq", scatter_dimension=0, tiled=True)
    up, down = sum_parts(backs, 1, low, high)
    up, down, *act_parts = tie(up, down, *act_parts)
    low, high = sum_send(up, down, 1)
    outs = {k: cols_dot(active, full_down) for k, active in zip(order, act_parts)}
    outs = {k: out.astype(bf16) if k else out for k, out in outs.items()}
    down_grad = rows_dot(jnp.concatenate(cot_parts), jnp.concatenate(act_parts)).astype(bf16)
    tied = tie(backs[0], low, high, all_qkv, down_grad, *[outs[k] for k in order])
    grad_normed = tied[0] + tied[1].astype(f32) + tied[2].astype(f32)
    all_qkv, down_grad = tied[3:5]
    down_shard = lax.psum_scatter(down_grad, "seq", scatter_dimension=0, tiled=True)
    outs = dict(zip(order, tied[5:]))

    cot_own = lax.dynamic_slice_in_dim(cotangent, z * share, share, 0).astype(f32)
    weighted = grad_normed * gain_two
    grad_mid = (
        cot_own
        + scale_two * weighted
        - residual * scale_two**3 * jnp.mean(weighted * residual, axis=-1, keepdims=True)
    )
    gain_two_term = jnp.sum(grad_normed * residual * scale_two, axis=0)
    grad_branch = grad_mid.astype(bf16)
    grad_heads = cols_dot(grad_branch, full_out).astype(bf16)
    pieces, offsets = columns_sent(grad_heads)
    pieces[1], heads_own = tie(pieces[1], heads_own)
    out_grad = rows_dot(heads_own, grad_branch).astype(bf16)
    pieces[2], out_grad = tie(pieces[2], out_grad)
    grad_heads = place(pieces, offsets, (token_count, grad_heads.shape[1] // zc))
    grad_heads, low, high = tie(grad_heads, *sum_step(outs, zc - 1))
    grad_heads, up, down = tie(grad_heads, *sum_parts(outs, 2, low, high))
    low, high = sum_send(up, down, 2)
    dnum, head_part = grad_tail_call(seq_ids, proj, grad_heads, numerator, denominator)
    outgoing = neighbour_sums(head_part, all_ids, -1, reach)
    low, high = sum_step(outs, 1, low, high)
    partial = local_call(seq_ids, proj, dnum, states)
    outgoing, low, high, partial = tie(outgoing, low, high, partial)
    result_own = (residual + outs[0] + low.astype(f32) + high.astype(f32)).astype(bf16)
    res_low, res_high = [along(result_own, 1)], [along(result_own, -1)]
    grad_qkv = backward_call(seq_ids, proj, dnum, partial, outgoing)
    grad_qkv, res_low[0], res_high[0], both_shard, out_grad = tie(
        grad_qkv, res_low[0], res_high[0], both_shard, out_grad
    )
    out_part = lax.psum_scatter(out_grad, "seq", scatter_dimension=0, tiled=True)
    qkv_grad = rows_dot(normed, grad_qkv)

    own_pieces, own_columns = rows_sent(grad_qkv)
    own_pieces[1], res_low[0], res_high[0] = tie(own_pieces[1], res_low[0], res_high[0])
    res_low.append(along(res_low[0], 1))
    res_high.append(along(res_high[0], -1))
    own_qkv = place(own_pieces, own_columns, (share, grad_qkv.shape[1] * zc), put_columns)
    grad_norm_one = cols_dot(own_qkv, all_qkv)
    grad_norm_one, res_low[1], res_high[1], down_shard = tie(
        grad_norm_one, res_low[1], res_high[1], down_shard
    )
    own_scale = lax.dynamic_slice_in_dim(scale_one, z * share, share, 0)
    weighted_one = grad_norm_one * gain_one
    grad_own = (
        grad_mid
        + own_scale * weighted_one
        - own_in * own_scale**3 * jnp.mean(weighted_one * own_in, axis=-1, keepdims=True)
    )
    gain_one_term = jnp.sum(grad_norm_one * own_in * own_scale, axis=0)
    tok_own, gain_one_term = tie(grad_own.astype(bf16), gain_one_term)
    out_cols = w_out.shape[1]
    tok_low, tok_high = [along(tok_own, 1)], [along(tok_own, -1)]
    for far in range(3, zc):
        res_low.append(along(res_low[-1], 1))
        res_high.append(along(res_high[-1], -1))
    tok_low[0], tok_high[0], res_low[-1], res_high[-1], out_part = tie(
        tok_low[0], tok_high[0], res_low[-1], res_high[-1], out_part
    )
    out_shard = lax.dynamic_slice_in_dim(out_part, z * out_cols, out_cols, 1).astype(f32)
    for k in range(1, zc):
        block = lax.dynamic_slice_in_dim(out_part, ((z + k) % zc) * out_cols, out_cols, 1)
        out_shard = out_shard + turn(block, "head", k).astype(f32)
    for far in range(2, zc):
        tok_low.append(along(tok_low[-1], 1))
        tok_high.append(along(tok_high[-1], -1))
    near_low, near_high = tok_low[:-1], tok_high[:-1]
    near_low[-1], out_shard = tie(near_low[-1], out_shard)

    def scatter(grad):
        return lax.psum_scatter(grad, "seq", scatter_dimension=0, tiled=True)

    down_shard = down_shard.astype(f32)
    both_shard = both_shard.astype(f32)
    gain_terms = jnp.pad(jnp.stack([gain_one_term, gain_two_term], axis=1), ((0, 0), (0, 126)))
    last = scatter(jnp.concatenate([qkv_grad, gain_terms], axis=1).astype(bf16)).astype(f32)
    gain_own = last[:, -128:-126].T[None]
    gain_parts = [gain_own] + [turn(gain_own, "head", k) for k in range(1, zc)]
    tok_low[-1], tok_high[-1], *gain_parts = tie(tok_low[-1], tok_high[-1], *gain_parts)
    gain_all = jnp.zeros((zc,) + gain_own.shape[1:], f32)
    for k, part in enumerate(gain_parts):
        gain_all = lax.dynamic_update_slice_in_dim(gain_all, part, (z - k) % zc, 0)
    gain_sums = jnp.sum(gain_all, axis=0)
    grad_tokens = join_line(tok_own, near_low, near_high, f32)
    grad_tokens = place(
        [tok_low[-1], tok_high[-1]],
        [(z - zc + 1) * share, jnp.where(z == 0, (zc - 1) * share, -1)],
        grad_tokens.shape,
        dtype=f32,
        base=grad_tokens,
    )
    result = join_line(result_own, res_low, res_high)
    return (
        result,
        grad_tokens,
        last[:, :qk_cols],
        last[:, qk_cols:-128],
        out_shard,
        both_shard[:, :hidden],
        both_shard[:, hidden:],
        down_shard,
        gain_sums[0],
        gain_sums[1],
    )


def solution(mesh):
    return jax.shard_map(
        body,
        mesh=mesh,
        in_specs=(
            P("seq", None),
            P("seq"),
            P("seq"),
            P("seq", "head"),
            P("seq", "head"),
            P("seq", "head"),
            P("seq"),
            P("seq", "head"),
            P("seq", "head"),
            P("seq", "head"),
            P("seq", None),
        ),
        out_specs=(
            P("seq", None),
            P("seq", None),
            P("seq", "head"),
            P("seq", "head"),
            P("seq", "head"),
            P("seq", "head"),
            P("seq", "head"),
            P("seq", "head"),
            P("seq"),
            P("seq"),
        ),
        check_vma=False,
    )
```
